256 devices in a mesh: ctx: 8 (over z), tp: 4 (over y_lo, core), dp: 8 (over x, y_hi).
Axes of the slice: x: 4, y: 4 (y_hi: 2, y_lo: 2; y = y_hi * 2 + y_lo), z: 8, core: 2. Of those that a mesh axis runs over, the one named last changes fastest.
Arguments:
- tokens: bfloat16 [8, 2, 2048, 4096], P('dp', None, 'ctx')
- norm_gain: float32 [4096], replicated, as said below
- query_weight: bfloat16 [4096, 2048], P(('ctx', 'dp'), 'tp'), may hold values from -0.09375 to 0.09375
- key_weight: bfloat16 [4096, 512], P(('ctx', 'dp'), 'tp'), may hold values from -0.09375 to 0.09375
- value_weight: bfloat16 [4096, 512], P(('ctx', 'dp'), 'tp'), may hold values from -0.09375 to 0.09375
- output_weight: bfloat16 [2048, 4096], P(None, ('tp', 'ctx', 'dp')), may hold values from -0.125 to 0.125
- query_noise: bfloat16 [4096, 2048], P(('ctx', 'dp'), 'tp'), may hold values from -6 to 6
- key_noise: bfloat16 [4096, 512], P(('ctx', 'dp'), 'tp'), may hold values from -6 to 6
- value_noise: bfloat16 [4096, 512], P(('ctx', 'dp'), 'tp'), may hold values from -6 to 6
- output_noise: bfloat16 [2048, 4096], P(None, ('tp', 'ctx', 'dp')), may hold values from -6 to 6
- sign: int32 [2], replicated, may hold values from -1 to 1, as said below
- segment_ids: int32 [8, 2, 2048], P('dp', None, 'ctx'), may hold values from 0 to 3, as said below
- doc_weight: float32 [8], P('dp'), may hold values from 0.5 to 8
Outputs:
- branch: bfloat16 [8, 2, 2048, 4096], P('dp', None, 'ctx', 'tp')
- loss: float32 [1], replicated
The draws below stay inside these ranges and needn't reach their ends.
Inputs may be any that keep to these rules, and one draw needn't show every extreme that they name: `segment_ids`: read in natural position order, each sequence's ids never fall, begin at 0 and end at 3. `sign`: the two entries are opposite, each -1 or 1. `norm_gain`: Positive.
All inputs are finite; a program needn't handle non-finite values.
Results may differ from the reference program's by a relative error of at most 0.017.
The reference program's roundings to bfloat16 on the way (of `normed`, `values`, `weights` and `mixed`) count: a program that leaves them out, or rounds other values in their place, can miss the bound.
Values may be sent and summed in bfloat16 or wider, within the bound.
No kernel may reach another device: no remote copies, remote signals or barrier semaphores. Data moves between devices by JAX's collectives and lax.ppermute only.
A program may use at most 128 MiB of HBM per device.

```python
import math
import jax
import jax.numpy as jnp
from jax import lax

D = 4096
HD = 128
QHEADS = 16
KVHEADS = 4
NSEG = 4
HALF = 256
DOCS = 8
SEQ = 4096
N_CTX = 8
N_TP = 4


def draw_tokens(key, part):
    first_key, second_key = jax.random.split(key, 2)
    shape = (DOCS, 2, SEQ // 2, D)
    row_scale = jnp.exp(jax.random.uniform(second_key, (DOCS, 2, SEQ // 2, 1), jnp.float32, 0.0, math.log(10.0)))
    values = jax.random.normal(first_key, shape, jnp.float32) * row_scale
    return values.astype(jnp.bfloat16)


def draw_norm_gain(key, part):
    values = jax.random.uniform(key, (D,), jnp.float32, 0.5, 1.5)
    return values


def draw_sign(key, part):
    first = (2 * jax.random.randint(key, (1,), 0, 2) - 1).astype(jnp.int32)
    return jnp.concatenate([first, -first]).astype(jnp.int32)


def draw_segment_ids(key, part):
    cuts = jax.random.randint(key, (DOCS, NSEG - 1), 1, SEQ)
    positions = jnp.arange(SEQ, dtype=jnp.int32)
    natural = jnp.sum((positions[None, :, None] >= cuts[:, None, :]).astype(jnp.int32), axis=-1).astype(jnp.int32)
    spans = SEQ // (2 * HALF)
    first_half = natural[:, :SEQ // 2]
    second_half = natural[:, SEQ // 2:].reshape(DOCS, spans, HALF)[:, ::-1].reshape(DOCS, SEQ // 2)
    return jnp.stack([first_half, second_half], axis=1).astype(jnp.int32)


def steps_of(key, shape, shards, low, largest):
    def one(axis_at, blocks):
        steps = jax.random.uniform(jax.random.fold_in(jax.random.fold_in(key, 6), axis_at), (blocks,), jnp.float32, low / len(shards), largest / len(shards))
        return jnp.repeat(jnp.exp(steps), shape[axis_at] // blocks).reshape((-1,) + (1,) * (len(shape) - axis_at - 1))

    loudness = one(*shards[0])
    for cut in shards[1:]:
        loudness = loudness * one(*cut)
    return loudness


def centred(rng, shape, scale, most, pieces=(), kind=jnp.bfloat16):
    entries = jax.random.normal(rng, shape, jnp.float32) * scale
    if len(pieces) > 0:
        entries = steps_of(rng, shape, pieces, -0.22, 0.18) * entries
    return jnp.clip(entries, min=-most, max=most).astype(kind)


def setup_inputs(seed: int = 0) -> dict:
    keys = jax.random.split(jax.random.key(seed), 14)
    tokens = draw_tokens(jax.random.fold_in(keys[13], 71), 0)
    norm_gain = draw_norm_gain(jax.random.fold_in(keys[13], 71), 0)
    query_weight = centred(keys[2], (D, QHEADS * HD), D ** -0.5, 0.09375, ((0, 64), (1, 4)))
    key_weight = centred(keys[3], (D, KVHEADS * HD), D ** -0.5, 0.09375, ((0, 64), (1, 4)))
    value_weight = centred(keys[4], (D, KVHEADS * HD), D ** -0.5, 0.09375, ((0, 64), (1, 4)))
    output_weight = centred(keys[5], (QHEADS * HD, D), (QHEADS * HD) ** -0.5, 0.125, ((1, 256),))
    query_noise = centred(keys[6], (D, QHEADS * HD), 1.0, 6.0, ((0, 64), (1, 4)))
    key_noise = centred(keys[7], (D, KVHEADS * HD), 1.0, 6.0, ((0, 64), (1, 4)))
    value_noise = centred(keys[8], (D, KVHEADS * HD), 1.0, 6.0, ((0, 64), (1, 4)))
    output_noise = centred(keys[9], (QHEADS * HD, D), 1.0, 6.0, ((1, 256),))
    sign = draw_sign(jax.random.fold_in(keys[13], 71), 0)
    segment_ids = draw_segment_ids(jax.random.fold_in(keys[13], 71), 0)
    doc_weight = jnp.clip(jnp.exp(math.log(8.0) - 2.7725887 * jax.random.uniform(keys[12], (DOCS,), jnp.float32) ** steps_of(keys[12], (DOCS,), ((0, 8),), -0.2, 0.2)), 0.5, 8.0)
    return {"tokens": tokens, "norm_gain": norm_gain, "query_weight": query_weight, "key_weight": key_weight, "value_weight": value_weight, "output_weight": output_weight, "query_noise": query_noise, "key_noise": key_noise, "value_noise": value_noise, "output_noise": output_noise, "sign": sign, "segment_ids": segment_ids, "doc_weight": doc_weight}


perturb_step = 0.004
rope_base = 500000.0
norm_epsilon = 1e-05
masked_score = -1e+30

def perturbed(weight, noise, factor):
    return (weight.astype(jnp.float32) + factor * noise.astype(jnp.float32)).astype(jnp.bfloat16)

def rotate(values, positions):
    head_size = values.shape[-1]
    half_size = head_size // 2
    inverse = rope_base ** (-jnp.arange(half_size, dtype=jnp.float32) * 2.0 / head_size)
    angles = positions.astype(jnp.float32)[:, None] * inverse[None, :]
    extra = (1,) * (values.ndim - 2)
    cosine = jnp.cos(angles).reshape(angles.shape[:1] + extra + angles.shape[1:])
    sine = jnp.sin(angles).reshape(angles.shape[:1] + extra + angles.shape[1:])
    first_half = values[..., :half_size]
    second_half = values[..., half_size:]
    return jnp.concatenate([first_half * cosine - second_half * sine, second_half * cosine + first_half * sine], axis=-1)

def unfold(folded, half_rows, spans):
    first_half = folded[0]
    second_half = folded[1].reshape((spans, half_rows) + folded.shape[2:])[::-1].reshape(folded.shape[1:])
    return jnp.concatenate([first_half, second_half], axis=0)

def refold(natural, half_rows, spans):
    middle = natural.shape[0] // 2
    first_half = natural[:middle]
    second_half = natural[middle:].reshape((spans, half_rows) + natural.shape[1:])[::-1].reshape((middle,) + natural.shape[1:])
    return jnp.stack([first_half, second_half])

def reference(tokens, norm_gain, query_weight, key_weight, value_weight, output_weight, query_noise, key_noise, value_noise, output_noise, sign, segment_ids, doc_weight):
    factor = sign[0].astype(jnp.float32) * perturb_step
    query_full = perturbed(query_weight, query_noise, factor)
    key_full = perturbed(key_weight, key_noise, factor)
    value_full = perturbed(value_weight, value_noise, factor)
    output_full = perturbed(output_weight, output_noise, factor)
    seq_len = 2 * HALF * N_CTX
    group = QHEADS // KVHEADS
    scale = 1.0 / HD ** 0.5
    positions = jnp.arange(seq_len, dtype=jnp.int32)
    block_rows = 2 * HALF
    width = QHEADS * HD // N_TP
    outputs = []
    loss = jnp.zeros((), jnp.float32)
    for sequence in range(DOCS):
        rows_f = unfold(tokens[sequence], HALF, N_CTX).astype(jnp.float32)
        normed = (rows_f * lax.rsqrt(lax.optimization_barrier(jnp.mean(rows_f * rows_f, axis=-1, keepdims=True)) + norm_epsilon) * norm_gain).astype(jnp.bfloat16)
        queries = rotate(jnp.dot(normed, query_full, preferred_element_type=jnp.float32).reshape(seq_len, KVHEADS, group, HD), positions).astype(jnp.bfloat16)
        keys_all = rotate(jnp.dot(normed, key_full, preferred_element_type=jnp.float32).reshape(seq_len, KVHEADS, HD), positions).astype(jnp.bfloat16)
        values_all = jnp.dot(normed, value_full, preferred_element_type=jnp.float32).astype(jnp.bfloat16).reshape(seq_len, KVHEADS, HD)
        segments = unfold(segment_ids[sequence], HALF, N_CTX)
        blocks_out = []
        for first_row in range(0, seq_len, block_rows):
            last_row = first_row + block_rows
            query_block = queries[first_row:last_row].astype(jnp.float32)
            scores = jnp.einsum('rhgd,khd->hgrk', query_block, keys_all[:last_row].astype(jnp.float32)) * scale
            allowed = (positions[None, :last_row] <= positions[first_row:last_row, None]) & (segments[None, :last_row] == segments[first_row:last_row, None])
            limited = jnp.where(allowed, scores, masked_score)
            highest = lax.optimization_barrier(jnp.max(limited, axis=-1, keepdims=True))
            weights = jnp.where(allowed, jnp.exp(scores - highest), 0.0)
            totals = lax.optimization_barrier(jnp.sum(weights, axis=-1))
            rounded = lax.optimization_barrier(weights.astype(jnp.bfloat16)).astype(jnp.float32)
            mixed = jnp.einsum('hgrk,khd->hgrd', rounded, values_all[:last_row].astype(jnp.float32)) / totals[..., None]
            blocks_out.append(jnp.transpose(mixed, (2, 0, 1, 3)).reshape(block_rows, QHEADS * HD).astype(jnp.bfloat16))
        attention = jnp.concatenate(blocks_out, axis=0)
        summed = jnp.zeros((seq_len, D), jnp.float32)
        for owner in range(N_TP):
            partial_term = jnp.dot(attention[:, owner * width:(owner + 1) * width], output_full[owner * width:(owner + 1) * width], preferred_element_type=jnp.float32)
            summed = summed + lax.optimization_barrier(partial_term.astype(jnp.bfloat16)).astype(jnp.float32)
        branch_out = summed.astype(jnp.bfloat16)
        squared = jnp.square(branch_out.astype(jnp.float32))
        loss = loss + doc_weight[sequence] * jnp.sum(squared) / (seq_len * D)
        outputs.append(refold(branch_out, HALF, N_CTX))
    return (jnp.stack(outputs), loss.reshape(1))
```

```python
import jax
import jax.numpy as jnp
from jax import lax
from jax.experimental import pallas as pl
from jax.experimental.pallas import tpu as pltpu
from jax.sharding import PartitionSpec as P

HD = 128

perturb_step = 0.004
rope_base = 500000.0
norm_epsilon = 1e-05
masked_score = -1e30


def perturbed(weight, noise, factor):
    return (weight.astype(jnp.float32) + factor * noise.astype(jnp.float32)).astype(jnp.bfloat16)


def dot_dims(lhs, rhs, dims):
    return lax.dot_general(lhs, rhs, (dims, ((), ())), preferred_element_type=jnp.float32)


def rope_tables(positions):
    half = HD // 2
    inverse = rope_base ** (-jnp.arange(half, dtype=jnp.float32) * 2.0 / HD)
    angles = positions.astype(jnp.float32)[:, None] * inverse[None, :]
    cosine = jnp.cos(angles)
    sine = jnp.sin(angles)
    return (
        jnp.concatenate([cosine, cosine], axis=1),
        jnp.concatenate([-sine, sine], axis=1),
    )


def project_kernel(normed_ref, weight_ref, cos_ref, sin_ref, out_ref, *, turned):
    sums = jnp.dot(normed_ref[...], weight_ref[...], preferred_element_type=jnp.float32)
    cosine = cos_ref[...]
    sine = sin_ref[...]
    for head in range(sums.shape[1] // HD):
        part = sums[:, head * HD : (head + 1) * HD]
        if head < turned:
            part = part * cosine + pltpu.roll(part, HD // 2, 1) * sine
        out_ref[:, head * HD : (head + 1) * HD] = part.astype(jnp.bfloat16)


def project(normed, weight, cosine, sine, width, turned, rows=128):
    count, model_width = normed.shape
    return pl.pallas_call(
        lambda *refs: project_kernel(*refs, turned=turned),
        grid=(count // rows,),
        in_specs=[
            pl.BlockSpec((rows, model_width), lambda i: (i, 0)),
            pl.BlockSpec((model_width, width), lambda i: (0, 0)),
            pl.BlockSpec((rows, HD), lambda i: (i, 0)),
            pl.BlockSpec((rows, HD), lambda i: (i, 0)),
        ],
        out_specs=pl.BlockSpec((rows, width), lambda i: (i, 0)),
        out_shape=jax.ShapeDtypeStruct((count, width), jnp.bfloat16),
        name="project",
    )(normed, weight, cosine, sine)


def attend_kernel(place_ref, query_ref, kv_ref, first_ref, out_ref, *, half_rows, heads, blocks):
    which = pl.program_id(0)
    queries = jnp.concatenate(
        [query_ref[0, :, h * HD : (h + 1) * HD] for h in range(heads)], axis=0
    )
    rows = heads * half_rows
    scale = 1.0 / HD**0.5
    first = first_ref[0]
    ctx = place_ref[0]
    own = jnp.where(which == 0, ctx, blocks - 1 - ctx)
    low = place_ref[1 + which]
    key_iota = lax.broadcasted_iota(jnp.int32, (half_rows, rows), 0)
    query_pos = own * half_rows + lax.rem(
        lax.broadcasted_iota(jnp.int32, (1, rows), 1), half_rows
    )

    def step(block, state):
        highest, totals, accum = state
        second = block >= blocks // 2
        holder = jnp.where(second, blocks - 1 - block, block)
        half = jnp.where(second, 1, 0)
        keys = kv_ref[holder, half, :half_rows, :HD]
        values = kv_ref[holder, half, :half_rows, HD : 2 * HD]
        scores = dot_dims(keys, queries, ((1,), (1,))) * scale
        key_pos = block * half_rows + key_iota
        allowed = (key_pos <= query_pos) & (key_pos >= first)
        limited = jnp.where(allowed, scores, masked_score)
        new_high = jnp.maximum(highest, jnp.max(limited, axis=0, keepdims=True))
        shrink = jnp.exp(highest - new_high)
        weights = jnp.where(allowed, jnp.exp(scores - new_high), 0.0)
        new_totals = totals * shrink + jnp.sum(weights, axis=0, keepdims=True)
        added = dot_dims(values, weights.astype(jnp.bfloat16), ((0,), (0,)))
        return (new_high, new_totals, accum * shrink + added)

    start = (
        jnp.full((1, rows), masked_score, jnp.float32),
        jnp.zeros((1, rows), jnp.float32),
        jnp.zeros((HD, rows), jnp.float32),
    )
    _, totals, accum = lax.fori_loop(low, own + 1, step, start)
    mixed = (accum / totals).astype(jnp.bfloat16)
    for h in range(heads):
        out_ref[0, :, h * HD : (h + 1) * HD] = mixed[:, h * half_rows : (h + 1) * half_rows].T


def attend(place, queries, kv, first, half_rows, heads, blocks):
    width = heads * HD
    return pl.pallas_call(
        lambda *refs: attend_kernel(*refs, half_rows=half_rows, heads=heads, blocks=blocks),
        grid_spec=pltpu.PrefetchScalarGridSpec(
            num_scalar_prefetch=1,
            grid=(2,),
            in_specs=[
                pl.BlockSpec((1, half_rows, width), lambda i, _: (i, 0, 0)),
                pl.BlockSpec(kv.shape, lambda i, _: (0, 0, 0, 0)),
                pl.BlockSpec((1, 1, heads * half_rows), lambda i, _: (i, 0, 0)),
            ],
            out_specs=pl.BlockSpec((1, half_rows, width), lambda i, _: (i, 0, 0)),
        ),
        out_shape=jax.ShapeDtypeStruct((2, half_rows, width), jnp.bfloat16),
        name="attend",
    )(place, queries, kv, first)


def blend_kernel(mixed_ref, weight_ref, out_ref, square_ref):
    owners = mixed_ref.shape[0]
    width = mixed_ref.shape[2]
    total = None
    for owner in range(owners):
        term = dot_dims(
            mixed_ref[owner], weight_ref[:, owner * width : (owner + 1) * width], ((1,), (1,))
        )
        term = term.astype(jnp.bfloat16).astype(jnp.float32)
        total = term if total is None else total + term
    branch = total.astype(jnp.bfloat16)
    out_ref[...] = branch
    square = jnp.square(branch.astype(jnp.float32))
    part = jnp.sum(square.reshape(-1, 8, square.shape[1]), axis=0)

    @pl.when(pl.program_id(0) == 0)
    def _():
        square_ref[...] = jnp.zeros_like(square_ref)

    square_ref[...] += part


def blend(mixed, weight, rows=128):
    owners, count, width = mixed.shape
    features = weight.shape[0]
    return pl.pallas_call(
        blend_kernel,
        grid=(count // rows,),
        in_specs=[
            pl.BlockSpec((owners, rows, width), lambda i: (0, i, 0)),
            pl.BlockSpec(weight.shape, lambda i: (0, 0)),
        ],
        out_specs=[
            pl.BlockSpec((rows, features), lambda i: (i, 0)),
            pl.BlockSpec((8, features), lambda i: (0, 0)),
        ],
        out_shape=[
            jax.ShapeDtypeStruct((count, features), jnp.bfloat16),
            jax.ShapeDtypeStruct((8, features), jnp.float32),
        ],
        name="blend",
    )(mixed, weight)


def shards(
    tokens,
    norm_gain,
    query_weight,
    key_weight,
    value_weight,
    output_weight,
    query_noise,
    key_noise,
    value_noise,
    output_noise,
    sign,
    segment_ids,
    doc_weight,
):
    factor = sign[0].astype(jnp.float32) * perturb_step
    half_rows = tokens.shape[2]
    model_width = tokens.shape[3]
    local_rows = 2 * half_rows
    ctx = lax.axis_index("ctx")
    ctx_count = lax.axis_size("ctx")
    seq_len = local_rows * ctx_count
    blocks = 2 * ctx_count
    heads = query_weight.shape[1] // HD
    width = heads * HD

    own_qkv = perturbed(
        jnp.concatenate([query_weight, key_weight, value_weight], axis=1),
        jnp.concatenate([query_noise, key_noise, value_noise], axis=1),
        factor,
    )
    own_out = perturbed(output_weight, output_noise, factor).T
    qkv_weight = lax.all_gather(own_qkv, ("ctx", "dp"), axis=0, tiled=True)

    rows_f = tokens[0].reshape(local_rows, model_width).astype(jnp.float32)
    normed = (
        rows_f
        * lax.rsqrt(jnp.mean(rows_f * rows_f, axis=-1, keepdims=True) + norm_epsilon)
        * norm_gain
    ).astype(jnp.bfloat16)
    offsets = jnp.arange(half_rows, dtype=jnp.int32)
    local_pos = jnp.concatenate(
        [ctx * half_rows + offsets, seq_len - (ctx + 1) * half_rows + offsets]
    )
    cosine, sine = rope_tables(local_pos)

    qkv = project(normed, qkv_weight, cosine, sine, width + 2 * HD, heads + 1)
    queries = qkv[:, :width].reshape(2, half_rows, width)
    kv_own = qkv[:, width:].reshape(2, half_rows, 2 * HD)
    seg_rows = segment_ids[0].astype(jnp.bfloat16).reshape(2, half_rows // (2 * HD), 2 * HD)
    pad = jnp.zeros((2, 16 - seg_rows.shape[1], 2 * HD), jnp.bfloat16)
    parcel = jnp.concatenate([kv_own, seg_rows, pad], axis=1)
    kv = lax.all_gather(parcel, "ctx", axis=0)

    all_seg = kv[:, :, half_rows, :]
    doc_first = jnp.sum(
        (all_seg[None] < jnp.arange(4, dtype=jnp.bfloat16)[:, None, None, None]).astype(jnp.int32),
        axis=(1, 2, 3),
    )
    first = jnp.zeros((2, half_rows), jnp.int32)
    for doc in range(1, 4):
        first = jnp.where(segment_ids[0] == doc, doc_first[doc], first)
    low = jnp.min(first, axis=1) // half_rows
    place = jnp.concatenate([ctx.reshape(1), low]).astype(jnp.int32)
    first = jnp.tile(first, (1, heads)).reshape(2, 1, heads * half_rows)
    mixed = attend(place, queries, kv, first, half_rows, heads, blocks)

    mixed_all = lax.all_gather(mixed.reshape(local_rows, width), "tp", axis=0)
    out_weight = lax.all_gather(own_out, ("ctx", "dp"), axis=0, tiled=True)
    branch, squares = blend(mixed_all, out_weight)
    local_total = jnp.sum(squares) * doc_weight[0]
    loss = lax.psum(local_total, ("ctx", "tp", "dp")) / (seq_len * model_width)
    return (branch.reshape(1, 2, half_rows, branch.shape[1]), loss.reshape(1))


def solution(mesh):
    return jax.shard_map(
        shards,
        mesh=mesh,
        in_specs=(
            P("dp", None, "ctx", None),
            P(),
            P(("ctx", "dp"), "tp"),
            P(("ctx", "dp"), "tp"),
            P(("ctx", "dp"), "tp"),
            P(None, ("tp", "ctx", "dp")),
            P(("ctx", "dp"), "tp"),
            P(("ctx", "dp"), "tp"),
            P(("ctx", "dp"), "tp"),
            P(None, ("tp", "ctx", "dp")),
            P(),
            P("dp", None, "ctx"),
            P("dp"),
        ),
        out_specs=(P("dp", None, "ctx", "tp"), P()),
        check_vma=False,
    )
```

```python
import jax
import jax.numpy as jnp
from jax import lax
from jax.experimental import pallas as pl
from jax.experimental.pallas import tpu as pltpu
from jax.sharding import PartitionSpec as P

HD = 128
LANES = 128

perturb_step = 0.004
rope_base = 500000.0
norm_epsilon = 1e-05
masked_score = -1e30
mesh_axes = ("ctx", "tp", "dp")


def perturbed(weight, noise, factor):
    return (weight.astype(jnp.float32) + factor * noise.astype(jnp.float32)).astype(jnp.bfloat16)


def dot_dims(lhs, rhs, dims):
    return lax.dot_general(lhs, rhs, (dims, ((), ())), preferred_element_type=jnp.float32)


def rope_tables(positions):
    half = HD // 2
    inverse = rope_base ** (-jnp.arange(half, dtype=jnp.float32) * 2.0 / HD)
    angles = positions.astype(jnp.float32)[:, None] * inverse[None, :]
    cosine = jnp.cos(angles)
    sine = jnp.sin(angles)
    return (
        jnp.concatenate([cosine, cosine], axis=1),
        jnp.concatenate([-sine, sine], axis=1),
    )


def fetch(values, source):
    sizes = [lax.axis_size(axis) for axis in mesh_axes]
    pairs = []
    for c in range(sizes[0]):
        for t in range(sizes[1]):
            for d in range(sizes[2]):
                fc, ft, fd = source(c, t, d)
                pairs.append(((fc * sizes[1] + ft) * sizes[2] + fd, (c * sizes[1] + t) * sizes[2] + d))
    return lax.ppermute(values, mesh_axes, pairs)


def from_z(values, step):
    count = lax.axis_size("ctx")
    return fetch(values, lambda c, t, d: ((c + step) % count, t, d))


def from_x(values, step):
    count = lax.axis_size("dp") // 2
    return fetch(values, lambda c, t, d: (c, t, ((d // 2 + step) % count) * 2 + d % 2))


def from_y(values):
    return fetch(values, lambda c, t, d: (c, t, d ^ 1))


def from_tp(values, flip):
    return fetch(values, lambda c, t, d: (c, t ^ flip, d))


def z_ring(own):
    up = [own]
    down = [own]
    for _ in range(3):
        up.append(from_z(up[-1], 1))
        down.append(from_z(down[-1], -1))
    return up, down


def gather_qkv(own, split):
    y = lax.axis_index("dp") % 2
    other = from_y(own)
    pair = jnp.where(
        y == 0, jnp.concatenate([own, other], axis=0), jnp.concatenate([other, own], axis=0)
    )
    left = pair[:, :split]
    right = pair[:, split:]
    line = jnp.concatenate(
        [left, from_x(left, 1), from_x(left, 2), from_x(left, -1)], axis=0
    )
    up_right, down_right = z_ring(right)
    column = jnp.concatenate(
        up_right + [from_z(up_right[3], 1)] + down_right[:0:-1], axis=0
    )
    up, down = z_ring(line)
    middle = line.shape[0] // 2
    left_pieces = up + [
        from_z(up[3][:middle], 1),
        from_z(down[3][middle:], -1),
    ] + down[:0:-1]
    next_x = from_x(column, 1)
    last_x = from_x(column, -1)
    middle = column.shape[0] // 2
    right_pieces = [
        column,
        next_x,
        from_x(next_x[:middle], 1),
        from_x(last_x[middle:], -1),
        last_x,
    ]
    return left_pieces, right_pieces


def norm_kernel(place_ref, tokens_ref, gain_ref, out_ref, *, groups, columns):
    rows, width = tokens_ref.shape
    total = jnp.zeros((rows, LANES), jnp.float32)
    for block in range(width // LANES):
        part = tokens_ref[:, block * LANES : (block + 1) * LANES].astype(jnp.float32)
        total += part * part
    mean = jnp.sum(total, axis=1, keepdims=True) / width
    rate = lax.rsqrt(mean + norm_epsilon)
    for group in range(groups):
        from_group = lax.rem(place_ref[0] + group, groups)
        for column in range(columns):
            from_column = lax.rem(place_ref[1] + column, columns)
            source = pl.multiple_of((from_group * columns + from_column) * LANES, LANES)
            block = group * columns + column
            part = tokens_ref[:, pl.ds(source, LANES)].astype(jnp.float32)
            part = part * rate * gain_ref[:, pl.ds(source, LANES)]
            out_ref[:, block * LANES : (block + 1) * LANES] = part.astype(jnp.bfloat16)


def norm(place, tokens, gain, groups, columns, rows=64):
    count, width = tokens.shape
    return pl.pallas_call(
        lambda *refs: norm_kernel(*refs, groups=groups, columns=columns),
        grid_spec=pltpu.PrefetchScalarGridSpec(
            num_scalar_prefetch=1,
            grid=(count // rows,),
            in_specs=[
                pl.BlockSpec((rows, width), lambda i, _: (i, 0)),
                pl.BlockSpec((1, width), lambda i, _: (0, 0)),
            ],
            out_specs=pl.BlockSpec((rows, width), lambda i, _: (i, 0)),
        ),
        out_shape=jax.ShapeDtypeStruct((count, width), jnp.bfloat16),
        name="norm",
    )(place, tokens, gain.reshape(1, width))


def project_kernel(*refs, left_count, right_count, groups, columns, heads):
    left = refs[:left_count]
    right = refs[left_count : left_count + right_count]
    rest = refs[left_count + right_count :]
    normed_any, cos_ref, sin_ref, seg_ref, query_ref, key_ref, value_ref = rest[:7]
    left_buf, right_buf, normed_ref, sems = rest[7:]
    half_rows = query_ref.shape[1]
    model_width = normed_ref.shape[1]
    copies = [pltpu.make_async_copy(normed_any, normed_ref, sems.at[0])]
    for pieces, buffer in ((left, left_buf), (right, right_buf)):
        start = 0
        for piece in pieces:
            size = piece.shape[0]
            copies.append(
                pltpu.make_async_copy(
                    piece, buffer.at[pl.ds(start, size)], sems.at[len(copies)]
                )
            )
            start += size
    for copy in copies:
        copy.start()
    copies[0].wait()
    for copy in copies[1 : 1 + left_count]:
        copy.wait()
    left_sums = jnp.dot(normed_ref[...], left_buf[...], preferred_element_type=jnp.float32)
    for copy in copies[1 + left_count :]:
        copy.wait()
    depth = groups * LANES
    right_sums = None
    for column in range(columns):
        lhs = jnp.concatenate(
            [
                normed_ref[:, (g * columns + column) * LANES : (g * columns + column + 1) * LANES]
                for g in range(groups)
            ],
            axis=1,
        )
        term = jnp.dot(
            lhs,
            right_buf[column * depth : (column + 1) * depth],
            preferred_element_type=jnp.float32,
        )
        right_sums = term if right_sums is None else right_sums + term
    cosine = cos_ref[...]
    sine = sin_ref[...]
    left_heads = left_sums.shape[1] // HD
    for head in range(heads + 2):
        if head < left_heads:
            part = left_sums[:, head * HD : (head + 1) * HD]
        else:
            part = right_sums[:, (head - left_heads) * HD : (head - left_heads + 1) * HD]
        if head <= heads:
            part = part * cosine + pltpu.roll(part, HD // 2, 1) * sine
        part = part.astype(jnp.bfloat16)
        for half in range(2):
            rows = part[half * half_rows : (half + 1) * half_rows]
            if head < heads:
                query_ref[half, :, head * HD : (head + 1) * HD] = rows
            elif head == heads:
                key_ref[half, :half_rows, :] = rows
                key_ref[half, half_rows:, :] = seg_ref[half]
            else:
                value_ref[half] = rows


def project(left, right, normed, cosine, sine, seg_rows, groups, columns, heads):
    count, model_width = normed.shape
    half_rows = count // 2
    any_spec = pl.BlockSpec(memory_space=pl.ANY)
    vmem_spec = pl.BlockSpec(memory_space=pltpu.VMEM)
    pieces = len(left) + len(right)
    return pl.pallas_call(
        lambda *refs: project_kernel(
            *refs,
            left_count=len(left),
            right_count=len(right),
            groups=groups,
            columns=columns,
            heads=heads,
        ),
        in_specs=[any_spec] * (pieces + 1) + [vmem_spec] * 3,
        out_specs=[vmem_spec] * 3,
        out_shape=[
            jax.ShapeDtypeStruct((2, half_rows, heads * HD), jnp.bfloat16),
            jax.ShapeDtypeStruct((2, half_rows + seg_rows.shape[1], HD), jnp.bfloat16),
            jax.ShapeDtypeStruct((2, half_rows, HD), jnp.bfloat16),
        ],
        scratch_shapes=[
            pltpu.VMEM((model_width, left[0].shape[1]), jnp.bfloat16),
            pltpu.VMEM((model_width, right[0].shape[1]), jnp.bfloat16),
            pltpu.VMEM((count, model_width), jnp.bfloat16),
            pltpu.SemaphoreType.DMA((pieces + 1,)),
        ],
        name="project",
    )(*left, *right, normed, cosine, sine, seg_rows)


def attend_kernel(place_ref, *refs, half_rows, heads, ctx_count):
    keys_any = refs[:ctx_count]
    values_any = refs[ctx_count : 2 * ctx_count]
    query_ref, seg_ref, out_ref, key_buf, value_buf, sems = refs[2 * ctx_count :]
    which = pl.program_id(0)
    ctx = place_ref[0]
    blocks = 2 * ctx_count

    @pl.when(which == 0)
    def _():
        copies = []
        for step in range(ctx_count):
            holder = lax.rem(ctx + step, ctx_count)
            for source, buffer in ((keys_any[step], key_buf), (values_any[step], value_buf)):
                copies.append(
                    pltpu.make_async_copy(source, buffer.at[holder], sems.at[len(copies)])
                )
        for copy in copies:
            copy.start()
        for copy in copies:
            copy.wait()

    seg_count = half_rows // LANES
    all_seg = key_buf[:, :, half_rows : half_rows + 16, :].astype(jnp.float32)
    all_seg = all_seg[:, :, :seg_count, :].reshape(-1, LANES)
    own_seg = seg_ref[0]
    first = jnp.zeros(own_seg.shape, jnp.int32)
    for doc in range(1, 4):
        before = jnp.sum((all_seg < doc).astype(jnp.float32)).astype(jnp.int32)
        first = jnp.where(own_seg == doc, before, first)
    low = jnp.min(first) // half_rows

    queries = jnp.concatenate(
        [query_ref[0, :, h * HD : (h + 1) * HD] for h in range(heads)], axis=0
    )
    rows = heads * half_rows
    scale = 1.0 / HD**0.5
    own = jnp.where(which == 0, ctx, blocks - 1 - ctx)
    key_iota = lax.broadcasted_iota(jnp.int32, (half_rows, rows), 0)
    query_pos = own * half_rows + lax.rem(
        lax.broadcasted_iota(jnp.int32, (1, rows), 1), half_rows
    )

    def step(block, state):
        highest, totals, accum = state
        second = block >= blocks // 2
        holder = jnp.where(second, blocks - 1 - block, block)
        half = jnp.where(second, 1, 0)
        keys = key_buf[holder, half, :half_rows, :]
        values = value_buf[holder, half]
        scores = dot_dims(keys, queries, ((1,), (1,))) * scale
        key_pos = block * half_rows + key_iota
        allowed = (key_pos <= query_pos) & (key_pos >= first)
        limited = jnp.where(allowed, scores, masked_score)
        new_high = jnp.maximum(highest, jnp.max(limited, axis=0, keepdims=True))
        shrink = jnp.exp(highest - new_high)
        weights = jnp.where(allowed, jnp.exp(scores - new_high), 0.0)
        new_totals = totals * shrink + jnp.sum(weights, axis=0, keepdims=True)
        added = dot_dims(values, weights.astype(jnp.bfloat16), ((0,), (0,)))
        return (new_high, new_totals, accum * shrink + added)

    start = (
        jnp.full((1, rows), masked_score, jnp.float32),
        jnp.zeros((1, rows), jnp.float32),
        jnp.zeros((HD, rows), jnp.float32),
    )
    _, totals, accum = lax.fori_loop(low, own + 1, step, start)
    mixed = (accum / totals).astype(jnp.bfloat16)
    for h in range(heads):
        out_ref[0, :, h * HD : (h + 1) * HD] = mixed[:, h * half_rows : (h + 1) * half_rows].T


def attend(place, keys, values, queries, seg, half_rows, heads):
    width = heads * HD
    ctx_count = len(keys)
    return pl.pallas_call(
        lambda *refs: attend_kernel(
            *refs, half_rows=half_rows, heads=heads, ctx_count=ctx_count
        ),
        grid_spec=pltpu.PrefetchScalarGridSpec(
            num_scalar_prefetch=1,
            grid=(2,),
            in_specs=[pl.BlockSpec(memory_space=pl.ANY)] * (2 * ctx_count)
            + [
                pl.BlockSpec((1, half_rows, width), lambda i, _: (i, 0, 0)),
                pl.BlockSpec((1, 1, heads * half_rows), lambda i, _: (i, 0, 0)),
            ],
            out_specs=pl.BlockSpec((1, half_rows, width), lambda i, _: (i, 0, 0)),
            scratch_shapes=[
                pltpu.VMEM((ctx_count,) + keys[0].shape, jnp.bfloat16),
                pltpu.VMEM((ctx_count,) + values[0].shape, jnp.bfloat16),
                pltpu.SemaphoreType.DMA((2 * ctx_count,)),
            ],
        ),
        out_shape=jax.ShapeDtypeStruct((2, half_rows, width), jnp.bfloat16),
        name="attend",
    )(place, *keys, *values, queries, seg)


def blend_kernel(owner_ref, *refs):
    weight_ref, out_ref, square_ref = refs[-3:]
    total = None
    for step, mixed_ref in enumerate(refs[:-3]):
        width = mixed_ref.shape[1]
        columns = pl.ds(pl.multiple_of(owner_ref[step] * width, LANES), width)
        term = dot_dims(mixed_ref[...], weight_ref[:, columns], ((1,), (1,)))
        term = term.astype(jnp.bfloat16).astype(jnp.float32)
        total = term if total is None else total + term
    branch = total.astype(jnp.bfloat16)
    out_ref[...] = branch
    square = jnp.square(branch.astype(jnp.float32))
    part = jnp.sum(square.reshape(-1, 8, square.shape[1]), axis=0)

    @pl.when(pl.program_id(0) == 0)
    def _():
        square_ref[...] = jnp.zeros_like(square_ref)

    square_ref[...] += part


def blend(owners, mixed, weight, rows=128):
    count, width = mixed[0].shape
    features = weight.shape[0]
    return pl.pallas_call(
        blend_kernel,
        grid_spec=pltpu.PrefetchScalarGridSpec(
            num_scalar_prefetch=1,
            grid=(count // rows,),
            in_specs=[pl.BlockSpec((rows, width), lambda i, _: (i, 0))] * len(mixed)
            + [pl.BlockSpec(weight.shape, lambda i, _: (0, 0))],
            out_specs=[
                pl.BlockSpec((rows, features), lambda i, _: (i, 0)),
                pl.BlockSpec((8, features), lambda i, _: (0, 0)),
            ],
        ),
        out_shape=[
            jax.ShapeDtypeStruct((count, features), jnp.bfloat16),
            jax.ShapeDtypeStruct((8, features), jnp.float32),
        ],
        name="blend",
    )(owners, *mixed, weight)


def shards(
    tokens,
    norm_gain,
    query_weight,
    key_weight,
    value_weight,
    output_weight,
    query_noise,
    key_noise,
    value_noise,
    output_noise,
    sign,
    segment_ids,
    doc_weight,
):
    factor = sign[0].astype(jnp.float32) * perturb_step
    half_rows = tokens.shape[2]
    model_width = tokens.shape[3]
    local_rows = 2 * half_rows
    ctx = lax.axis_index("ctx")
    tp = lax.axis_index("tp")
    ctx_count = lax.axis_size("ctx")
    columns = lax.axis_size("dp") // 2
    x = lax.axis_index("dp") // 2
    seq_len = local_rows * ctx_count
    heads = query_weight.shape[1] // HD
    width = heads * HD

    own_qkv = perturbed(
        jnp.concatenate([query_weight, key_weight, value_weight], axis=1),
        jnp.concatenate([query_noise, key_noise, value_noise], axis=1),
        factor,
    )
    own_out = perturbed(output_weight, output_noise, factor).T
    out_weight = lax.all_gather(own_out, ("ctx", "dp"), axis=0, tiled=True)
    left, right = gather_qkv(own_qkv, 3 * HD)

    place = jnp.stack([ctx, x]).astype(jnp.int32)
    normed = norm(place, tokens[0].reshape(local_rows, model_width), norm_gain, ctx_count, columns)
    offsets = jnp.arange(half_rows, dtype=jnp.int32)
    local_pos = jnp.concatenate(
        [ctx * half_rows + offsets, seq_len - (ctx + 1) * half_rows + offsets]
    )
    cosine, sine = rope_tables(local_pos)
    seg_rows = segment_ids[0].astype(jnp.bfloat16).reshape(2, half_rows // LANES, LANES)
    seg_rows = jnp.pad(seg_rows, ((0, 0), (0, 16 - seg_rows.shape[1]), (0, 0)))
    queries, own_keys, own_values = project(
        left, right, normed, cosine, sine, seg_rows, ctx_count, columns, heads
    )

    key_up, key_down = z_ring(own_keys)
    value_up, value_down = z_ring(own_values)
    keys = key_up + [from_z(key_up[3], 1)] + key_down[:0:-1]
    values = value_up + [from_z(value_down[3], -1)] + value_down[:0:-1]
    own_seg = jnp.tile(segment_ids[0], (1, heads)).reshape(2, 1, heads * half_rows)
    mixed = attend(place, keys, values, queries, own_seg, half_rows, heads)

    mixed = mixed.reshape(local_rows, width)
    near = from_tp(mixed, 1)
    far = from_tp(mixed, 2)
    both = from_tp(far, 1)
    owners = jnp.stack([tp, tp ^ 1, tp ^ 2, tp ^ 3]).astype(jnp.int32)
    branch, squares = blend(owners, [mixed, near, far, both], out_weight)
    local_total = jnp.sum(squares) * doc_weight[0]
    everyone = ctx_count * lax.axis_size("tp") * lax.axis_size("dp")
    shares = lax.all_to_all(
        jnp.broadcast_to(local_total, (everyone, LANES)), mesh_axes, 0, 0, tiled=True
    )
    loss = jnp.sum(shares[:, 0]) / (seq_len * model_width)
    return (branch.reshape(1, 2, half_rows, branch.shape[1]), loss.reshape(1))


def solution(mesh):
    return jax.shard_map(
        shards,
        mesh=mesh,
        in_specs=(
            P("dp", None, "ctx", None),
            P(),
            P(("ctx", "dp"), "tp"),
            P(("ctx", "dp"), "tp"),
            P(("ctx", "dp"), "tp"),
            P(None, ("tp", "ctx", "dp")),
            P(("ctx", "dp"), "tp"),
            P(("ctx", "dp"), "tp"),
            P(("ctx", "dp"), "tp"),
            P(None, ("tp", "ctx", "dp")),
            P(),
            P("dp", None, "ctx"),
            P("dp"),
        ),
        out_specs=(P("dp", None, "ctx", "tp"), P()),
        check_vma=False,
    )
```

```python
import math

import jax
import jax.numpy as jnp
from jax import lax
from jax.experimental import pallas as pl
from jax.experimental.pallas import tpu as pltpu
from jax.sharding import PartitionSpec as P

HD = 128
LANES = 128

perturb_step = 0.004
rope_base = 500000.0
norm_epsilon = 1e-05
masked_score = -1e30
mesh_axes = ("ctx", "tp", "dp")


def perturbed(weight, noise, factor):
    return (weight.astype(jnp.float32) + factor * noise.astype(jnp.float32)).astype(jnp.bfloat16)


def dot_dims(lhs, rhs, dims):
    return lax.dot_general(lhs, rhs, (dims, ((), ())), preferred_element_type=jnp.float32)


def rope_tables(positions):
    half = HD // 2
    inverse = rope_base ** (-jnp.arange(half, dtype=jnp.float32) * 2.0 / HD)
    angles = positions.astype(jnp.float32)[:, None] * inverse[None, :]
    cosine = jnp.cos(angles)
    sine = jnp.sin(angles)
    return (
        jnp.concatenate([cosine, cosine], axis=1),
        jnp.concatenate([-sine, sine], axis=1),
    )


def fetch(values, source):
    sizes = [lax.axis_size(axis) for axis in mesh_axes]
    pairs = []
    for c in range(sizes[0]):
        for t in range(sizes[1]):
            for d in range(sizes[2]):
                fc, ft, fd = source(c, t, d)
                pairs.append(((fc * sizes[1] + ft) * sizes[2] + fd, (c * sizes[1] + t) * sizes[2] + d))
    return lax.ppermute(values, mesh_axes, pairs)


def side(t):
    return 1 if t % 2 == 0 else -1


def walk_z(values):
    count = lax.axis_size("ctx")
    return fetch(values, lambda c, t, d: ((c + side(t)) % count, t, d))


def from_x(values, step):
    count = lax.axis_size("dp") // 2
    return fetch(values, lambda c, t, d: (c, t, ((d // 2 + step) % count) * 2 + d % 2))


def walk_x(values):
    count = lax.axis_size("dp") // 2
    return fetch(values, lambda c, t, d: (c, t, ((d // 2 + side(t)) % count) * 2 + d % 2))


def from_y(values):
    return fetch(values, lambda c, t, d: (c, t, d ^ 1))


def from_tp(values, flip):
    return fetch(values, lambda c, t, d: (c, t ^ flip, d))


def both_cores(own, core):
    other = from_tp(own, 1)
    return jnp.stack([jnp.where(core == 0, own, other), jnp.where(core == 0, other, own)])


def z_walk(both, core, cut):
    mine = []
    theirs = []
    last = both
    for _ in range(3):
        last = walk_z(last)
        mine.append(last)
        theirs.append(from_tp(last, 1))
    last = walk_z(cut(last, core))
    return mine + [last], theirs + [from_tp(last, 1)]


def cut_rows(values, core):
    half = values.shape[1] // 2
    return lax.dynamic_slice_in_dim(values, core * half, half, axis=1)


def gather_qkv(own, split, core):
    y = lax.axis_index("dp") % 2
    other = from_y(own)
    pair = jnp.where(
        y == 0, jnp.concatenate([own, other], axis=0), jnp.concatenate([other, own], axis=0)
    )
    left = pair[:, :split]
    right = both_cores(pair[:, split:], core)
    line = both_cores(
        jnp.concatenate([left, from_x(left, 1), from_x(left, 2), from_x(left, -1)], axis=0), core
    )
    steps = [right]
    back = []
    for _ in range(3):
        steps.append(walk_z(steps[-1]))
        back.append(from_tp(steps[-1], 1))
    steps.append(walk_z(steps[-1]))
    column = jnp.concatenate(steps + back[::-1], axis=1)
    mine, theirs = z_walk(line, core, cut_rows)
    beside = walk_x(column)
    rows = pair.shape[0]
    half = column.shape[1] // 2
    across = walk_x(lax.dynamic_slice_in_dim(beside, core * rows, half, axis=1))
    return (
        (line, mine, theirs),
        (column, beside, from_tp(beside, 1), across, from_tp(across, 1)),
    )


def norm_kernel(place_ref, tokens_ref, gain_ref, out_ref, *, groups, columns):
    rows, width = tokens_ref.shape
    total = jnp.zeros((rows, LANES), jnp.float32)
    for block in range(width // LANES):
        part = tokens_ref[:, block * LANES : (block + 1) * LANES].astype(jnp.float32)
        total += part * part
    mean = jnp.sum(total, axis=1, keepdims=True) / width
    rate = lax.rsqrt(mean + norm_epsilon)
    for group in range(groups):
        from_group = lax.rem(place_ref[0] + group, groups)
        for column in range(columns):
            from_column = lax.rem(place_ref[1] + column, columns)
            source = pl.multiple_of((from_group * columns + from_column) * LANES, LANES)
            block = group * columns + column
            part = tokens_ref[:, pl.ds(source, LANES)].astype(jnp.float32)
            part = part * rate * gain_ref[:, pl.ds(source, LANES)]
            out_ref[:, block * LANES : (block + 1) * LANES] = part.astype(jnp.bfloat16)


def norm(place, tokens, gain, groups, columns, rows=64):
    count, width = tokens.shape
    return pl.pallas_call(
        lambda *refs: norm_kernel(*refs, groups=groups, columns=columns),
        grid_spec=pltpu.PrefetchScalarGridSpec(
            num_scalar_prefetch=1,
            grid=(count // rows,),
            in_specs=[
                pl.BlockSpec((rows, width), lambda i, _: (i, 0)),
                pl.BlockSpec((1, width), lambda i, _: (0, 0)),
            ],
            out_specs=pl.BlockSpec((rows, width), lambda i, _: (i, 0)),
        ),
        out_shape=jax.ShapeDtypeStruct((count, width), jnp.bfloat16),
        name="norm",
    )(place, tokens, gain.reshape(1, width))


def turn(part, cosine, sine):
    return part * cosine + pltpu.roll(part, HD // 2, 1) * sine


def left_kernel(place_ref, *refs, ctx_count):
    line_any = refs[0]
    mine_any = refs[1 : 1 + ctx_count // 2]
    theirs_any = refs[1 + ctx_count // 2 : 1 + ctx_count]
    normed_any, cos_ref, sin_ref, out_ref, buffer, normed_ref, sems = refs[1 + ctx_count :]
    core = place_ref[2]
    depth = line_any.shape[1]
    half = depth // 2
    copies = [
        pltpu.make_async_copy(normed_any, normed_ref, sems.at[0]),
        pltpu.make_async_copy(line_any.at[core], buffer.at[pl.ds(0, depth)], sems.at[1]),
    ]
    middle = ctx_count // 2
    for step in range(1, middle + 1):
        for pieces, walker in ((mine_any, core), (theirs_any, 1 - core)):
            if step < middle:
                start = jnp.where(walker == 0, step, ctx_count - step) * depth
                size = depth
            else:
                start = middle * depth + walker * half
                size = half
            start = pl.multiple_of(start, half)
            copies.append(
                pltpu.make_async_copy(
                    pieces[step - 1].at[core],
                    buffer.at[pl.ds(start, size)],
                    sems.at[len(copies)],
                )
            )
    for copy in copies:
        copy.start()
    for copy in copies:
        copy.wait()
    sums = jnp.dot(normed_ref[...], buffer[...], preferred_element_type=jnp.float32)
    for head in range(sums.shape[1] // HD):
        columns = slice(head * HD, (head + 1) * HD)
        part = turn(sums[:, columns], cos_ref[...], sin_ref[...])
        out_ref[:, columns] = part.astype(jnp.bfloat16)


def project_left(place, pieces, normed, cosine, sine):
    line, mine, theirs = pieces
    count, model_width = normed.shape
    ctx_count = 2 * len(mine)
    width = line.shape[2]
    any_spec = pl.BlockSpec(memory_space=pl.ANY)
    vmem_spec = pl.BlockSpec(memory_space=pltpu.VMEM)
    smem_spec = pl.BlockSpec(memory_space=pltpu.SMEM)
    return pl.pallas_call(
        lambda *refs: left_kernel(*refs, ctx_count=ctx_count),
        in_specs=[smem_spec] + [any_spec] * (ctx_count + 2) + [vmem_spec] * 2,
        out_specs=vmem_spec,
        out_shape=jax.ShapeDtypeStruct((count, width), jnp.bfloat16),
        scratch_shapes=[
            pltpu.VMEM((model_width, width), jnp.bfloat16),
            pltpu.VMEM((count, model_width), jnp.bfloat16),
            pltpu.SemaphoreType.DMA((ctx_count + 2,)),
        ],
        name="project_left",
    )(place, line, *mine, *theirs, normed, cosine, sine)


def right_kernel(place_ref, *refs, ctx_count, columns):
    column_any, beside_any, back_any, across_any, rest_any = refs[:5]
    normed_any, cos_ref, sin_ref, seg_ref, query_ref, parcel_ref = refs[5:11]
    buffer, normed_ref, sems = refs[11:]
    core = place_ref[2]
    half_rows = parcel_ref.shape[1] // 2 - seg_ref.shape[1] // 2
    rows = column_any.shape[1] // ctx_count
    copies = [pltpu.make_async_copy(normed_any, normed_ref, sems.at[0])]

    def place_rows(source, entry, offset, walker, x_step):
        group = jnp.where(walker == 0, entry, lax.rem(ctx_count - entry, ctx_count))
        target = pl.multiple_of((group * columns + x_step) * rows, rows)
        copies.append(
            pltpu.make_async_copy(
                source.at[core, pl.ds(pl.multiple_of(offset, rows), rows)],
                buffer.at[pl.ds(target, rows)],
                sems.at[len(copies)],
            )
        )

    for entry in range(ctx_count):
        place_rows(column_any, entry, entry * rows, core, 0)
        for source, walker in ((beside_any, core), (back_any, 1 - core)):
            x_step = jnp.where(walker == 0, 1, columns - 1)
            place_rows(source, entry, entry * rows, walker, x_step)
    for entry in range(ctx_count // 2):
        for source, walker in ((across_any, core), (rest_any, 1 - core)):
            place_rows(source, entry + walker, entry * rows, walker, columns // 2)
    for copy in copies:
        copy.start()
    for copy in copies:
        copy.wait()
    sums = jnp.dot(normed_ref[...], buffer[...], preferred_element_type=jnp.float32)
    cosine = cos_ref[...]
    sine = sin_ref[...]
    heads = sums.shape[1] // HD - 2
    for head in range(heads):
        part = turn(sums[:, head * HD : (head + 1) * HD], cosine, sine)
        query_ref[:, head * HD : (head + 1) * HD] = part.astype(jnp.bfloat16)
    keys = turn(sums[:, heads * HD : (heads + 1) * HD], cosine, sine).astype(jnp.bfloat16)
    values = sums[:, (heads + 1) * HD :].astype(jnp.bfloat16)
    for half in range(2):
        parcel_ref[half, :half_rows] = keys[half * half_rows : (half + 1) * half_rows]
        parcel_ref[half, half_rows : 2 * half_rows] = values[
            half * half_rows : (half + 1) * half_rows
        ]
        parcel_ref[half, 2 * half_rows :] = seg_ref[half]


def project_right(place, pieces, normed, cosine, sine, seg_rows, ctx_count, columns):
    count, model_width = normed.shape
    width = pieces[0].shape[2]
    any_spec = pl.BlockSpec(memory_space=pl.ANY)
    vmem_spec = pl.BlockSpec(memory_space=pltpu.VMEM)
    smem_spec = pl.BlockSpec(memory_space=pltpu.SMEM)
    return pl.pallas_call(
        lambda *refs: right_kernel(*refs, ctx_count=ctx_count, columns=columns),
        in_specs=[smem_spec] + [any_spec] * 6 + [vmem_spec] * 3,
        out_specs=[vmem_spec] * 2,
        out_shape=[
            jax.ShapeDtypeStruct((count, width - 2 * HD), jnp.bfloat16),
            jax.ShapeDtypeStruct((2, count + seg_rows.shape[1], HD), jnp.bfloat16),
        ],
        scratch_shapes=[
            pltpu.VMEM((model_width, width), jnp.bfloat16),
            pltpu.VMEM((count, model_width), jnp.bfloat16),
            pltpu.SemaphoreType.DMA((1 + ctx_count * columns,)),
        ],
        name="project_right",
    )(place, *pieces, normed, cosine, sine, seg_rows)


def attend_kernel(place_ref, *refs, half_rows, heads, ctx_count, which):
    middle = ctx_count // 2
    both_any = refs[0]
    mine_any = refs[1 : 1 + middle]
    theirs_any = refs[1 + middle : 1 + ctx_count]
    left_ref, right_ref, seg_ref, out_ref, buffer, sems = refs[1 + ctx_count :]
    ctx = place_ref[0]
    core = place_ref[2]
    blocks = 2 * ctx_count

    copies = [pltpu.make_async_copy(both_any.at[core], buffer.at[ctx], sems.at[0])]
    for step in range(1, middle + 1):
        for pieces, walker in ((mine_any, core), (theirs_any, 1 - core)):
            distance = jnp.where(walker == 0, step, ctx_count - step)
            holder = lax.rem(ctx + distance, ctx_count)
            if step < middle:
                source = pieces[step - 1].at[core]
                target = buffer.at[holder]
            else:
                source = pieces[step - 1].at[core, 0]
                target = buffer.at[holder, walker]
            copies.append(pltpu.make_async_copy(source, target, sems.at[len(copies)]))
    for copy in copies:
        copy.start()
    for copy in copies:
        copy.wait()

    seg_count = half_rows // LANES
    all_seg = buffer[:, :, 2 * half_rows :, :].astype(jnp.float32)
    all_seg = all_seg[:, :, :seg_count, :].reshape(-1, LANES)
    own_seg = seg_ref[...]
    first = jnp.zeros(own_seg.shape, jnp.int32)
    for doc in range(1, 4):
        before = jnp.sum((all_seg < doc).astype(jnp.float32)).astype(jnp.int32)
        first = jnp.where(own_seg == doc, before, first)
    own = ctx if which == 0 else blocks - 1 - ctx
    low = jnp.min(first) // half_rows
    inner = jnp.minimum((jnp.max(first) + half_rows - 1) // half_rows, own)

    left_heads = left_ref.shape[1] // HD
    queries = [
        (left_ref if h < left_heads else right_ref)[
            :, (h % left_heads) * HD : (h % left_heads + 1) * HD
        ]
        for h in range(heads)
    ]
    factor = math.log2(math.e) / HD**0.5
    key_iota = lax.broadcasted_iota(jnp.int32, (half_rows, half_rows), 0)
    query_pos = own * half_rows + lax.broadcasted_iota(jnp.int32, (1, half_rows), 1)

    def step(block, state, masked):
        second = block >= ctx_count
        holder = jnp.where(second, blocks - 1 - block, block)
        half = jnp.where(second, 1, 0)
        keys = buffer[holder, half, :half_rows, :]
        values = buffer[holder, half, half_rows : 2 * half_rows, :]
        if masked:
            key_pos = block * half_rows + key_iota
            allowed = (key_pos <= query_pos) & (key_pos >= first)
        result = []
        for h in range(heads):
            highest, totals, accum = state[h]
            scores = dot_dims(keys, queries[h], ((1,), (1,)))
            limited = jnp.where(allowed, scores, masked_score) if masked else scores
            new_high = jnp.maximum(highest, jnp.max(limited, axis=0, keepdims=True))
            shrink = jnp.exp2((highest - new_high) * factor)
            weights = jnp.exp2((scores - new_high) * factor)
            if masked:
                weights = jnp.where(allowed, weights, 0.0)
            new_totals = totals * shrink + jnp.sum(weights, axis=0, keepdims=True)
            added = dot_dims(values, weights.astype(jnp.bfloat16), ((0,), (0,)))
            result.append((new_high, new_totals, accum * shrink + added))
        return tuple(result)

    state = tuple(
        (
            jnp.full((1, half_rows), masked_score, jnp.float32),
            jnp.zeros((1, half_rows), jnp.float32),
            jnp.zeros((HD, half_rows), jnp.float32),
        )
        for _ in range(heads)
    )
    state = lax.fori_loop(low, inner, lambda b, s: step(b, s, True), state)
    state = lax.fori_loop(inner, own, lambda b, s: step(b, s, False), state)
    state = step(own, state, True)
    for h in range(heads):
        _, totals, accum = state[h]
        out_ref[:, h * HD : (h + 1) * HD] = (accum / totals).astype(jnp.bfloat16).T


def attend(place, both, mine, theirs, left, right, seg, half_rows, heads, which):
    ctx_count = 2 * len(mine)
    any_spec = pl.BlockSpec(memory_space=pl.ANY)
    vmem_spec = pl.BlockSpec(memory_space=pltpu.VMEM)
    smem_spec = pl.BlockSpec(memory_space=pltpu.SMEM)
    rows = pl.BlockSpec((half_rows, left.shape[1]), lambda i: (which, 0))
    rest = pl.BlockSpec((half_rows, right.shape[1]), lambda i: (which, 0))
    return pl.pallas_call(
        lambda *refs: attend_kernel(
            *refs, half_rows=half_rows, heads=heads, ctx_count=ctx_count, which=which
        ),
        grid=(1,),
        in_specs=[smem_spec] + [any_spec] * (1 + ctx_count) + [rows, rest, vmem_spec],
        out_specs=pl.BlockSpec((half_rows, heads * HD), lambda i: (0, 0)),
        out_shape=jax.ShapeDtypeStruct((half_rows, heads * HD), jnp.bfloat16),
        scratch_shapes=[
            pltpu.VMEM((ctx_count,) + both.shape[1:], jnp.bfloat16),
            pltpu.SemaphoreType.DMA((1 + ctx_count,)),
        ],
        name="attend_second" if which else "attend_first",
    )(place, both, *mine, *theirs, left, right, seg)


def blend_kernel(owner_ref, *refs):
    mixed = refs[:8]
    weight_any, out_ref, square_ref, buffer, sems = refs[8:]
    half_rows, width = mixed[0].shape
    copies = []
    for step in range(4):
        columns = pl.ds(pl.multiple_of(owner_ref[step] * width, LANES), width)
        copies.append(
            pltpu.make_async_copy(weight_any.at[:, columns], buffer.at[step], sems.at[step])
        )
    for copy in copies:
        copy.start()
    total = None
    for step in range(4):
        copies[step].wait()
        lhs = jnp.concatenate([mixed[2 * step][...], mixed[2 * step + 1][...]], axis=0)
        term = dot_dims(lhs, buffer[step], ((1,), (1,)))
        term = term.astype(jnp.bfloat16).astype(jnp.float32)
        total = term if total is None else total + term
    branch = total.astype(jnp.bfloat16)
    out_ref[...] = branch
    square = jnp.square(branch.astype(jnp.float32))
    square = jnp.sum(square.reshape(-1, 8, square.shape[1]), axis=0)
    part = square[:, :LANES]
    for block in range(1, square.shape[1] // LANES):
        part += square[:, block * LANES : (block + 1) * LANES]
    square_ref[...] = part


def blend(owners, mixed, weight):
    half_rows, width = mixed[0].shape
    features = weight.shape[0]
    vmem_spec = pl.BlockSpec(memory_space=pltpu.VMEM)
    return pl.pallas_call(
        blend_kernel,
        in_specs=[pl.BlockSpec(memory_space=pltpu.SMEM)]
        + [vmem_spec] * len(mixed)
        + [pl.BlockSpec(memory_space=pl.ANY)],
        out_specs=[vmem_spec, vmem_spec],
        out_shape=[
            jax.ShapeDtypeStruct((2 * half_rows, features), jnp.bfloat16),
            jax.ShapeDtypeStruct((8, LANES), jnp.float32),
        ],
        scratch_shapes=[
            pltpu.VMEM((4, features, width), jnp.bfloat16),
            pltpu.SemaphoreType.DMA((4,)),
        ],
        name="blend",
    )(owners, *mixed, weight)


def shards(
    tokens,
    norm_gain,
    query_weight,
    key_weight,
    value_weight,
    output_weight,
    query_noise,
    key_noise,
    value_noise,
    output_noise,
    sign,
    segment_ids,
    doc_weight,
):
    factor = sign[0].astype(jnp.float32) * perturb_step
    half_rows = tokens.shape[2]
    model_width = tokens.shape[3]
    local_rows = 2 * half_rows
    ctx = lax.axis_index("ctx")
    tp = lax.axis_index("tp")
    ctx_count = lax.axis_size("ctx")
    columns = lax.axis_size("dp") // 2
    x = lax.axis_index("dp") // 2
    seq_len = local_rows * ctx_count
    heads = query_weight.shape[1] // HD
    width = heads * HD

    own_qkv = perturbed(
        jnp.concatenate([query_weight, key_weight, value_weight], axis=1),
        jnp.concatenate([query_noise, key_noise, value_noise], axis=1),
        factor,
    )
    own_out = perturbed(output_weight, output_noise, factor).T
    out_weight = lax.all_gather(own_out, ("ctx", "dp"), axis=0, tiled=True)
    core = tp % 2
    left, right = gather_qkv(own_qkv, 3 * HD, core)

    place = jnp.stack([ctx, x, core]).astype(jnp.int32)
    normed = norm(place, tokens[0].reshape(local_rows, model_width), norm_gain, ctx_count, columns)
    offsets = jnp.arange(half_rows, dtype=jnp.int32)
    local_pos = jnp.concatenate(
        [ctx * half_rows + offsets, seq_len - (ctx + 1) * half_rows + offsets]
    )
    cosine, sine = rope_tables(local_pos)
    seg_rows = segment_ids[0].astype(jnp.bfloat16).reshape(2, half_rows // LANES, LANES)
    seg_rows = jnp.pad(seg_rows, ((0, 0), (0, 16 - seg_rows.shape[1]), (0, 0)))
    left_queries = project_left(place, left, normed, cosine, sine)
    right_queries, parcel = project_right(
        place, right, normed, cosine, sine, seg_rows, ctx_count, columns
    )

    both = both_cores(parcel, core)
    mine, theirs = z_walk(
        both, core, lambda values, at: lax.dynamic_slice_in_dim(values, at, 1, axis=1)
    )
    parts = []
    for which in (1, 0):
        mixed = attend(
            place,
            both,
            mine,
            theirs,
            left_queries,
            right_queries,
            segment_ids[0, which].reshape(1, half_rows),
            half_rows,
            heads,
            which,
        )
        far = from_tp(mixed, 2)
        parts.append([mixed, from_tp(mixed, 1), far, from_tp(far, 1)])
    owners = jnp.stack([tp, tp ^ 1, tp ^ 2, tp ^ 3]).astype(jnp.int32)
    pairs = [part for step in range(4) for part in (parts[1][step], parts[0][step])]
    branch, squares = blend(owners, pairs, out_weight)
    local_total = jnp.sum(squares) * doc_weight[0]
    everyone = ctx_count * lax.axis_size("tp") * lax.axis_size("dp")
    shares = lax.all_to_all(
        jnp.broadcast_to(local_total, (everyone, LANES)), mesh_axes, 0, 0, tiled=True
    )
    loss = jnp.sum(shares[:, 0]) / (seq_len * model_width)
    return (branch.reshape(1, 2, half_rows, branch.shape[1]), loss.reshape(1))


def solution(mesh):
    return jax.shard_map(
        shards,
        mesh=mesh,
        in_specs=(
            P("dp", None, "ctx", None),
            P(),
            P(("ctx", "dp"), "tp"),
            P(("ctx", "dp"), "tp"),
            P(("ctx", "dp"), "tp"),
            P(None, ("tp", "ctx", "dp")),
            P(("ctx", "dp"), "tp"),
            P(("ctx", "dp"), "tp"),
            P(("ctx", "dp"), "tp"),
            P(None, ("tp", "ctx", "dp")),
            P(),
            P("dp", None, "ctx"),
            P("dp"),
        ),
        out_specs=(P("dp", None, "ctx", "tp"), P()),
        check_vma=False,
    )
```

```python
import math

import jax
import jax.numpy as jnp
from jax import lax
from jax.experimental import pallas as pl
from jax.experimental.pallas import tpu as pltpu
from jax.sharding import PartitionSpec as P

HD = 128
LANES = 128

perturb_step = 0.004
rope_base = 500000.0
norm_epsilon = 1e-05
masked_score = -1e30
mesh_axes = ("ctx", "tp", "dp")


def perturbed(weight, noise, factor):
    return (weight.astype(jnp.float32) + factor * noise.astype(jnp.float32)).astype(jnp.bfloat16)


def dot_dims(lhs, rhs, dims):
    return lax.dot_general(lhs, rhs, (dims, ((), ())), preferred_element_type=jnp.float32)


def rope_tables(positions):
    half = HD // 2
    inverse = rope_base ** (-jnp.arange(half, dtype=jnp.float32) * 2.0 / HD)
    angles = positions.astype(jnp.float32)[:, None] * inverse[None, :]
    cosine = jnp.cos(angles)
    sine = jnp.sin(angles)
    return (
        jnp.concatenate([cosine, cosine], axis=1),
        jnp.concatenate([-sine, sine], axis=1),
    )


def fetch(values, source):
    sizes = [lax.axis_size(axis) for axis in mesh_axes]
    pairs = []
    for c in range(sizes[0]):
        for t in range(sizes[1]):
            for d in range(sizes[2]):
                fc, ft, fd = source(c, t, d)
                pairs.append(((fc * sizes[1] + ft) * sizes[2] + fd, (c * sizes[1] + t) * sizes[2] + d))
    return lax.ppermute(values, mesh_axes, pairs)


def side(t):
    return 1 if t % 2 == 0 else -1


def walk_z(values):
    count = lax.axis_size("ctx")
    return fetch(values, lambda c, t, d: ((c + side(t)) % count, t, d))


def from_x(values, step):
    count = lax.axis_size("dp") // 2
    return fetch(values, lambda c, t, d: (c, t, ((d // 2 + step) % count) * 2 + d % 2))


def walk_x(values):
    count = lax.axis_size("dp") // 2
    return fetch(values, lambda c, t, d: (c, t, ((d // 2 + side(t)) % count) * 2 + d % 2))


def from_y(values):
    return fetch(values, lambda c, t, d: (c, t, d ^ 1))


def from_tp(values, flip):
    return fetch(values, lambda c, t, d: (c, t ^ flip, d))


def both_cores(own, core):
    other = from_tp(own, 1)
    return jnp.stack([jnp.where(core == 0, own, other), jnp.where(core == 0, other, own)])


def after(value, *others):
    return lax.optimization_barrier((value,) + others)[0]


def cut_rows(values, core):
    half = values.shape[1] // 2
    return lax.dynamic_slice_in_dim(values, core * half, half, axis=1)


def cut_half(values, core):
    return lax.dynamic_slice_in_dim(values, core, 1, axis=1)


def swap_all(steps):
    return [from_tp(step, 1) for step in steps]


def norm_kernel(place_ref, tokens_ref, gain_ref, out_ref, *, groups, columns):
    rows, width = tokens_ref.shape
    total = jnp.zeros((rows, LANES), jnp.float32)
    for block in range(width // LANES):
        part = tokens_ref[:, block * LANES : (block + 1) * LANES].astype(jnp.float32)
        total += part * part
    mean = jnp.sum(total, axis=1, keepdims=True) / width
    rate = jnp.broadcast_to(lax.rsqrt(mean + norm_epsilon), (rows, LANES))
    for group in range(groups):
        from_group = lax.rem(place_ref[0] + group, groups)
        for column in range(columns):
            from_column = lax.rem(place_ref[1] + column, columns)
            source = pl.multiple_of((from_group * columns + from_column) * LANES, LANES)
            block = group * columns + column
            part = tokens_ref[:, pl.ds(source, LANES)].astype(jnp.float32)
            part = part * rate * gain_ref[:, pl.ds(source, LANES)]
            out_ref[:, block * LANES : (block + 1) * LANES] = part.astype(jnp.bfloat16)


def norm(place, tokens, gain, groups, columns, rows=64):
    count, width = tokens.shape
    return pl.pallas_call(
        lambda *refs: norm_kernel(*refs, groups=groups, columns=columns),
        grid_spec=pltpu.PrefetchScalarGridSpec(
            num_scalar_prefetch=1,
            grid=(count // rows,),
            in_specs=[
                pl.BlockSpec((rows, width), lambda i, _: (i, 0)),
                pl.BlockSpec((1, width), lambda i, _: (0, 0)),
            ],
            out_specs=pl.BlockSpec((rows, width), lambda i, _: (i, 0)),
        ),
        out_shape=jax.ShapeDtypeStruct((count, width), jnp.bfloat16),
        name="norm",
    )(place, tokens, gain.reshape(1, width))


def turn(part, cosine, sine):
    return part * cosine + pltpu.roll(part, HD // 2, 1) * sine


def left_kernel(place_ref, *refs, ctx_count):
    line_any = refs[0]
    mine_any = refs[1 : 1 + ctx_count // 2]
    theirs_any = refs[1 + ctx_count // 2 : 1 + ctx_count]
    normed_any, cos_ref, sin_ref, out_ref, buffer, normed_ref, sems = refs[1 + ctx_count :]
    core = place_ref[2]
    depth = line_any.shape[1]
    half = depth // 2
    copies = [
        pltpu.make_async_copy(normed_any, normed_ref, sems.at[0]),
        pltpu.make_async_copy(line_any.at[core], buffer.at[pl.ds(0, depth)], sems.at[1]),
    ]
    middle = ctx_count // 2
    for step in range(1, middle + 1):
        for pieces, walker in ((mine_any, core), (theirs_any, 1 - core)):
            if step < middle:
                start = jnp.where(walker == 0, step, ctx_count - step) * depth
                size = depth
            else:
                start = middle * depth + walker * half
                size = half
            start = pl.multiple_of(start, half)
            copies.append(
                pltpu.make_async_copy(
                    pieces[step - 1].at[core],
                    buffer.at[pl.ds(start, size)],
                    sems.at[len(copies)],
                )
            )
    for copy in copies:
        copy.start()
    for copy in copies:
        copy.wait()
    sums = jnp.dot(normed_ref[...], buffer[...], preferred_element_type=jnp.float32)
    for head in range(sums.shape[1] // HD):
        columns = slice(head * HD, (head + 1) * HD)
        part = turn(sums[:, columns], cos_ref[...], sin_ref[...])
        out_ref[:, columns] = part.astype(jnp.bfloat16)


def project_left(place, pieces, normed, cosine, sine):
    line, mine, theirs = pieces
    count, model_width = normed.shape
    ctx_count = 2 * len(mine)
    width = line.shape[2]
    any_spec = pl.BlockSpec(memory_space=pl.ANY)
    vmem_spec = pl.BlockSpec(memory_space=pltpu.VMEM)
    smem_spec = pl.BlockSpec(memory_space=pltpu.SMEM)
    return pl.pallas_call(
        lambda *refs: left_kernel(*refs, ctx_count=ctx_count),
        in_specs=[smem_spec] + [any_spec] * (ctx_count + 2) + [vmem_spec] * 2,
        out_specs=vmem_spec,
        out_shape=jax.ShapeDtypeStruct((count, width), jnp.bfloat16),
        scratch_shapes=[
            pltpu.VMEM((model_width, width), jnp.bfloat16),
            pltpu.VMEM((count, model_width), jnp.bfloat16),
            pltpu.SemaphoreType.DMA((ctx_count + 2,)),
        ],
        name="project_left",
    )(place, line, *mine, *theirs, normed, cosine, sine)


def right_kernel(place_ref, *refs, ctx_count, columns):
    column_any, beside_any, back_any, across_any, rest_any = refs[:5]
    normed_any, cos_ref, sin_ref, seg_ref, key_ref, value_ref = refs[5:11]
    buffer, normed_ref, sems = refs[11:]
    core = place_ref[2]
    half_rows = value_ref.shape[1]
    rows = column_any.shape[1] // ctx_count
    copies = [pltpu.make_async_copy(normed_any, normed_ref, sems.at[0])]

    def place_rows(source, entry, offset, walker, x_step):
        group = jnp.where(walker == 0, entry, lax.rem(ctx_count - entry, ctx_count))
        target = pl.multiple_of((group * columns + x_step) * rows, rows)
        copies.append(
            pltpu.make_async_copy(
                source.at[core, pl.ds(pl.multiple_of(offset, rows), rows)],
                buffer.at[pl.ds(target, rows)],
                sems.at[len(copies)],
            )
        )

    for entry in range(ctx_count):
        place_rows(column_any, entry, entry * rows, core, 0)
        for source, walker in ((beside_any, core), (back_any, 1 - core)):
            x_step = jnp.where(walker == 0, 1, columns - 1)
            place_rows(source, entry, entry * rows, walker, x_step)
    for entry in range(ctx_count // 2):
        for source, walker in ((across_any, core), (rest_any, 1 - core)):
            place_rows(source, entry + walker, entry * rows, walker, columns // 2)
    for copy in copies:
        copy.start()
    for copy in copies:
        copy.wait()
    sums = jnp.dot(normed_ref[...], buffer[...], preferred_element_type=jnp.float32)
    keys = turn(sums[:, :HD], cos_ref[...], sin_ref[...]).astype(jnp.bfloat16)
    values = sums[:, HD:].astype(jnp.bfloat16)
    for half in range(2):
        rows_of = slice(half * half_rows, (half + 1) * half_rows)
        key_ref[half, :half_rows] = keys[rows_of]
        key_ref[half, half_rows:] = seg_ref[half]
        value_ref[half] = values[rows_of]


def project_right(place, pieces, normed, cosine, sine, seg_rows, ctx_count, columns):
    count, model_width = normed.shape
    width = pieces[0].shape[2]
    any_spec = pl.BlockSpec(memory_space=pl.ANY)
    vmem_spec = pl.BlockSpec(memory_space=pltpu.VMEM)
    smem_spec = pl.BlockSpec(memory_space=pltpu.SMEM)
    return pl.pallas_call(
        lambda *refs: right_kernel(*refs, ctx_count=ctx_count, columns=columns),
        in_specs=[smem_spec] + [any_spec] * 6 + [vmem_spec] * 3,
        out_specs=[vmem_spec] * 2,
        out_shape=[
            jax.ShapeDtypeStruct((2, count // 2 + seg_rows.shape[1], HD), jnp.bfloat16),
            jax.ShapeDtypeStruct((2, count // 2, HD), jnp.bfloat16),
        ],
        scratch_shapes=[
            pltpu.VMEM((model_width, width), jnp.bfloat16),
            pltpu.VMEM((count, model_width), jnp.bfloat16),
            pltpu.SemaphoreType.DMA((1 + ctx_count * columns,)),
        ],
        name="project_right",
    )(place, *pieces, normed, cosine, sine, seg_rows)


def attend_kernel(place_ref, *refs, half_rows, heads, ctx_count, which):
    middle = ctx_count // 2
    query_ref, seg_ref, out_ref, key_buf, value_buf, sems = refs[2 * (1 + ctx_count) :]
    ctx = place_ref[0]
    core = place_ref[2]
    blocks = 2 * ctx_count

    copies = []
    for start, buffer in ((0, key_buf), (1 + ctx_count, value_buf)):
        pieces = refs[start : start + 1 + ctx_count]
        copies.append((pieces[0].at[core], buffer.at[ctx]))
        for step in range(1, middle + 1):
            for piece, walker in ((pieces[step], core), (pieces[step + middle], 1 - core)):
                distance = jnp.where(walker == 0, step, ctx_count - step)
                holder = lax.rem(ctx + distance, ctx_count)
                if step < middle:
                    copies.append((piece.at[core], buffer.at[holder]))
                else:
                    copies.append((piece.at[core, 0], buffer.at[holder, walker]))
    copies = [
        pltpu.make_async_copy(source, target, sems.at[at])
        for at, (source, target) in enumerate(copies)
    ]
    for copy in copies:
        copy.start()
    for copy in copies:
        copy.wait()

    seg_count = half_rows // LANES
    all_seg = key_buf[:, :, half_rows:, :].astype(jnp.float32)
    all_seg = all_seg[:, :, :seg_count, :].reshape(-1, LANES)
    own_seg = seg_ref[...]
    first = jnp.zeros(own_seg.shape, jnp.int32)
    for doc in range(1, 4):
        before = jnp.sum(
            (all_seg < doc).astype(jnp.float32), axis=(0, 1), keepdims=True
        ).astype(jnp.int32)
        first = jnp.where(own_seg == doc, before, first)
    own = ctx if which == 0 else blocks - 1 - ctx
    low = jnp.min(first) // half_rows
    inner = jnp.minimum((jnp.max(first) + half_rows - 1) // half_rows, own)

    queries = [query_ref[:, h * HD : (h + 1) * HD] for h in range(heads)]
    factor = math.log2(math.e) / HD**0.5
    key_iota = lax.broadcasted_iota(jnp.int32, (half_rows, half_rows), 0)
    query_pos = own * half_rows + lax.broadcasted_iota(jnp.int32, (1, half_rows), 1)

    def step(block, state, masked):
        second = block >= ctx_count
        holder = jnp.where(second, blocks - 1 - block, block)
        half = jnp.where(second, 1, 0)
        keys = key_buf[holder, half, :half_rows, :]
        values = value_buf[holder, half]
        if masked:
            key_pos = block * half_rows + key_iota
            allowed = (key_pos <= query_pos) & (key_pos >= first)
        result = []
        for h in range(heads):
            highest, totals, accum = state[h]
            scores = dot_dims(keys, queries[h], ((1,), (1,)))
            limited = jnp.where(allowed, scores, masked_score) if masked else scores
            new_high = jnp.maximum(highest, jnp.max(limited, axis=0, keepdims=True))
            shrink = jnp.exp2((highest - new_high) * factor)
            weights = jnp.exp2((scores - new_high) * factor)
            if masked:
                weights = jnp.where(allowed, weights, 0.0)
            new_totals = totals * shrink + jnp.sum(weights, axis=0, keepdims=True)
            added = dot_dims(values, weights.astype(jnp.bfloat16), ((0,), (0,)))
            result.append((new_high, new_totals, accum * shrink + added))
        return tuple(result)

    state = tuple(
        (
            jnp.full((1, half_rows), masked_score, jnp.float32),
            jnp.zeros((1, half_rows), jnp.float32),
            jnp.zeros((HD, half_rows), jnp.float32),
        )
        for _ in range(heads)
    )
    state = lax.fori_loop(low, inner, lambda b, s: step(b, s, True), state)
    state = lax.fori_loop(inner, own, lambda b, s: step(b, s, False), state)
    state = step(own, state, True)
    for h in range(heads):
        _, totals, accum = state[h]
        out_ref[:, h * HD : (h + 1) * HD] = (accum / totals).astype(jnp.bfloat16).T


def attend(place, keys, values, queries, seg, half_rows, heads, which):
    ctx_count = len(keys) - 1
    any_spec = pl.BlockSpec(memory_space=pl.ANY)
    vmem_spec = pl.BlockSpec(memory_space=pltpu.VMEM)
    smem_spec = pl.BlockSpec(memory_space=pltpu.SMEM)
    rows = pl.BlockSpec((half_rows, heads * HD), lambda i: (which, 0))
    pieces = 2 * (1 + ctx_count)
    return pl.pallas_call(
        lambda *refs: attend_kernel(
            *refs, half_rows=half_rows, heads=heads, ctx_count=ctx_count, which=which
        ),
        grid=(1,),
        in_specs=[smem_spec] + [any_spec] * pieces + [rows, vmem_spec],
        out_specs=pl.BlockSpec((half_rows, heads * HD), lambda i: (0, 0)),
        out_shape=jax.ShapeDtypeStruct((half_rows, heads * HD), jnp.bfloat16),
        scratch_shapes=[
            pltpu.VMEM((ctx_count,) + keys[0].shape[1:], jnp.bfloat16),
            pltpu.VMEM((ctx_count,) + values[0].shape[1:], jnp.bfloat16),
            pltpu.SemaphoreType.DMA((pieces,)),
        ],
        name="attend_second" if which else "attend_first",
    )(place, *keys, *values, queries, seg)


def blend_kernel(owner_ref, *refs):
    mixed = refs[:8]
    weight_any, out_ref, square_ref, buffer, sems = refs[8:]
    half_rows, width = mixed[0].shape
    copies = []
    for step in range(4):
        columns = pl.ds(pl.multiple_of(owner_ref[step] * width, LANES), width)
        copies.append(
            pltpu.make_async_copy(weight_any.at[:, columns], buffer.at[step], sems.at[step])
        )
    for copy in copies:
        copy.start()
    total = None
    for step in range(4):
        copies[step].wait()
        lhs = jnp.concatenate([mixed[2 * step][...], mixed[2 * step + 1][...]], axis=0)
        term = dot_dims(lhs, buffer[step], ((1,), (1,)))
        term = term.astype(jnp.bfloat16).astype(jnp.float32)
        total = term if total is None else total + term
    branch = total.astype(jnp.bfloat16)
    out_ref[...] = branch
    square = jnp.square(branch.astype(jnp.float32))
    square = jnp.sum(square.reshape(-1, 8, square.shape[1]), axis=0)
    part = square[:, :LANES]
    for block in range(1, square.shape[1] // LANES):
        part += square[:, block * LANES : (block + 1) * LANES]
    square_ref[...] = part


def blend(owners, mixed, weight):
    half_rows, width = mixed[0].shape
    features = weight.shape[0]
    vmem_spec = pl.BlockSpec(memory_space=pltpu.VMEM)
    return pl.pallas_call(
        blend_kernel,
        in_specs=[pl.BlockSpec(memory_space=pltpu.SMEM)]
        + [vmem_spec] * len(mixed)
        + [pl.BlockSpec(memory_space=pl.ANY)],
        out_specs=[vmem_spec, vmem_spec],
        out_shape=[
            jax.ShapeDtypeStruct((2 * half_rows, features), jnp.bfloat16),
            jax.ShapeDtypeStruct((8, LANES), jnp.float32),
        ],
        scratch_shapes=[
            pltpu.VMEM((4, features, width), jnp.bfloat16),
            pltpu.SemaphoreType.DMA((4,)),
        ],
        name="blend",
    )(owners, *mixed, weight)


def shards(
    tokens,
    norm_gain,
    query_weight,
    key_weight,
    value_weight,
    output_weight,
    query_noise,
    key_noise,
    value_noise,
    output_noise,
    sign,
    segment_ids,
    doc_weight,
):
    factor = sign[0].astype(jnp.float32) * perturb_step
    half_rows = tokens.shape[2]
    model_width = tokens.shape[3]
    local_rows = 2 * half_rows
    ctx = lax.axis_index("ctx")
    tp = lax.axis_index("tp")
    ctx_count = lax.axis_size("ctx")
    columns = lax.axis_size("dp") // 2
    x = lax.axis_index("dp") // 2
    seq_len = local_rows * ctx_count
    heads = query_weight.shape[1] // HD
    width = heads * HD

    own_qkv = perturbed(
        jnp.concatenate([query_weight, key_weight, value_weight], axis=1),
        jnp.concatenate([query_noise, key_noise, value_noise], axis=1),
        factor,
    )
    core = tp % 2
    other = from_y(own_qkv)
    own_out = perturbed(after(output_weight, own_qkv), output_noise, factor).T
    out_weight = lax.all_gather(own_out, ("ctx", "dp"), axis=0, tiled=True)

    place = jnp.stack([ctx, x, core]).astype(jnp.int32)
    normed = norm(place, tokens[0].reshape(local_rows, model_width), norm_gain, ctx_count, columns)
    offsets = jnp.arange(half_rows, dtype=jnp.int32)
    local_pos = jnp.concatenate(
        [ctx * half_rows + offsets, seq_len - (ctx + 1) * half_rows + offsets]
    )
    cosine, sine = rope_tables(local_pos)
    seg_rows = segment_ids[0].astype(jnp.bfloat16).reshape(2, half_rows // LANES, LANES)
    seg_rows = jnp.pad(seg_rows, ((0, 0), (0, 16 - seg_rows.shape[1]), (0, 0)))
    other, normed, cosine, sine, seg_rows = lax.optimization_barrier(
        (other, normed, cosine, sine, seg_rows)
    )
    first = lax.axis_index("dp") % 2 == 0
    pair = jnp.where(
        first,
        jnp.concatenate([own_qkv, other], axis=0),
        jnp.concatenate([other, own_qkv], axis=0),
    )
    rows = pair.shape[0]

    left = pair[:, :width]
    beside = [from_x(left, step) for step in (1, 2, -1)]
    right = both_cores(pair[:, width:], core)
    right_1 = walk_z(right)
    line = both_cores(jnp.concatenate([left] + beside, axis=0), core)
    line_1 = walk_z(line)
    right_2 = walk_z(after(right_1, line))
    right_3 = walk_z(right_2)
    right_4 = walk_z(right_3)
    back = swap_all([right_1, right_2, right_3])
    column = jnp.concatenate([right, right_1, right_2, right_3, right_4] + back[::-1], axis=1)
    line_2 = walk_z(line_1)
    side_1 = walk_x(after(column, line_1))
    half = column.shape[1] // 2
    side_2 = walk_x(
        after(lax.dynamic_slice_in_dim(side_1, core * rows, half, axis=1), line_2)
    )
    line_3 = walk_z(line_2)
    line_4 = walk_z(cut_rows(line_3, core))
    sides = (column, side_1, from_tp(side_1, 1), side_2, from_tp(side_2, 1))
    own_keys, own_values = project_right(
        after(place, line_3), sides, normed, cosine, sine, seg_rows, ctx_count, columns
    )

    keys = [both_cores(own_keys, core)]
    values = [both_cores(own_values, core)]
    for step in range(1, ctx_count // 2):
        last_key, last_value = keys[-1], values[-1]
        if step == 2:
            last_key, last_value, line_4 = lax.optimization_barrier((last_key, last_value, line_4))
        keys.append(walk_z(last_key))
        values.append(walk_z(last_value))
    steps = [line_1, line_2, line_3, line_4]
    queries = project_left(place, (line, steps, swap_all(steps)), normed, cosine, sine)
    keys.append(walk_z(cut_half(keys[-1], core)))
    values.append(walk_z(cut_half(values[-1], core)))
    keys += swap_all(keys[1:])
    values += swap_all(values[1:])
    parts = []
    for which in (1, 0):
        mixed = attend(
            place,
            keys,
            values,
            queries,
            segment_ids[0, which].reshape(1, half_rows),
            half_rows,
            heads,
            which,
        )
        far = from_tp(mixed, 2)
        parts.append([mixed, from_tp(mixed, 1), far, from_tp(far, 1)])
    owners = jnp.stack([tp, tp ^ 1, tp ^ 2, tp ^ 3]).astype(jnp.int32)
    pairs = [part for step in range(4) for part in (parts[1][step], parts[0][step])]
    branch, squares = blend(owners, pairs, out_weight)
    local_total = jnp.sum(squares) * doc_weight[0]
    everyone = ctx_count * lax.axis_size("tp") * lax.axis_size("dp")
    shares = lax.all_to_all(
        jnp.broadcast_to(local_total, (everyone, LANES)), mesh_axes, 0, 0, tiled=True
    )
    loss = jnp.sum(shares[:, 0]) / (seq_len * model_width)
    return (branch.reshape(1, 2, half_rows, branch.shape[1]), loss.reshape(1))


def solution(mesh):
    return jax.shard_map(
        shards,
        mesh=mesh,
        in_specs=(
            P("dp", None, "ctx", None),
            P(),
            P(("ctx", "dp"), "tp"),
            P(("ctx", "dp"), "tp"),
            P(("ctx", "dp"), "tp"),
            P(None, ("tp", "ctx", "dp")),
            P(("ctx", "dp"), "tp"),
            P(("ctx", "dp"), "tp"),
            P(("ctx", "dp"), "tp"),
            P(None, ("tp", "ctx", "dp")),
            P(),
            P("dp", None, "ctx"),
            P("dp"),
        ),
        out_specs=(P("dp", None, "ctx", "tp"), P()),
        check_vma=False,
    )
```

```python
import math

import jax
import jax.numpy as jnp
from jax import lax
from jax.experimental import pallas as pl
from jax.experimental.pallas import tpu as pltpu
from jax.sharding import PartitionSpec as P

HD = 128
LANES = 128

perturb_step = 0.004
rope_base = 500000.0
norm_epsilon = 1e-05
masked_score = -1e30
mesh_axes = ("ctx", "tp", "dp")


def perturbed(weight, noise, factor):
    return (weight.astype(jnp.float32) + factor * noise.astype(jnp.float32)).astype(jnp.bfloat16)


def dot_dims(lhs, rhs, dims):
    return lax.dot_general(lhs, rhs, (dims, ((), ())), preferred_element_type=jnp.float32)


def rope_tables(positions):
    half = HD // 2
    inverse = rope_base ** (-jnp.arange(half, dtype=jnp.float32) * 2.0 / HD)
    angles = positions.astype(jnp.float32)[:, None] * inverse[None, :]
    cosine = jnp.cos(angles)
    sine = jnp.sin(angles)
    return (
        jnp.concatenate([cosine, cosine], axis=1),
        jnp.concatenate([-sine, sine], axis=1),
    )


def fetch(values, source):
    sizes = [lax.axis_size(axis) for axis in mesh_axes]
    pairs = []
    for c in range(sizes[0]):
        for t in range(sizes[1]):
            for d in range(sizes[2]):
                fc, ft, fd = source(c, t, d)
                pairs.append(((fc * sizes[1] + ft) * sizes[2] + fd, (c * sizes[1] + t) * sizes[2] + d))
    return lax.ppermute(values, mesh_axes, pairs)


def from_z(values, step):
    count = lax.axis_size("ctx")
    return fetch(values, lambda c, t, d: ((c + step) % count, t, d))


def from_x(values, step):
    count = lax.axis_size("dp") // 2
    return fetch(values, lambda c, t, d: (c, t, ((d // 2 + step) % count) * 2 + d % 2))


def from_y(values):
    return fetch(values, lambda c, t, d: (c, t, d ^ 1))


def from_tp(values, flip):
    return fetch(values, lambda c, t, d: (c, t ^ flip, d))


def after(value, *others):
    return lax.optimization_barrier((value,) + others)[0]


def norm_kernel(place_ref, tokens_ref, gain_ref, out_ref, *, groups, columns):
    rows, width = tokens_ref.shape
    total = jnp.zeros((rows, LANES), jnp.float32)
    for block in range(width // LANES):
        part = tokens_ref[:, block * LANES : (block + 1) * LANES].astype(jnp.float32)
        total += part * part
    mean = jnp.sum(total, axis=1, keepdims=True) / width
    rate = jnp.broadcast_to(lax.rsqrt(mean + norm_epsilon), (rows, LANES))
    for group in range(groups):
        from_group = lax.rem(place_ref[0] + group, groups)
        for column in range(columns):
            from_column = lax.rem(place_ref[1] + column, columns)
            source = pl.multiple_of((from_group * columns + from_column) * LANES, LANES)
            block = group * columns + column
            part = tokens_ref[:, pl.ds(source, LANES)].astype(jnp.float32)
            part = part * rate * gain_ref[:, pl.ds(source, LANES)]
            out_ref[:, block * LANES : (block + 1) * LANES] = part.astype(jnp.bfloat16)


def norm(place, tokens, gain, groups, columns, rows=64):
    count, width = tokens.shape
    return pl.pallas_call(
        lambda *refs: norm_kernel(*refs, groups=groups, columns=columns),
        grid_spec=pltpu.PrefetchScalarGridSpec(
            num_scalar_prefetch=1,
            grid=(count // rows,),
            in_specs=[
                pl.BlockSpec((rows, width), lambda i, _: (i, 0)),
                pl.BlockSpec((1, width), lambda i, _: (0, 0)),
            ],
            out_specs=pl.BlockSpec((rows, width), lambda i, _: (i, 0)),
        ),
        out_shape=jax.ShapeDtypeStruct((count, width), jnp.bfloat16),
        name="norm",
    )(place, tokens, gain.reshape(1, width))


def turn(part, cosine, sine):
    return part * cosine + pltpu.roll(part, HD // 2, 1) * sine


def load_pieces(pieces, normed_any, buffer, normed_ref, sems):
    copies = [pltpu.make_async_copy(normed_any, normed_ref, sems.at[0])]
    start = 0
    for piece in pieces:
        size = piece.shape[0]
        copies.append(
            pltpu.make_async_copy(piece, buffer.at[pl.ds(start, size)], sems.at[len(copies)])
        )
        start += size
    for copy in copies:
        copy.start()
    for copy in copies:
        copy.wait()


def pair_kernel(*refs, count):
    normed_any, cos_ref, sin_ref, seg_ref, key_ref, value_ref = refs[count : count + 6]
    buffer, normed_ref, sems = refs[count + 6 :]
    load_pieces(refs[:count], normed_any, buffer, normed_ref, sems)
    half_rows = value_ref.shape[1]
    sums = jnp.dot(normed_ref[...], buffer[...], preferred_element_type=jnp.float32)
    keys = turn(sums[:, :HD], cos_ref[...], sin_ref[...]).astype(jnp.bfloat16)
    values = sums[:, HD:].astype(jnp.bfloat16)
    for half in range(2):
        rows_of = slice(half * half_rows, (half + 1) * half_rows)
        key_ref[half, :half_rows] = keys[rows_of]
        key_ref[half, half_rows:] = seg_ref[half]
        value_ref[half] = values[rows_of]


def project_pair(pieces, normed, cosine, sine, seg_rows):
    count, model_width = normed.shape
    any_spec = pl.BlockSpec(memory_space=pl.ANY)
    vmem_spec = pl.BlockSpec(memory_space=pltpu.VMEM)
    return pl.pallas_call(
        lambda *refs: pair_kernel(*refs, count=len(pieces)),
        in_specs=[any_spec] * (len(pieces) + 1) + [vmem_spec] * 3,
        out_specs=[vmem_spec] * 2,
        out_shape=[
            jax.ShapeDtypeStruct((2, count // 2 + seg_rows.shape[1], HD), jnp.bfloat16),
            jax.ShapeDtypeStruct((2, count // 2, HD), jnp.bfloat16),
        ],
        scratch_shapes=[
            pltpu.VMEM((model_width, 2 * HD), jnp.bfloat16),
            pltpu.VMEM((count, model_width), jnp.bfloat16),
            pltpu.SemaphoreType.DMA((len(pieces) + 1,)),
        ],
        name="project_pair",
    )(*pieces, normed, cosine, sine, seg_rows)


def query_kernel(*refs, count, groups, columns):
    normed_any, cos_ref, sin_ref, out_ref = refs[count : count + 4]
    buffer, normed_ref, sems = refs[count + 4 :]
    load_pieces(refs[:count], normed_any, buffer, normed_ref, sems)
    depth = groups * LANES
    sums = None
    for column in range(columns):
        lhs = jnp.concatenate(
            [
                normed_ref[:, (g * columns + column) * LANES : (g * columns + column + 1) * LANES]
                for g in range(groups)
            ],
            axis=1,
        )
        term = jnp.dot(
            lhs,
            buffer[column * depth : (column + 1) * depth],
            preferred_element_type=jnp.float32,
        )
        sums = term if sums is None else sums + term
    for head in range(sums.shape[1] // HD):
        part = turn(sums[:, head * HD : (head + 1) * HD], cos_ref[...], sin_ref[...])
        out_ref[:, head * HD : (head + 1) * HD] = part.astype(jnp.bfloat16)


def project_queries(pieces, normed, cosine, sine, groups, columns):
    count, model_width = normed.shape
    width = pieces[0].shape[1]
    any_spec = pl.BlockSpec(memory_space=pl.ANY)
    vmem_spec = pl.BlockSpec(memory_space=pltpu.VMEM)
    return pl.pallas_call(
        lambda *refs: query_kernel(
            *refs, count=len(pieces), groups=groups, columns=columns
        ),
        in_specs=[any_spec] * (len(pieces) + 1) + [vmem_spec] * 2,
        out_specs=vmem_spec,
        out_shape=jax.ShapeDtypeStruct((count, width), jnp.bfloat16),
        scratch_shapes=[
            pltpu.VMEM((model_width, width), jnp.bfloat16),
            pltpu.VMEM((count, model_width), jnp.bfloat16),
            pltpu.SemaphoreType.DMA((len(pieces) + 1,)),
        ],
        name="project_queries",
    )(*pieces, normed, cosine, sine)


def attend_kernel(place_ref, *refs, half_rows, heads, ctx_count, which):
    query_ref, seg_ref, out_ref, key_buf, value_buf, sems = refs[2 * ctx_count :]
    ctx = place_ref[0]
    blocks = 2 * ctx_count
    copies = []
    for step in range(ctx_count):
        holder = lax.rem(ctx + step, ctx_count)
        for source, buffer in ((refs[step], key_buf), (refs[ctx_count + step], value_buf)):
            copies.append(
                pltpu.make_async_copy(source, buffer.at[holder], sems.at[len(copies)])
            )
    for copy in copies:
        copy.start()
    for copy in copies:
        copy.wait()

    seg_count = half_rows // LANES
    all_seg = key_buf[:, :, half_rows:, :].astype(jnp.float32)
    all_seg = all_seg[:, :, :seg_count, :].reshape(-1, LANES)
    own_seg = seg_ref[...]
    first = jnp.zeros(own_seg.shape, jnp.int32)
    for doc in range(1, 4):
        before = jnp.sum(
            (all_seg < doc).astype(jnp.float32), axis=(0, 1), keepdims=True
        ).astype(jnp.int32)
        first = jnp.where(own_seg == doc, before, first)
    own = ctx if which == 0 else blocks - 1 - ctx
    low = jnp.min(first) // half_rows
    inner = jnp.minimum((jnp.max(first) + half_rows - 1) // half_rows, own)

    queries = [query_ref[:, h * HD : (h + 1) * HD] for h in range(heads)]
    factor = math.log2(math.e) / HD**0.5
    key_iota = lax.broadcasted_iota(jnp.int32, (half_rows, half_rows), 0)
    query_pos = own * half_rows + lax.broadcasted_iota(jnp.int32, (1, half_rows), 1)

    def step(block, state, masked):
        second = block >= ctx_count
        holder = jnp.where(second, blocks - 1 - block, block)
        half = jnp.where(second, 1, 0)
        keys = key_buf[holder, half, :half_rows, :]
        values = value_buf[holder, half]
        if masked:
            key_pos = block * half_rows + key_iota
            allowed = (key_pos <= query_pos) & (key_pos >= first)
        result = []
        for h in range(heads):
            highest, totals, accum = state[h]
            scores = dot_dims(keys, queries[h], ((1,), (1,)))
            limited = jnp.where(allowed, scores, masked_score) if masked else scores
            new_high = jnp.maximum(highest, jnp.max(limited, axis=0, keepdims=True))
            shrink = jnp.exp2((highest - new_high) * factor)
            weights = jnp.exp2((scores - new_high) * factor)
            if masked:
                weights = jnp.where(allowed, weights, 0.0)
            new_totals = totals * shrink + jnp.sum(weights, axis=0, keepdims=True)
            added = dot_dims(values, weights.astype(jnp.bfloat16), ((0,), (0,)))
            result.append((new_high, new_totals, accum * shrink + added))
        return tuple(result)

    state = tuple(
        (
            jnp.full((1, half_rows), masked_score, jnp.float32),
            jnp.zeros((1, half_rows), jnp.float32),
            jnp.zeros((HD, half_rows), jnp.float32),
        )
        for _ in range(heads)
    )
    state = lax.fori_loop(low, inner, lambda b, s: step(b, s, True), state)
    state = lax.fori_loop(inner, own, lambda b, s: step(b, s, False), state)
    state = step(own, state, True)
    for h in range(heads):
        _, totals, accum = state[h]
        out_ref[:, h * HD : (h + 1) * HD] = (accum / totals).astype(jnp.bfloat16).T


def attend(place, keys, values, queries, seg, half_rows, heads, which):
    ctx_count = len(keys)
    any_spec = pl.BlockSpec(memory_space=pl.ANY)
    vmem_spec = pl.BlockSpec(memory_space=pltpu.VMEM)
    smem_spec = pl.BlockSpec(memory_space=pltpu.SMEM)
    rows = pl.BlockSpec((half_rows, heads * HD), lambda i: (which, 0))
    pieces = 2 * ctx_count
    return pl.pallas_call(
        lambda *refs: attend_kernel(
            *refs, half_rows=half_rows, heads=heads, ctx_count=ctx_count, which=which
        ),
        grid=(1,),
        in_specs=[smem_spec] + [any_spec] * pieces + [rows, vmem_spec],
        out_specs=pl.BlockSpec((half_rows, heads * HD), lambda i: (0, 0)),
        out_shape=jax.ShapeDtypeStruct((half_rows, heads * HD), jnp.bfloat16),
        scratch_shapes=[
            pltpu.VMEM((ctx_count,) + keys[0].shape, jnp.bfloat16),
            pltpu.VMEM((ctx_count,) + values[0].shape, jnp.bfloat16),
            pltpu.SemaphoreType.DMA((pieces,)),
        ],
        name="attend_second" if which else "attend_first",
    )(place, *keys, *values, queries, seg)


def blend_kernel(owner_ref, *refs):
    mixed = refs[:8]
    weight_any, out_ref, square_ref, buffer, sems = refs[8:]
    half_rows, width = mixed[0].shape
    copies = []
    for step in range(4):
        columns = pl.ds(pl.multiple_of(owner_ref[step] * width, LANES), width)
        copies.append(
            pltpu.make_async_copy(weight_any.at[:, columns], buffer.at[step], sems.at[step])
        )
    for copy in copies:
        copy.start()
    total = None
    for step in range(4):
        copies[step].wait()
        lhs = jnp.concatenate([mixed[2 * step][...], mixed[2 * step + 1][...]], axis=0)
        term = dot_dims(lhs, buffer[step], ((1,), (1,)))
        term = term.astype(jnp.bfloat16).astype(jnp.float32)
        total = term if total is None else total + term
    branch = total.astype(jnp.bfloat16)
    out_ref[...] = branch
    square = jnp.square(branch.astype(jnp.float32))
    square = jnp.sum(square.reshape(-1, 8, square.shape[1]), axis=0)
    part = square[:, :LANES]
    for block in range(1, square.shape[1] // LANES):
        part += square[:, block * LANES : (block + 1) * LANES]
    square_ref[...] = part


def blend(owners, mixed, weight):
    half_rows, width = mixed[0].shape
    features = weight.shape[0]
    vmem_spec = pl.BlockSpec(memory_space=pltpu.VMEM)
    return pl.pallas_call(
        blend_kernel,
        in_specs=[pl.BlockSpec(memory_space=pltpu.SMEM)]
        + [vmem_spec] * len(mixed)
        + [pl.BlockSpec(memory_space=pl.ANY)],
        out_specs=[vmem_spec, vmem_spec],
        out_shape=[
            jax.ShapeDtypeStruct((2 * half_rows, features), jnp.bfloat16),
            jax.ShapeDtypeStruct((8, LANES), jnp.float32),
        ],
        scratch_shapes=[
            pltpu.VMEM((4, features, width), jnp.bfloat16),
            pltpu.SemaphoreType.DMA((4,)),
        ],
        name="blend",
    )(owners, *mixed, weight)


def shards(
    tokens,
    norm_gain,
    query_weight,
    key_weight,
    value_weight,
    output_weight,
    query_noise,
    key_noise,
    value_noise,
    output_noise,
    sign,
    segment_ids,
    doc_weight,
):
    factor = sign[0].astype(jnp.float32) * perturb_step
    half_rows = tokens.shape[2]
    model_width = tokens.shape[3]
    local_rows = 2 * half_rows
    ctx = lax.axis_index("ctx")
    tp = lax.axis_index("tp")
    ctx_count = lax.axis_size("ctx")
    columns = lax.axis_size("dp") // 2
    x = lax.axis_index("dp") // 2
    seq_len = local_rows * ctx_count
    heads = query_weight.shape[1] // HD
    width = heads * HD

    own_qkv = perturbed(
        jnp.concatenate([query_weight, key_weight, value_weight], axis=1),
        jnp.concatenate([query_noise, key_noise, value_noise], axis=1),
        factor,
    )
    other = from_y(own_qkv)
    own_out = perturbed(after(output_weight, own_qkv), output_noise, factor).T
    out_weight = lax.all_gather(own_out, ("ctx", "dp"), axis=0, tiled=True)

    place = jnp.stack([ctx, x]).astype(jnp.int32)
    normed = norm(place, tokens[0].reshape(local_rows, model_width), norm_gain, ctx_count, columns)
    offsets = jnp.arange(half_rows, dtype=jnp.int32)
    local_pos = jnp.concatenate(
        [ctx * half_rows + offsets, seq_len - (ctx + 1) * half_rows + offsets]
    )
    cosine, sine = rope_tables(local_pos)
    seg_rows = segment_ids[0].astype(jnp.bfloat16).reshape(2, half_rows // LANES, LANES)
    seg_rows = jnp.pad(seg_rows, ((0, 0), (0, 16 - seg_rows.shape[1]), (0, 0)))
    other, normed, cosine, sine, seg_rows = lax.optimization_barrier(
        (other, normed, cosine, sine, seg_rows)
    )
    first = lax.axis_index("dp") % 2 == 0
    pair = jnp.where(
        first,
        jnp.concatenate([own_qkv, other], axis=0),
        jnp.concatenate([other, own_qkv], axis=0),
    )

    left = pair[:, width:]
    right = pair[:, :width]
    line = jnp.concatenate(
        [left, from_x(left, 1), from_x(left, 2), from_x(left, -1)], axis=0
    )
    up, down = [line], [line]
    right_up, right_down = [right, from_z(right, 1)], [right, from_z(right, -1)]
    for step in range(1, 4):
        ends = (up[-1], down[-1], right_up[-1], right_down[-1])
        ends = lax.optimization_barrier(ends)
        up.append(from_z(ends[0], 1))
        down.append(from_z(ends[1], -1))
        right_up.append(from_z(ends[2], 1))
        if step < 3:
            right_down.append(from_z(ends[3], -1))
    middle = line.shape[0] // 2
    last_up, last_down, last_right = lax.optimization_barrier(
        (up[3][:middle], down[3][middle:], right_up[4])
    )
    pieces = up + [from_z(last_up, 1), from_z(last_down, -1)] + down[:0:-1]
    column = jnp.concatenate(right_up[:4] + [last_right] + right_down[:0:-1], axis=0)
    next_x = from_x(column, 1)
    last_x = from_x(column, -1)
    own_keys, own_values = project_pair(
        pieces, after(normed, column), cosine, sine, seg_rows
    )

    key_up, key_down = [own_keys], [own_keys]
    value_up, value_down = [own_values], [own_values]
    for step in range(3):
        ends = (key_up[-1], key_down[-1], value_up[-1], value_down[-1])
        if step == 2:
            ends = lax.optimization_barrier(ends + (next_x, last_x))[:4]
        key_up.append(from_z(ends[0], 1))
        value_down.append(from_z(ends[3], -1))
        value_up.append(from_z(ends[2], 1))
        key_down.append(from_z(ends[1], -1))
    keys = key_up + [from_z(key_up[3], 1)] + key_down[:0:-1]
    values = value_up + [from_z(value_down[3], -1)] + value_down[:0:-1]
    middle = column.shape[0] // 2
    next_half, last_half = lax.optimization_barrier(
        (next_x[:middle], last_x[middle:], key_up[1], key_down[1], value_up[1], value_down[1])
    )[:2]
    columns_in = [column, next_x, from_x(next_half, 1), from_x(last_half, -1), last_x]
    queries = project_queries(columns_in, normed, cosine, sine, ctx_count, columns)
    parts = []
    for which in (1, 0):
        mixed = attend(
            place,
            keys,
            values,
            queries,
            segment_ids[0, which].reshape(1, half_rows),
            half_rows,
            heads,
            which,
        )
        far = from_tp(mixed, 2)
        parts.append([mixed, from_tp(mixed, 1), far, from_tp(far, 1)])
    owners = jnp.stack([tp, tp ^ 1, tp ^ 2, tp ^ 3]).astype(jnp.int32)
    pairs = [part for step in range(4) for part in (parts[1][step], parts[0][step])]
    branch, squares = blend(owners, pairs, out_weight)
    local_total = jnp.sum(squares) * doc_weight[0]
    everyone = ctx_count * lax.axis_size("tp") * lax.axis_size("dp")
    shares = lax.all_to_all(
        jnp.broadcast_to(local_total, (everyone, LANES)), mesh_axes, 0, 0, tiled=True
    )
    loss = jnp.sum(shares[:, 0]) / (seq_len * model_width)
    return (branch.reshape(1, 2, half_rows, branch.shape[1]), loss.reshape(1))


def solution(mesh):
    return jax.shard_map(
        shards,
        mesh=mesh,
        in_specs=(
            P("dp", None, "ctx", None),
            P(),
            P(("ctx", "dp"), "tp"),
            P(("ctx", "dp"), "tp"),
            P(("ctx", "dp"), "tp"),
            P(None, ("tp", "ctx", "dp")),
            P(("ctx", "dp"), "tp"),
            P(("ctx", "dp"), "tp"),
            P(("ctx", "dp"), "tp"),
            P(None, ("tp", "ctx", "dp")),
            P(),
            P("dp", None, "ctx"),
            P("dp"),
        ),
        out_specs=(P("dp", None, "ctx", "tp"), P()),
        check_vma=False,
    )
```

```python
import math

import jax
import jax.numpy as jnp
from jax import lax
from jax.experimental import pallas as pl
from jax.experimental.pallas import tpu as pltpu
from jax.sharding import PartitionSpec as P

HD = 128
LANES = 128

perturb_step = 0.004
rope_base = 500000.0
norm_epsilon = 1e-05
masked_score = -1e30
mesh_axes = ("ctx", "tp", "dp")


def perturbed(weight, noise, factor):
    return (weight.astype(jnp.float32) + factor * noise.astype(jnp.float32)).astype(jnp.bfloat16)


def dot_dims(lhs, rhs, dims):
    return lax.dot_general(lhs, rhs, (dims, ((), ())), preferred_element_type=jnp.float32)


def rope_tables(positions):
    half = HD // 2
    inverse = rope_base ** (-jnp.arange(half, dtype=jnp.float32) * 2.0 / HD)
    angles = positions.astype(jnp.float32)[:, None] * inverse[None, :]
    cosine = jnp.cos(angles)
    sine = jnp.sin(angles)
    return (
        jnp.concatenate([cosine, cosine], axis=1),
        jnp.concatenate([-sine, sine], axis=1),
    )


def fetch(values, source):
    sizes = [lax.axis_size(axis) for axis in mesh_axes]
    pairs = []
    for c in range(sizes[0]):
        for t in range(sizes[1]):
            for d in range(sizes[2]):
                fc, ft, fd = source(c, t, d)
                pairs.append(((fc * sizes[1] + ft) * sizes[2] + fd, (c * sizes[1] + t) * sizes[2] + d))
    return lax.ppermute(values, mesh_axes, pairs)


def from_z(values, step):
    count = lax.axis_size("ctx")
    return fetch(values, lambda c, t, d: ((c + step) % count, t, d))


def from_x(values, step):
    count = lax.axis_size("dp") // 2
    return fetch(values, lambda c, t, d: (c, t, ((d // 2 + step) % count) * 2 + d % 2))


def from_y(values):
    return fetch(values, lambda c, t, d: (c, t, d ^ 1))


def from_tp(values, flip):
    return fetch(values, lambda c, t, d: (c, t ^ flip, d))


def after(value, *others):
    return lax.optimization_barrier((value,) + others)[0]


def norm_kernel(place_ref, tokens_ref, gain_ref, out_ref, *, groups):
    width = tokens_ref.shape[1]
    depth = width // groups
    values = tokens_ref[...].astype(jnp.float32)
    mean = jnp.sum(values * values, axis=1, keepdims=True) / width
    rate = lax.rsqrt(mean + norm_epsilon)
    for group in range(groups):
        columns = slice(group * depth, (group + 1) * depth)
        part = tokens_ref[:, columns].astype(jnp.float32) * rate * gain_ref[:, columns]
        target = lax.rem(group + groups - place_ref[0], groups)
        target = pl.multiple_of(target * depth, depth)
        out_ref[:, pl.ds(target, depth)] = part.astype(jnp.bfloat16)


def norm(place, tokens, gain, groups, start, count, rows=64):
    width = tokens.shape[1]
    return pl.pallas_call(
        lambda *refs: norm_kernel(*refs, groups=groups),
        grid_spec=pltpu.PrefetchScalarGridSpec(
            num_scalar_prefetch=1,
            grid=(count // rows,),
            in_specs=[
                pl.BlockSpec((rows, width), lambda i, _: (i + start // rows, 0)),
                pl.BlockSpec((1, width), lambda i, _: (0, 0)),
            ],
            out_specs=pl.BlockSpec((rows, width), lambda i, _: (i, 0)),
        ),
        out_shape=jax.ShapeDtypeStruct((count, width), jnp.bfloat16),
        name="norm",
    )(place, tokens, gain.reshape(1, width))


def turn(part, cosine, sine):
    return part * cosine + pltpu.roll(part, HD // 2, 1) * sine


def run_copies(pairs, sems):
    copies = [
        pltpu.make_async_copy(source, target, sems.at[at])
        for at, (source, target) in enumerate(pairs)
    ]
    for copy in copies:
        copy.start()
    for copy in copies:
        copy.wait()


def halves_of(normed_any, normed_ref):
    rows = normed_any[0].shape[0]
    return [
        (piece, normed_ref.at[pl.ds(at * rows, rows)]) for at, piece in enumerate(normed_any)
    ]


def pair_kernel(*refs, count):
    first_any, second_any, cos_ref, sin_ref, seg_ref, parcel_ref = refs[count : count + 6]
    buffer, normed_ref, sems = refs[count + 6 :]
    pairs = halves_of((first_any, second_any), normed_ref)
    start = 0
    for piece in refs[:count]:
        size = piece.shape[0]
        pairs.append((piece, buffer.at[pl.ds(start, size)]))
        start += size
    run_copies(pairs, sems)
    half_rows = first_any.shape[0]
    sums = jnp.dot(normed_ref[...], buffer[...], preferred_element_type=jnp.float32)
    keys = turn(sums[:, :HD], cos_ref[...], sin_ref[...]).astype(jnp.bfloat16)
    values = sums[:, HD:].astype(jnp.bfloat16)
    for half in range(2):
        rows_of = slice(half * half_rows, (half + 1) * half_rows)
        parcel_ref[half, :half_rows] = keys[rows_of]
        parcel_ref[half, half_rows : 2 * half_rows] = values[rows_of]
        parcel_ref[half, 2 * half_rows :] = seg_ref[half]


def project_pair(pieces, normed, cosine, sine, seg_rows):
    half_rows, model_width = normed[0].shape
    any_spec = pl.BlockSpec(memory_space=pl.ANY)
    vmem_spec = pl.BlockSpec(memory_space=pltpu.VMEM)
    return pl.pallas_call(
        lambda *refs: pair_kernel(*refs, count=len(pieces)),
        in_specs=[any_spec] * (len(pieces) + 2) + [vmem_spec] * 3,
        out_specs=vmem_spec,
        out_shape=jax.ShapeDtypeStruct(
            (2, 2 * half_rows + seg_rows.shape[1], HD), jnp.bfloat16
        ),
        scratch_shapes=[
            pltpu.VMEM((model_width, 2 * HD), jnp.bfloat16),
            pltpu.VMEM((2 * half_rows, model_width), jnp.bfloat16),
            pltpu.SemaphoreType.DMA((len(pieces) + 2,)),
        ],
        name="project_pair",
    )(*pieces, *normed, cosine, sine, seg_rows)


def query_kernel(place_ref, *refs, groups, columns):
    own_any, next_any, top_any, low_any, last_any, first_any, second_any = refs[:7]
    cos_ref, sin_ref, out_ref, buffer, normed_ref, sums_ref, sems = refs[7:]
    depth = groups * LANES
    half = depth // 2
    pairs = halves_of((first_any, second_any), normed_ref)
    for piece, step, offset in (
        (own_any, 0, 0),
        (next_any, 1, 0),
        (top_any, 2, 0),
        (low_any, 2, half),
        (last_any, columns - 1, 0),
    ):
        column = lax.rem(place_ref[1] + step, columns)
        target = pl.multiple_of(column * depth + offset, half)
        pairs.append((piece, buffer.at[pl.ds(target, piece.shape[0])]))
    run_copies(pairs, sems)
    sums_ref[...] = jnp.zeros_like(sums_ref)

    def step(column, _):
        parts = []
        for group in range(groups):
            start = pl.multiple_of((group * columns + column) * LANES, LANES)
            parts.append(normed_ref[:, pl.ds(start, LANES)])
        start = pl.multiple_of(column * depth, depth)
        sums_ref[...] += jnp.dot(
            jnp.concatenate(parts, axis=1),
            buffer[pl.ds(start, depth)],
            preferred_element_type=jnp.float32,
        )
        return 0

    lax.fori_loop(0, columns, step, 0)
    for head in range(sums_ref.shape[1] // HD):
        lanes = slice(head * HD, (head + 1) * HD)
        part = turn(sums_ref[:, lanes], cos_ref[...], sin_ref[...])
        out_ref[:, lanes] = part.astype(jnp.bfloat16)


def project_queries(place, pieces, normed, cosine, sine, groups, columns):
    half_rows, model_width = normed[0].shape
    width = pieces[0].shape[1]
    any_spec = pl.BlockSpec(memory_space=pl.ANY)
    vmem_spec = pl.BlockSpec(memory_space=pltpu.VMEM)
    return pl.pallas_call(
        lambda *refs: query_kernel(*refs, groups=groups, columns=columns),
        in_specs=[pl.BlockSpec(memory_space=pltpu.SMEM)] + [any_spec] * 7 + [vmem_spec] * 2,
        out_specs=vmem_spec,
        out_shape=jax.ShapeDtypeStruct((2 * half_rows, width), jnp.bfloat16),
        scratch_shapes=[
            pltpu.VMEM((model_width, width), jnp.bfloat16),
            pltpu.VMEM((2 * half_rows, model_width), jnp.bfloat16),
            pltpu.VMEM((2 * half_rows, width), jnp.float32),
            pltpu.SemaphoreType.DMA((7,)),
        ],
        name="project_queries",
    )(place, *pieces, *normed, cosine, sine)


def attend_kernel(place_ref, *refs, half_rows, heads, ctx_count):
    query_ref, seg_ref, out_ref, key_buf, value_buf, seg_buf, sems = refs[ctx_count + 1 :]
    which = pl.program_id(0)
    ctx = place_ref[0]
    blocks = 2 * ctx_count
    span = 2 * half_rows
    seg_count = half_rows // LANES

    @pl.when(which == 0)
    def _():
        pairs = []
        sources = []
        for step in range(ctx_count + 1):
            parcel = refs[step]
            distance = step if step <= ctx_count // 2 else step - 1
            if parcel.shape[0] == 1:
                sources.append((parcel.at[0], distance, step - ctx_count // 2))
            else:
                sources.append((parcel.at[0], distance, 0))
                sources.append((parcel.at[1], distance, 1))
        for source, distance, half in sources:
            holder = lax.rem(ctx + distance, ctx_count)
            block = blocks - 1 - holder if half else holder
            rows = pl.ds(pl.multiple_of(block * half_rows, half_rows), half_rows)
            pairs.append((source.at[pl.ds(0, half_rows)], key_buf.at[rows]))
            pairs.append((source.at[pl.ds(half_rows, half_rows)], value_buf.at[rows]))
            pairs.append(
                (source.at[pl.ds(2 * half_rows, 16)], seg_buf.at[block])
            )
        run_copies(pairs, sems)

    all_seg = seg_buf[...].astype(jnp.float32)
    real = lax.broadcasted_iota(jnp.int32, all_seg.shape, 1) < seg_count
    own_seg = seg_ref[0]
    first = jnp.zeros(own_seg.shape, jnp.int32)
    for doc in range(1, 4):
        smaller = jnp.where(real & (all_seg < doc), 1.0, 0.0)
        before = jnp.sum(jnp.sum(smaller, axis=0), axis=(0, 1), keepdims=True)
        first = jnp.where(own_seg == doc, before.astype(jnp.int32), first)
    own = jnp.where(which == 0, ctx, blocks - 1 - ctx)
    low = jnp.min(first) // span
    last = own * half_rows // span
    inner = jnp.minimum((jnp.max(first) + span - 1) // span, last)

    queries = jnp.concatenate(
        [query_ref[:, h * HD : (h + 1) * HD] for h in range(heads)], axis=0
    )
    rows = heads * half_rows
    factor = math.log2(math.e) / HD**0.5
    first = jnp.concatenate([first] * heads, axis=1)
    query_pos = own * half_rows + lax.rem(
        lax.broadcasted_iota(jnp.int32, (1, rows), 1), half_rows
    )

    def step(block, state, masked):
        highest, totals, accum = state
        start = pl.multiple_of(block * span, span)
        scores = dot_dims(key_buf[pl.ds(start, span)], queries, ((1,), (1,)))
        if masked:
            key_pos = start + lax.broadcasted_iota(jnp.int32, (span, rows), 0)
            allowed = (key_pos <= query_pos) & (key_pos >= first)
            limited = jnp.where(allowed, scores, masked_score)
        else:
            limited = scores
        new_high = jnp.maximum(highest, jnp.max(limited, axis=0, keepdims=True))
        shrink = jnp.exp2((highest - new_high) * factor)
        weights = jnp.exp2((scores - new_high) * factor)
        if masked:
            weights = jnp.where(allowed, weights, 0.0)
        new_totals = totals * shrink + jnp.sum(weights, axis=0, keepdims=True)
        added = dot_dims(
            value_buf[pl.ds(start, span)], weights.astype(jnp.bfloat16), ((0,), (0,))
        )
        return (new_high, new_totals, accum * shrink + added)

    state = (
        jnp.full((1, rows), masked_score, jnp.float32),
        jnp.zeros((1, rows), jnp.float32),
        jnp.zeros((HD, rows), jnp.float32),
    )
    state = lax.fori_loop(inner, last, lambda b, s: step(b, s, False), state)
    edges = jnp.minimum(inner, last) - low
    state = lax.fori_loop(
        0,
        edges + 1,
        lambda b, s: step(jnp.where(b < edges, low + b, last), s, True),
        state,
    )
    _, totals, accum = state
    mixed = (accum / totals).astype(jnp.bfloat16)
    for h in range(heads):
        out_ref[:, h * HD : (h + 1) * HD] = mixed[:, h * half_rows : (h + 1) * half_rows].T


def attend(place, parcels, queries, seg, half_rows, heads):
    ctx_count = len(parcels) - 1
    width = heads * HD
    keys = 2 * ctx_count * half_rows
    return pl.pallas_call(
        lambda *refs: attend_kernel(
            *refs, half_rows=half_rows, heads=heads, ctx_count=ctx_count
        ),
        grid=(2,),
        in_specs=[pl.BlockSpec(memory_space=pltpu.SMEM)]
        + [pl.BlockSpec(memory_space=pl.ANY)] * len(parcels)
        + [
            pl.BlockSpec((half_rows, width), lambda i: (i, 0)),
            pl.BlockSpec((1, 1, half_rows), lambda i: (i, 0, 0)),
        ],
        out_specs=pl.BlockSpec((half_rows, width), lambda i: (i, 0)),
        out_shape=jax.ShapeDtypeStruct((2 * half_rows, width), jnp.bfloat16),
        scratch_shapes=[
            pltpu.VMEM((keys, HD), jnp.bfloat16),
            pltpu.VMEM((keys, HD), jnp.bfloat16),
            pltpu.VMEM((2 * ctx_count, 16, HD), jnp.bfloat16),
            pltpu.SemaphoreType.DMA((6 * ctx_count,)),
        ],
        name="attend",
    )(place, *parcels, queries, seg)


def blend_kernel(owner_ref, *refs):
    weight_any, out_ref, square_ref, mixed_buf, buffer, total_ref, sems = refs[4:]
    width = mixed_buf.shape[2]

    def weight_copy(step):
        columns = pl.ds(pl.multiple_of(owner_ref[step] * width, LANES), width)
        return pltpu.make_async_copy(
            weight_any.at[:, columns], buffer.at[step], sems.at[4 + step]
        )

    for step in range(4):
        weight_copy(step).start()
    run_copies([(refs[step], mixed_buf.at[step]) for step in range(4)], sems)
    total_ref[...] = jnp.zeros_like(total_ref)

    def add(step, _):
        weight_copy(step).wait()
        term = dot_dims(mixed_buf[step], buffer[step], ((1,), (1,)))
        total_ref[...] += term.astype(jnp.bfloat16).astype(jnp.float32)
        return 0

    lax.fori_loop(0, 4, add, 0)
    branch = total_ref[...].astype(jnp.bfloat16)
    out_ref[...] = branch
    square = jnp.square(branch.astype(jnp.float32))
    square = jnp.sum(square.reshape(-1, 8, square.shape[1]), axis=0)
    part = square[:, :LANES]
    for block in range(1, square.shape[1] // LANES):
        part += square[:, block * LANES : (block + 1) * LANES]
    square_ref[...] = part


def blend(owners, mixed, weight):
    count, width = mixed[0].shape
    features = weight.shape[0]
    any_spec = pl.BlockSpec(memory_space=pl.ANY)
    vmem_spec = pl.BlockSpec(memory_space=pltpu.VMEM)
    return pl.pallas_call(
        blend_kernel,
        in_specs=[pl.BlockSpec(memory_space=pltpu.SMEM)] + [any_spec] * 5,
        out_specs=[vmem_spec, vmem_spec],
        out_shape=[
            jax.ShapeDtypeStruct((count, features), jnp.bfloat16),
            jax.ShapeDtypeStruct((8, LANES), jnp.float32),
        ],
        scratch_shapes=[
            pltpu.VMEM((4, count, width), jnp.bfloat16),
            pltpu.VMEM((4, features, width), jnp.bfloat16),
            pltpu.VMEM((count, features), jnp.float32),
            pltpu.SemaphoreType.DMA((8,)),
        ],
        name="blend",
    )(owners, *mixed, weight)


def shards(
    tokens,
    norm_gain,
    query_weight,
    key_weight,
    value_weight,
    output_weight,
    query_noise,
    key_noise,
    value_noise,
    output_noise,
    sign,
    segment_ids,
    doc_weight,
):
    factor = sign[0].astype(jnp.float32) * perturb_step
    half_rows = tokens.shape[2]
    model_width = tokens.shape[3]
    local_rows = 2 * half_rows
    ctx = lax.axis_index("ctx")
    tp = lax.axis_index("tp")
    ctx_count = lax.axis_size("ctx")
    columns = lax.axis_size("dp") // 2
    x = lax.axis_index("dp") // 2
    seq_len = local_rows * ctx_count
    heads = query_weight.shape[1] // HD
    width = heads * HD

    own_pair = perturbed(
        jnp.concatenate([key_weight, value_weight], axis=1),
        jnp.concatenate([key_noise, value_noise], axis=1),
        factor,
    )
    own_query = perturbed(query_weight, query_noise, factor)
    dp_count = lax.axis_size("dp")
    spread = jnp.broadcast_to(own_pair[None], (dp_count,) + own_pair.shape)
    spread, own_query = lax.optimization_barrier((spread, own_query))
    other = from_y(own_query)
    line = lax.all_to_all(spread, "dp", 0, 0).reshape(-1, 2 * HD)
    own_out = perturbed(after(output_weight, own_query), output_noise, factor).T
    out_weight = lax.all_gather(own_out, ("ctx", "dp"), axis=0, tiled=True)
    even = lax.axis_index("dp") % 2 == 0
    right = jnp.where(
        even,
        jnp.concatenate([own_query, other], axis=0),
        jnp.concatenate([other, own_query], axis=0),
    )

    place = jnp.stack([ctx, x]).astype(jnp.int32)
    rows_in = tokens[0].reshape(local_rows, model_width)
    normed = [
        norm(place, rows_in, norm_gain, ctx_count, half * half_rows, half_rows)
        for half in range(2)
    ]
    offsets = jnp.arange(half_rows, dtype=jnp.int32)
    local_pos = jnp.concatenate(
        [ctx * half_rows + offsets, seq_len - (ctx + 1) * half_rows + offsets]
    )
    cosine, sine = rope_tables(local_pos)
    seg_rows = segment_ids[0].astype(jnp.bfloat16).reshape(2, half_rows // LANES, LANES)
    seg_rows = jnp.pad(seg_rows, ((0, 0), (0, 16 - seg_rows.shape[1]), (0, 0)))

    up, down = [line], [line]
    right_up, right_down = [right], [right]
    for step in range(3):
        ends = (up[-1], down[-1], right_up[-1], right_down[-1])
        if step:
            ends = lax.optimization_barrier(ends + (normed[step - 1],))
            normed[step - 1] = ends[4]
        else:
            ends = lax.optimization_barrier(ends)
        up.append(from_z(ends[0], 1))
        down.append(from_z(ends[1], -1))
        right_up.append(from_z(ends[2], 1))
        right_down.append(from_z(ends[3], -1))
    middle = line.shape[0] // 2
    last_up, last_down, last_right, cosine, sine, seg_rows = lax.optimization_barrier(
        (up[3][:middle], down[3][middle:], right_up[3], cosine, sine, seg_rows)
    )
    far_right = from_z(last_right, 1)
    pieces = up + [from_z(last_up, 1), from_z(last_down, -1)] + down[:0:-1]
    column = jnp.concatenate(right_up + [far_right] + right_down[:0:-1], axis=0)
    next_x = from_x(column, 1)
    last_x = from_x(column, -1)
    parcel = project_pair(pieces, (after(normed[0], column), normed[1]), cosine, sine, seg_rows)

    parcel_up, parcel_down = [parcel], [parcel]
    for step in range(3):
        ends = (parcel_up[-1], parcel_down[-1])
        if step == 2:
            ends = lax.optimization_barrier(ends + (next_x, last_x))[:2]
        parcel_up.append(from_z(ends[0], 1))
        parcel_down.append(from_z(ends[1], -1))
    parcels = (
        parcel_up
        + [from_z(parcel_up[3][:1], 1), from_z(parcel_down[3][1:], -1)]
        + parcel_down[:0:-1]
    )
    middle = column.shape[0] // 2
    next_half, last_half = lax.optimization_barrier(
        (next_x[:middle], last_x[middle:], parcel_up[1], parcel_down[1])
    )[:2]
    columns_in = [column, next_x, from_x(next_half, 1), from_x(last_half, -1), last_x]
    queries = project_queries(place, columns_in, normed, cosine, sine, ctx_count, columns)

    own_seg = segment_ids[0].reshape(2, 1, half_rows)
    mixed = attend(place, parcels, queries, own_seg, half_rows, heads)
    near = from_tp(mixed, 1)
    far = from_tp(mixed, 2)
    owners = jnp.stack([tp, tp ^ 1, tp ^ 2, tp ^ 3]).astype(jnp.int32)
    branch, squares = blend(owners, [mixed, near, far, from_tp(far, 1)], out_weight)
    local_total = jnp.sum(squares) * doc_weight[0]
    everyone = ctx_count * lax.axis_size("tp") * lax.axis_size("dp")
    shares = lax.all_to_all(
        jnp.broadcast_to(local_total, (everyone, LANES)), mesh_axes, 0, 0, tiled=True
    )
    loss = jnp.sum(shares[:, 0]) / (seq_len * model_width)
    return (branch.reshape(1, 2, half_rows, branch.shape[1]), loss.reshape(1))


def solution(mesh):
    return jax.shard_map(
        shards,
        mesh=mesh,
        in_specs=(
            P("dp", None, "ctx", None),
            P(),
            P(("ctx", "dp"), "tp"),
            P(("ctx", "dp"), "tp"),
            P(("ctx", "dp"), "tp"),
            P(None, ("tp", "ctx", "dp")),
            P(("ctx", "dp"), "tp"),
            P(("ctx", "dp"), "tp"),
            P(("ctx", "dp"), "tp"),
            P(None, ("tp", "ctx", "dp")),
            P(),
            P("dp", None, "ctx"),
            P("dp"),
        ),
        out_specs=(P("dp", None, "ctx", "tp"), P()),
        check_vma=False,
    )
```

```python
import math

import jax
import jax.numpy as jnp
from jax import lax
from jax.experimental import pallas as pl
from jax.experimental.pallas import tpu as pltpu
from jax.sharding import PartitionSpec as P

HD = 128
LANES = 128

perturb_step = 0.004
rope_base = 500000.0
norm_epsilon = 1e-05
masked_score = -1e30
mesh_axes = ("ctx", "tp", "dp")


def perturbed(weight, noise, factor):
    return (weight.astype(jnp.float32) + factor * noise.astype(jnp.float32)).astype(jnp.bfloat16)


def dot_dims(lhs, rhs, dims):
    return lax.dot_general(lhs, rhs, (dims, ((), ())), preferred_element_type=jnp.float32)


def rope_tables(positions):
    half = HD // 2
    inverse = rope_base ** (-jnp.arange(half, dtype=jnp.float32) * 2.0 / HD)
    angles = positions.astype(jnp.float32)[:, None] * inverse[None, :]
    cosine = jnp.cos(angles)
    sine = jnp.sin(angles)
    return (
        jnp.concatenate([cosine, cosine], axis=1),
        jnp.concatenate([-sine, sine], axis=1),
    )


def fetch(values, source):
    sizes = [lax.axis_size(axis) for axis in mesh_axes]
    pairs = []
    for c in range(sizes[0]):
        for t in range(sizes[1]):
            for d in range(sizes[2]):
                fc, ft, fd = source(c, t, d)
                pairs.append(((fc * sizes[1] + ft) * sizes[2] + fd, (c * sizes[1] + t) * sizes[2] + d))
    return lax.ppermute(values, mesh_axes, pairs)


def from_z(values, step):
    count = lax.axis_size("ctx")
    return fetch(values, lambda c, t, d: ((c + step) % count, t, d))


def from_x(values, step):
    count = lax.axis_size("dp") // 2
    return fetch(values, lambda c, t, d: (c, t, ((d // 2 + step) % count) * 2 + d % 2))


def from_y(values):
    return fetch(values, lambda c, t, d: (c, t, d ^ 1))


def from_tp(values, flip):
    return fetch(values, lambda c, t, d: (c, t ^ flip, d))


def after(value, *others):
    return lax.optimization_barrier((value,) + others)[0]


def norm_kernel(place_ref, tokens_ref, gain_ref, out_ref, *, groups):
    width = tokens_ref.shape[1]
    depth = width // groups
    values = tokens_ref[...].astype(jnp.float32)
    mean = jnp.sum(values * values, axis=1, keepdims=True) / width
    rate = lax.rsqrt(mean + norm_epsilon)
    for group in range(groups):
        columns = slice(group * depth, (group + 1) * depth)
        part = tokens_ref[:, columns].astype(jnp.float32) * rate * gain_ref[:, columns]
        target = lax.rem(group + groups - place_ref[0], groups)
        target = pl.multiple_of(target * depth, depth)
        out_ref[:, pl.ds(target, depth)] = part.astype(jnp.bfloat16)


def norm(place, tokens, gain, groups, start, count, rows=64):
    width = tokens.shape[1]
    return pl.pallas_call(
        lambda *refs: norm_kernel(*refs, groups=groups),
        grid_spec=pltpu.PrefetchScalarGridSpec(
            num_scalar_prefetch=1,
            grid=(count // rows,),
            in_specs=[
                pl.BlockSpec((rows, width), lambda i, _: (i + start // rows, 0)),
                pl.BlockSpec((1, width), lambda i, _: (0, 0)),
            ],
            out_specs=pl.BlockSpec((rows, width), lambda i, _: (i, 0)),
        ),
        out_shape=jax.ShapeDtypeStruct((count, width), jnp.bfloat16),
        name="norm",
    )(place, tokens, gain.reshape(1, width))


def turn(part, cosine, sine):
    return part * cosine + pltpu.roll(part, HD // 2, 1) * sine


def run_copies(pairs, sems):
    copies = [
        pltpu.make_async_copy(source, target, sems.at[at])
        for at, (source, target) in enumerate(pairs)
    ]
    for copy in copies:
        copy.start()
    for copy in copies:
        copy.wait()


def halves_of(normed_any, normed_ref):
    rows = normed_any[0].shape[0]
    return [
        (piece, normed_ref.at[pl.ds(at * rows, rows)]) for at, piece in enumerate(normed_any)
    ]


def pair_kernel(*refs, count):
    first_any, second_any, cos_ref, sin_ref, seg_ref, parcel_ref = refs[count : count + 6]
    buffer, normed_ref, sems = refs[count + 6 :]
    pairs = halves_of((first_any, second_any), normed_ref)
    start = 0
    for piece in refs[:count]:
        size = piece.shape[0] * 2 // 3
        pairs.append((piece.at[pl.ds(0, size)], buffer.at[pl.ds(start, size)]))
        start += size
    run_copies(pairs, sems)
    half_rows = first_any.shape[0]
    sums = jnp.dot(normed_ref[...], buffer[...], preferred_element_type=jnp.float32)
    keys = turn(sums[:, :HD], cos_ref[...], sin_ref[...]).astype(jnp.bfloat16)
    values = sums[:, HD:].astype(jnp.bfloat16)
    for half in range(2):
        rows_of = slice(half * half_rows, (half + 1) * half_rows)
        parcel_ref[half, :half_rows] = keys[rows_of]
        parcel_ref[half, half_rows : 2 * half_rows] = values[rows_of]
        parcel_ref[half, 2 * half_rows :] = seg_ref[half]


def project_pair(pieces, normed, cosine, sine, seg_rows):
    half_rows, model_width = normed[0].shape
    any_spec = pl.BlockSpec(memory_space=pl.ANY)
    vmem_spec = pl.BlockSpec(memory_space=pltpu.VMEM)
    return pl.pallas_call(
        lambda *refs: pair_kernel(*refs, count=len(pieces)),
        in_specs=[any_spec] * (len(pieces) + 2) + [vmem_spec] * 3,
        out_specs=vmem_spec,
        out_shape=jax.ShapeDtypeStruct(
            (2, 2 * half_rows + seg_rows.shape[1], HD), jnp.bfloat16
        ),
        scratch_shapes=[
            pltpu.VMEM((model_width, 2 * HD), jnp.bfloat16),
            pltpu.VMEM((2 * half_rows, model_width), jnp.bfloat16),
            pltpu.SemaphoreType.DMA((len(pieces) + 2,)),
        ],
        name="project_pair",
    )(*pieces, *normed, cosine, sine, seg_rows)


def query_kernel(place_ref, *refs, groups, columns):
    own_any, next_any, first_half, second_half, last_any, first_any, second_any = refs[:7]
    cos_ref, sin_ref, out_ref, buffer, normed_ref, sems = refs[7:]
    depth = groups * LANES
    width = own_any.shape[1]
    copies = []

    def load(source, target):
        copy = pltpu.make_async_copy(source, target, sems.at[len(copies)])
        copy.start()
        copies.append(copy)

    for source, target in halves_of((first_any, second_any), normed_ref):
        load(source, target)
    for step, sources in (
        (0, (own_any.at[pl.ds(0, depth)], own_any.at[pl.ds(depth, depth)])),
        (1, (next_any.at[pl.ds(0, depth)], next_any.at[pl.ds(depth, depth)])),
        (2, (first_half, second_half)),
        (3, (last_any.at[pl.ds(0, depth)], last_any.at[pl.ds(depth, depth)])),
    ):
        for half in range(2):
            load(
                sources[half],
                buffer.at[pl.ds(step * depth, depth), pl.ds(half * width, width)],
            )
    copies[0].wait()
    copies[1].wait()
    sums = None
    for step in range(columns):
        copies[2 + 2 * step].wait()
        copies[3 + 2 * step].wait()
        column = lax.rem(place_ref[1] + step, columns)
        parts = []
        for group in range(groups):
            start = pl.multiple_of((group * columns + column) * LANES, LANES)
            parts.append(normed_ref[:, pl.ds(start, LANES)])
        term = jnp.dot(
            jnp.concatenate(parts, axis=1),
            buffer[step * depth : (step + 1) * depth],
            preferred_element_type=jnp.float32,
        )
        sums = term if sums is None else sums + term
    for head in range(sums.shape[1] // HD):
        lanes = slice(head * HD, (head + 1) * HD)
        part = turn(sums[:, lanes], cos_ref[...], sin_ref[...])
        out_ref[:, lanes] = part.astype(jnp.bfloat16)


def project_queries(place, pieces, normed, cosine, sine, groups, columns):
    half_rows, model_width = normed[0].shape
    width = 2 * pieces[0].shape[1]
    any_spec = pl.BlockSpec(memory_space=pl.ANY)
    vmem_spec = pl.BlockSpec(memory_space=pltpu.VMEM)
    return pl.pallas_call(
        lambda *refs: query_kernel(*refs, groups=groups, columns=columns),
        in_specs=[pl.BlockSpec(memory_space=pltpu.SMEM)] + [any_spec] * 7 + [vmem_spec] * 2,
        out_specs=vmem_spec,
        out_shape=jax.ShapeDtypeStruct((2 * half_rows, width), jnp.bfloat16),
        scratch_shapes=[
            pltpu.VMEM((model_width, width), jnp.bfloat16),
            pltpu.VMEM((2 * half_rows, model_width), jnp.bfloat16),
            pltpu.SemaphoreType.DMA((2 + 2 * columns,)),
        ],
        name="project_queries",
    )(place, *pieces, *normed, cosine, sine)


def attend_kernel(place_ref, *refs, half_rows, heads, ctx_count):
    query_ref, seg_ref, out_ref, key_buf, value_buf, seg_buf, sems = refs[ctx_count + 1 :]
    which = pl.program_id(0)
    ctx = place_ref[0]
    blocks = 2 * ctx_count
    span = 2 * half_rows
    seg_count = half_rows // LANES

    @pl.when(which == 0)
    def _():
        pairs = []
        sources = []
        for step in range(ctx_count + 1):
            parcel = refs[step]
            distance = step if step <= ctx_count // 2 else step - 1
            if parcel.shape[0] == 1:
                sources.append((parcel.at[0], distance, step - ctx_count // 2))
            else:
                sources.append((parcel.at[0], distance, 0))
                sources.append((parcel.at[1], distance, 1))
        for source, distance, half in sources:
            holder = lax.rem(ctx + distance, ctx_count)
            block = blocks - 1 - holder if half else holder
            rows = pl.ds(pl.multiple_of(block * half_rows, half_rows), half_rows)
            pairs.append((source.at[pl.ds(0, half_rows)], key_buf.at[rows]))
            pairs.append((source.at[pl.ds(half_rows, half_rows)], value_buf.at[rows]))
            pairs.append(
                (source.at[pl.ds(2 * half_rows, 16)], seg_buf.at[block])
            )
        run_copies(pairs, sems)

    all_seg = seg_buf[...].astype(jnp.float32)
    real = lax.broadcasted_iota(jnp.int32, all_seg.shape, 1) < seg_count
    own_seg = seg_ref[0]
    first = jnp.zeros(own_seg.shape, jnp.int32)
    for doc in range(1, 4):
        smaller = jnp.where(real & (all_seg < doc), 1.0, 0.0)
        before = jnp.sum(jnp.sum(smaller, axis=0), axis=(0, 1), keepdims=True)
        first = jnp.where(own_seg == doc, before.astype(jnp.int32), first)
    own = jnp.where(which == 0, ctx, blocks - 1 - ctx)
    low = jnp.min(first) // span
    last = own * half_rows // span
    inner = jnp.minimum((jnp.max(first) + span - 1) // span, last)

    queries = jnp.concatenate(
        [query_ref[:, h * HD : (h + 1) * HD] for h in range(heads)], axis=0
    )
    rows = heads * half_rows
    factor = math.log2(math.e) / HD**0.5
    first = jnp.concatenate([first] * heads, axis=1)
    query_pos = own * half_rows + lax.rem(
        lax.broadcasted_iota(jnp.int32, (1, rows), 1), half_rows
    )

    def step(block, state, masked):
        highest, totals, accum = state
        start = pl.multiple_of(block * span, span)
        scores = dot_dims(key_buf[pl.ds(start, span)], queries, ((1,), (1,)))
        if masked:
            key_pos = start + lax.broadcasted_iota(jnp.int32, (span, rows), 0)
            allowed = (key_pos <= query_pos) & (key_pos >= first)
            limited = jnp.where(allowed, scores, masked_score)
        else:
            limited = scores
        new_high = jnp.maximum(highest, jnp.max(limited, axis=0, keepdims=True))
        shrink = jnp.exp2((highest - new_high) * factor)
        weights = jnp.exp2((scores - new_high) * factor)
        if masked:
            weights = jnp.where(allowed, weights, 0.0)
        new_totals = totals * shrink + jnp.sum(weights, axis=0, keepdims=True)
        added = dot_dims(
            value_buf[pl.ds(start, span)], weights.astype(jnp.bfloat16), ((0,), (0,))
        )
        return (new_high, new_totals, accum * shrink + added)

    state = (
        jnp.full((1, rows), masked_score, jnp.float32),
        jnp.zeros((1, rows), jnp.float32),
        jnp.zeros((HD, rows), jnp.float32),
    )
    state = lax.fori_loop(inner, last, lambda b, s: step(b, s, False), state)
    edges = jnp.minimum(inner, last) - low
    state = lax.fori_loop(
        0,
        edges + 1,
        lambda b, s: step(jnp.where(b < edges, low + b, last), s, True),
        state,
    )
    _, totals, accum = state
    mixed = (accum / totals).astype(jnp.bfloat16)
    for h in range(heads):
        out_ref[:, h * HD : (h + 1) * HD] = mixed[:, h * half_rows : (h + 1) * half_rows].T


def attend(place, parcels, queries, seg, half_rows, heads):
    ctx_count = len(parcels) - 1
    width = heads * HD
    keys = 2 * ctx_count * half_rows
    return pl.pallas_call(
        lambda *refs: attend_kernel(
            *refs, half_rows=half_rows, heads=heads, ctx_count=ctx_count
        ),
        grid=(2,),
        in_specs=[pl.BlockSpec(memory_space=pltpu.SMEM)]
        + [pl.BlockSpec(memory_space=pl.ANY)] * len(parcels)
        + [
            pl.BlockSpec((half_rows, width), lambda i: (i, 0)),
            pl.BlockSpec((1, 1, half_rows), lambda i: (i, 0, 0)),
        ],
        out_specs=pl.BlockSpec((half_rows, width), lambda i: (i, 0)),
        out_shape=jax.ShapeDtypeStruct((2 * half_rows, width), jnp.bfloat16),
        scratch_shapes=[
            pltpu.VMEM((keys, HD), jnp.bfloat16),
            pltpu.VMEM((keys, HD), jnp.bfloat16),
            pltpu.VMEM((2 * ctx_count, 16, HD), jnp.bfloat16),
            pltpu.SemaphoreType.DMA((6 * ctx_count,)),
        ],
        name="attend",
    )(place, *parcels, queries, seg)


def blend_kernel(owner_ref, *refs):
    weight_any, out_ref, square_ref, mixed_buf, buffer, total_ref, sems = refs[4:]
    width = mixed_buf.shape[2]

    def weight_copy(step):
        columns = pl.ds(pl.multiple_of(owner_ref[step] * width, LANES), width)
        return pltpu.make_async_copy(
            weight_any.at[:, columns], buffer.at[step], sems.at[4 + step]
        )

    for step in range(4):
        weight_copy(step).start()
    run_copies([(refs[step], mixed_buf.at[step]) for step in range(4)], sems)
    total_ref[...] = jnp.zeros_like(total_ref)

    def add(step, _):
        weight_copy(step).wait()
        term = dot_dims(mixed_buf[step], buffer[step], ((1,), (1,)))
        total_ref[...] += term.astype(jnp.bfloat16).astype(jnp.float32)
        return 0

    lax.fori_loop(0, 4, add, 0)
    branch = total_ref[...].astype(jnp.bfloat16)
    out_ref[...] = branch
    square = jnp.square(branch.astype(jnp.float32))
    square = jnp.sum(square.reshape(-1, 8, square.shape[1]), axis=0)
    part = square[:, :LANES]
    for block in range(1, square.shape[1] // LANES):
        part += square[:, block * LANES : (block + 1) * LANES]
    square_ref[...] = part


def blend(owners, mixed, weight):
    count, width = mixed[0].shape
    features = weight.shape[0]
    any_spec = pl.BlockSpec(memory_space=pl.ANY)
    vmem_spec = pl.BlockSpec(memory_space=pltpu.VMEM)
    return pl.pallas_call(
        blend_kernel,
        in_specs=[pl.BlockSpec(memory_space=pltpu.SMEM)] + [any_spec] * 5,
        out_specs=[vmem_spec, vmem_spec],
        out_shape=[
            jax.ShapeDtypeStruct((count, features), jnp.bfloat16),
            jax.ShapeDtypeStruct((8, LANES), jnp.float32),
        ],
        scratch_shapes=[
            pltpu.VMEM((4, count, width), jnp.bfloat16),
            pltpu.VMEM((4, features, width), jnp.bfloat16),
            pltpu.VMEM((count, features), jnp.float32),
            pltpu.SemaphoreType.DMA((8,)),
        ],
        name="blend",
    )(owners, *mixed, weight)


def shards(
    tokens,
    norm_gain,
    query_weight,
    key_weight,
    value_weight,
    output_weight,
    query_noise,
    key_noise,
    value_noise,
    output_noise,
    sign,
    segment_ids,
    doc_weight,
):
    factor = sign[0].astype(jnp.float32) * perturb_step
    half_rows = tokens.shape[2]
    model_width = tokens.shape[3]
    local_rows = 2 * half_rows
    ctx = lax.axis_index("ctx")
    tp = lax.axis_index("tp")
    ctx_count = lax.axis_size("ctx")
    columns = lax.axis_size("dp") // 2
    x = lax.axis_index("dp") // 2
    seq_len = local_rows * ctx_count
    heads = query_weight.shape[1] // HD
    width = heads * HD

    own_pair = perturbed(
        jnp.concatenate([key_weight, value_weight], axis=1),
        jnp.concatenate([key_noise, value_noise], axis=1),
        factor,
    )
    own_query = perturbed(query_weight, query_noise, factor)
    dp_count = lax.axis_size("dp")
    spread = jnp.broadcast_to(own_pair[None], (dp_count,) + own_pair.shape)
    spread, own_query = lax.optimization_barrier((spread, own_query))
    other = from_y(own_query)
    line = lax.all_to_all(spread, "dp", 0, 0).reshape(-1, 2 * HD)
    own_out = perturbed(after(output_weight, own_query), output_noise, factor).T
    out_weight = lax.all_gather(own_out, ("ctx", "dp"), axis=0, tiled=True)
    even = lax.axis_index("dp") % 2 == 0
    right = jnp.where(
        even,
        jnp.concatenate([own_query, other], axis=0),
        jnp.concatenate([other, own_query], axis=0),
    )

    place = jnp.stack([ctx, x]).astype(jnp.int32)
    rows_in = tokens[0].reshape(local_rows, model_width)
    normed = [
        norm(place, rows_in, norm_gain, ctx_count, half * half_rows, half_rows)
        for half in range(2)
    ]
    offsets = jnp.arange(half_rows, dtype=jnp.int32)
    local_pos = jnp.concatenate(
        [ctx * half_rows + offsets, seq_len - (ctx + 1) * half_rows + offsets]
    )
    cosine, sine = rope_tables(local_pos)
    seg_rows = segment_ids[0].astype(jnp.bfloat16).reshape(2, half_rows // LANES, LANES)
    seg_rows = jnp.pad(seg_rows, ((0, 0), (0, 16 - seg_rows.shape[1]), (0, 0)))

    depth = line.shape[0]
    fold = right.shape[0]
    ring = jnp.concatenate([line, right[:, : 2 * HD], right[:, 2 * HD :]], axis=0)
    up, down = [ring], [ring]
    for step in range(3):
        ends = (up[-1], down[-1])
        if step:
            ends = lax.optimization_barrier(ends + (normed[step - 1],))
            normed[step - 1] = ends[2]
        else:
            ends = lax.optimization_barrier(ends)
        up.append(from_z(ends[0], 1))
        down.append(from_z(ends[1], -1))
    last_up = jnp.concatenate([up[3][: depth // 2], up[3][depth : depth + fold]], axis=0)
    last_down = jnp.concatenate([down[3][depth // 2 : depth], down[3][depth + fold :]], axis=0)
    last_up, last_down, cosine, sine, seg_rows = lax.optimization_barrier(
        (last_up, last_down, cosine, sine, seg_rows)
    )
    far_up = from_z(last_up, 1)
    far_down = from_z(last_down, -1)
    column = jnp.concatenate(
        [piece[depth : depth + fold] for piece in up]
        + [far_up[depth // 2 :]]
        + [piece[depth : depth + fold] for piece in down[:0:-1]]
        + [piece[depth + fold :] for piece in up]
        + [far_down[depth // 2 :]]
        + [piece[depth + fold :] for piece in down[:0:-1]],
        axis=0,
    )
    next_x = from_x(column, 1)
    last_x = from_x(column, -1)
    pieces = up + [far_up, far_down] + down[:0:-1]
    parcel = project_pair(pieces, (after(normed[0], column), normed[1]), cosine, sine, seg_rows)

    parcel_up, parcel_down = [parcel], [parcel]
    for step in range(3):
        ends = (parcel_up[-1], parcel_down[-1])
        if step == 2:
            ends = lax.optimization_barrier(ends + (next_x, last_x))[:2]
        parcel_up.append(from_z(ends[0], 1))
        parcel_down.append(from_z(ends[1], -1))
    parcels = (
        parcel_up
        + [from_z(parcel_up[3][:1], 1), from_z(parcel_down[3][1:], -1)]
        + parcel_down[:0:-1]
    )
    middle = column.shape[0] // 2
    next_half, last_half = lax.optimization_barrier(
        (next_x[:middle], last_x[middle:], parcel_up[1], parcel_down[1])
    )[:2]
    columns_in = [column, next_x, from_x(next_half, 1), from_x(last_half, -1), last_x]
    queries = project_queries(place, columns_in, normed, cosine, sine, ctx_count, columns)

    own_seg = segment_ids[0].reshape(2, 1, half_rows)
    mixed = attend(place, parcels, queries, own_seg, half_rows, heads)
    near = from_tp(mixed, 1)
    far = from_tp(mixed, 2)
    owners = jnp.stack([tp, tp ^ 1, tp ^ 2, tp ^ 3]).astype(jnp.int32)
    branch, squares = blend(owners, [mixed, near, far, from_tp(far, 1)], out_weight)
    local_total = jnp.sum(squares) * doc_weight[0]
    everyone = ctx_count * lax.axis_size("tp") * lax.axis_size("dp")
    shares = lax.all_to_all(
        jnp.broadcast_to(local_total, (everyone, LANES)), mesh_axes, 0, 0, tiled=True
    )
    loss = jnp.sum(shares[:, 0]) / (seq_len * model_width)
    return (branch.reshape(1, 2, half_rows, branch.shape[1]), loss.reshape(1))


def solution(mesh):
    return jax.shard_map(
        shards,
        mesh=mesh,
        in_specs=(
            P("dp", None, "ctx", None),
            P(),
            P(("ctx", "dp"), "tp"),
            P(("ctx", "dp"), "tp"),
            P(("ctx", "dp"), "tp"),
            P(None, ("tp", "ctx", "dp")),
            P(("ctx", "dp"), "tp"),
            P(("ctx", "dp"), "tp"),
            P(("ctx", "dp"), "tp"),
            P(None, ("tp", "ctx", "dp")),
            P(),
            P("dp", None, "ctx"),
            P("dp"),
        ),
        out_specs=(P("dp", None, "ctx", "tp"), P()),
        check_vma=False,
    )
```

```python
import math

import jax
import jax.numpy as jnp
from jax import lax
from jax.experimental import pallas as pl
from jax.experimental.pallas import tpu as pltpu
from jax.sharding import PartitionSpec as P

HD = 128
LANES = 128

perturb_step = 0.004
rope_base = 500000.0
norm_epsilon = 1e-05
masked_score = -1e30
mesh_axes = ("ctx", "tp", "dp")


def perturbed(weight, noise, factor):
    return (weight.astype(jnp.float32) + factor * noise.astype(jnp.float32)).astype(jnp.bfloat16)


def dot_dims(lhs, rhs, dims):
    return lax.dot_general(lhs, rhs, (dims, ((), ())), preferred_element_type=jnp.float32)


def rope_tables(positions):
    half = HD // 2
    inverse = rope_base ** (-jnp.arange(half, dtype=jnp.float32) * 2.0 / HD)
    angles = positions.astype(jnp.float32)[:, None] * inverse[None, :]
    cosine = jnp.cos(angles)
    sine = jnp.sin(angles)
    return (
        jnp.concatenate([cosine, cosine], axis=1),
        jnp.concatenate([-sine, sine], axis=1),
    )


def fetch(values, source):
    sizes = [lax.axis_size(axis) for axis in mesh_axes]
    pairs = []
    for c in range(sizes[0]):
        for t in range(sizes[1]):
            for d in range(sizes[2]):
                fc, ft, fd = source(c, t, d)
                pairs.append(((fc * sizes[1] + ft) * sizes[2] + fd, (c * sizes[1] + t) * sizes[2] + d))
    return lax.ppermute(values, mesh_axes, pairs)


def from_z(values, step):
    count = lax.axis_size("ctx")
    return fetch(values, lambda c, t, d: ((c + step) % count, t, d))


def from_x(values, step):
    count = lax.axis_size("dp") // 2
    return fetch(values, lambda c, t, d: (c, t, ((d // 2 + step) % count) * 2 + d % 2))


def from_y(values):
    return fetch(values, lambda c, t, d: (c, t, d ^ 1))


def from_tp(values, flip):
    return fetch(values, lambda c, t, d: (c, t ^ flip, d))


def after(value, *others):
    return lax.optimization_barrier((value,) + others)[0]


def norm_kernel(place_ref, tokens_ref, gain_ref, out_ref, *, groups):
    width = tokens_ref.shape[1]
    depth = width // groups
    values = tokens_ref[...].astype(jnp.float32)
    mean = jnp.sum(values * values, axis=1, keepdims=True) / width
    rate = lax.rsqrt(mean + norm_epsilon)
    for group in range(groups):
        columns = slice(group * depth, (group + 1) * depth)
        part = tokens_ref[:, columns].astype(jnp.float32) * rate * gain_ref[:, columns]
        target = lax.rem(group + groups - place_ref[0], groups)
        target = pl.multiple_of(target * depth, depth)
        out_ref[:, pl.ds(target, depth)] = part.astype(jnp.bfloat16)


def norm(place, tokens, gain, groups, start, count, rows=64):
    width = tokens.shape[1]
    return pl.pallas_call(
        lambda *refs: norm_kernel(*refs, groups=groups),
        grid_spec=pltpu.PrefetchScalarGridSpec(
            num_scalar_prefetch=1,
            grid=(count // rows,),
            in_specs=[
                pl.BlockSpec((rows, width), lambda i, _: (i + start // rows, 0)),
                pl.BlockSpec((1, width), lambda i, _: (0, 0)),
            ],
            out_specs=pl.BlockSpec((rows, width), lambda i, _: (i, 0)),
        ),
        out_shape=jax.ShapeDtypeStruct((count, width), jnp.bfloat16),
        name="norm",
    )(place, tokens, gain.reshape(1, width))


def turn(part, cosine, sine):
    return part * cosine + pltpu.roll(part, HD // 2, 1) * sine


def run_copies(pairs, sems):
    copies = [
        pltpu.make_async_copy(source, target, sems.at[at])
        for at, (source, target) in enumerate(pairs)
    ]
    for copy in copies:
        copy.start()
    for copy in copies:
        copy.wait()


def load_columns(normed_any, normed_ref, ranges):
    pairs = []
    target = 0
    for start, size in ranges:
        for half, source in enumerate(normed_any):
            rows = source.shape[0]
            pairs.append(
                (
                    source.at[:, pl.ds(start, size)],
                    normed_ref.at[pl.ds(half * rows, rows), pl.ds(target, size)],
                )
            )
        target += size
    return pairs


def pair_sums(pieces, normed_any, ranges, buffer, normed_ref, sems):
    pairs = load_columns(normed_any, normed_ref, ranges)
    start = 0
    for piece in pieces:
        size = piece.shape[0] * 2 // 3
        pairs.append((piece.at[pl.ds(0, size)], buffer.at[pl.ds(start, size)]))
        start += size
    run_copies(pairs, sems)
    return jnp.dot(normed_ref[...], buffer[...], preferred_element_type=jnp.float32)


def pair_first_kernel(*refs, count, ranges):
    out_ref, buffer, normed_ref, sems = refs[count + 2 :]
    out_ref[...] = pair_sums(
        refs[:count], refs[count : count + 2], ranges, buffer, normed_ref, sems
    )


def pair_last_kernel(*refs, count, ranges):
    sums_ref, cos_ref, sin_ref, seg_ref, parcel_ref = refs[count + 2 : count + 7]
    buffer, normed_ref, sems = refs[count + 7 :]
    sums = sums_ref[...] + pair_sums(
        refs[:count], refs[count : count + 2], ranges, buffer, normed_ref, sems
    )
    half_rows = refs[count].shape[0]
    keys = turn(sums[:, :HD], cos_ref[...], sin_ref[...]).astype(jnp.bfloat16)
    values = sums[:, HD:].astype(jnp.bfloat16)
    for half in range(2):
        rows_of = slice(half * half_rows, (half + 1) * half_rows)
        parcel_ref[half, :half_rows] = keys[rows_of]
        parcel_ref[half, half_rows : 2 * half_rows] = values[rows_of]
        parcel_ref[half, 2 * half_rows :] = seg_ref[half]


def project_pair(pieces, normed, ranges, tail=None):
    half_rows = normed[0].shape[0]
    depth = sum(size for _, size in ranges)
    count = len(pieces)
    any_spec = pl.BlockSpec(memory_space=pl.ANY)
    vmem_spec = pl.BlockSpec(memory_space=pltpu.VMEM)
    kernel = pair_first_kernel if tail is None else pair_last_kernel
    if tail is None:
        out = jax.ShapeDtypeStruct((2 * half_rows, 2 * HD), jnp.float32)
    else:
        out = jax.ShapeDtypeStruct((2, 2 * half_rows + tail[3].shape[1], HD), jnp.bfloat16)
    extra = () if tail is None else tail
    return pl.pallas_call(
        lambda *refs: kernel(*refs, count=count, ranges=ranges),
        in_specs=[any_spec] * (count + 2) + [vmem_spec] * len(extra),
        out_specs=vmem_spec,
        out_shape=out,
        scratch_shapes=[
            pltpu.VMEM((depth, 2 * HD), jnp.bfloat16),
            pltpu.VMEM((2 * half_rows, depth), jnp.bfloat16),
            pltpu.SemaphoreType.DMA((count + 2 * len(ranges),)),
        ],
        name="pair_first" if tail is None else "pair_last",
    )(*pieces, *normed, *extra)


def column_parts(source, depth):
    return (source.at[pl.ds(0, depth)], source.at[pl.ds(depth, depth)])


def query_first_kernel(place_ref, *refs, groups, columns):
    own_any, next_any, last_any, first_any, second_any, out_ref = refs[:6]
    buffer, normed_ref, sems = refs[6:]
    depth = groups * LANES
    width = own_any.shape[1]
    pairs = load_columns((first_any, second_any), normed_ref, ((0, normed_ref.shape[1]),))
    for at, source in enumerate((own_any, next_any, last_any)):
        for half, part in enumerate(column_parts(source, depth)):
            pairs.append(
                (part, buffer.at[pl.ds(at * depth, depth), pl.ds(half * width, width)])
            )
    run_copies(pairs, sems)
    sums = None
    for at, step in enumerate((0, 1, columns - 1)):
        column = lax.rem(place_ref[1] + step, columns)
        parts = []
        for group in range(groups):
            start = pl.multiple_of((group * columns + column) * LANES, LANES)
            parts.append(normed_ref[:, pl.ds(start, LANES)])
        term = jnp.dot(
            jnp.concatenate(parts, axis=1),
            buffer[at * depth : (at + 1) * depth],
            preferred_element_type=jnp.float32,
        )
        sums = term if sums is None else sums + term
    out_ref[...] = sums


def query_last_kernel(place_ref, *refs, groups, columns):
    top_any, low_any, first_any, second_any = refs[:4]
    sums_ref, cos_ref, sin_ref, out_ref, buffer, normed_ref, sems = refs[4:]
    width = top_any.shape[1]
    column = lax.rem(place_ref[1] + columns // 2, columns)
    ranges = [
        (pl.multiple_of((group * columns + column) * LANES, LANES), LANES)
        for group in range(groups)
    ]
    pairs = load_columns((first_any, second_any), normed_ref, ranges)
    for half, part in enumerate((top_any, low_any)):
        pairs.append((part, buffer.at[:, pl.ds(half * width, width)]))
    run_copies(pairs, sems)
    sums = sums_ref[...] + jnp.dot(
        normed_ref[...], buffer[...], preferred_element_type=jnp.float32
    )
    for head in range(sums.shape[1] // HD):
        lanes = slice(head * HD, (head + 1) * HD)
        part = turn(sums[:, lanes], cos_ref[...], sin_ref[...])
        out_ref[:, lanes] = part.astype(jnp.bfloat16)


def project_queries(place, pieces, normed, groups, columns, tail=None):
    half_rows, model_width = normed[0].shape
    width = 2 * pieces[0].shape[1]
    depth = groups * LANES
    any_spec = pl.BlockSpec(memory_space=pl.ANY)
    vmem_spec = pl.BlockSpec(memory_space=pltpu.VMEM)
    kernel = query_first_kernel if tail is None else query_last_kernel
    extra = () if tail is None else tail
    shape = (2 * half_rows, width)
    return pl.pallas_call(
        lambda *refs: kernel(*refs, groups=groups, columns=columns),
        in_specs=[pl.BlockSpec(memory_space=pltpu.SMEM)]
        + [any_spec] * (len(pieces) + 2)
        + [vmem_spec] * len(extra),
        out_specs=vmem_spec,
        out_shape=jax.ShapeDtypeStruct(shape, jnp.float32 if tail is None else jnp.bfloat16),
        scratch_shapes=[
            pltpu.VMEM((depth * (3 if tail is None else 1), width), jnp.bfloat16),
            pltpu.VMEM((2 * half_rows, model_width if tail is None else depth), jnp.bfloat16),
            pltpu.SemaphoreType.DMA((8 if tail is None else 2 * groups + 2,)),
        ],
        name="query_first" if tail is None else "query_last",
    )(place, *pieces, *normed, *extra)


def attend_kernel(place_ref, *refs, half_rows, heads, ctx_count):
    query_ref, seg_ref, out_ref, key_buf, value_buf, seg_buf, sems = refs[ctx_count + 1 :]
    which = pl.program_id(0)
    ctx = place_ref[0]
    blocks = 2 * ctx_count
    span = 2 * half_rows
    seg_count = half_rows // LANES

    @pl.when(which == 0)
    def _():
        pairs = []
        sources = []
        for step in range(ctx_count + 1):
            parcel = refs[step]
            distance = step if step <= ctx_count // 2 else step - 1
            if parcel.shape[0] == 1:
                sources.append((parcel.at[0], distance, step - ctx_count // 2))
            else:
                sources.append((parcel.at[0], distance, 0))
                sources.append((parcel.at[1], distance, 1))
        for source, distance, half in sources:
            holder = lax.rem(ctx + distance, ctx_count)
            block = blocks - 1 - holder if half else holder
            rows = pl.ds(pl.multiple_of(block * half_rows, half_rows), half_rows)
            pairs.append((source.at[pl.ds(0, half_rows)], key_buf.at[rows]))
            pairs.append((source.at[pl.ds(half_rows, half_rows)], value_buf.at[rows]))
            pairs.append(
                (source.at[pl.ds(2 * half_rows, 16)], seg_buf.at[block])
            )
        run_copies(pairs, sems)

    all_seg = seg_buf[...].astype(jnp.float32)
    real = lax.broadcasted_iota(jnp.int32, all_seg.shape, 1) < seg_count
    own_seg = seg_ref[0]
    first = jnp.zeros(own_seg.shape, jnp.int32)
    for doc in range(1, 4):
        smaller = jnp.where(real & (all_seg < doc), 1.0, 0.0)
        before = jnp.sum(jnp.sum(smaller, axis=0), axis=(0, 1), keepdims=True)
        first = jnp.where(own_seg == doc, before.astype(jnp.int32), first)
    own = jnp.where(which == 0, ctx, blocks - 1 - ctx)
    low = jnp.min(first) // span
    last = own * half_rows // span
    inner = jnp.minimum((jnp.max(first) + span - 1) // span, last)

    queries = jnp.concatenate(
        [query_ref[:, h * HD : (h + 1) * HD] for h in range(heads)], axis=0
    )
    rows = heads * half_rows
    factor = math.log2(math.e) / HD**0.5
    first = jnp.concatenate([first] * heads, axis=1)
    query_pos = own * half_rows + lax.rem(
        lax.broadcasted_iota(jnp.int32, (1, rows), 1), half_rows
    )

    def step(block, state, masked):
        highest, totals, accum = state
        start = pl.multiple_of(block * span, span)
        scores = dot_dims(key_buf[pl.ds(start, span)], queries, ((1,), (1,)))
        if masked:
            key_pos = start + lax.broadcasted_iota(jnp.int32, (span, rows), 0)
            allowed = (key_pos <= query_pos) & (key_pos >= first)
            limited = jnp.where(allowed, scores, masked_score)
        else:
            limited = scores
        new_high = jnp.maximum(highest, jnp.max(limited, axis=0, keepdims=True))
        shrink = jnp.exp2((highest - new_high) * factor)
        weights = jnp.exp2((scores - new_high) * factor)
        if masked:
            weights = jnp.where(allowed, weights, 0.0)
        new_totals = totals * shrink + jnp.sum(weights, axis=0, keepdims=True)
        added = dot_dims(
            value_buf[pl.ds(start, span)], weights.astype(jnp.bfloat16), ((0,), (0,))
        )
        return (new_high, new_totals, accum * shrink + added)

    state = (
        jnp.full((1, rows), masked_score, jnp.float32),
        jnp.zeros((1, rows), jnp.float32),
        jnp.zeros((HD, rows), jnp.float32),
    )
    state = lax.fori_loop(inner, last, lambda b, s: step(b, s, False), state)
    edges = jnp.minimum(inner, last) - low
    state = lax.fori_loop(
        0,
        edges + 1,
        lambda b, s: step(jnp.where(b < edges, low + b, last), s, True),
        state,
    )
    _, totals, accum = state
    mixed = (accum / totals).astype(jnp.bfloat16)
    for h in range(heads):
        out_ref[:, h * HD : (h + 1) * HD] = mixed[:, h * half_rows : (h + 1) * half_rows].T


def attend(place, parcels, queries, seg, half_rows, heads):
    ctx_count = len(parcels) - 1
    width = heads * HD
    keys = 2 * ctx_count * half_rows
    return pl.pallas_call(
        lambda *refs: attend_kernel(
            *refs, half_rows=half_rows, heads=heads, ctx_count=ctx_count
        ),
        grid=(2,),
        in_specs=[pl.BlockSpec(memory_space=pltpu.SMEM)]
        + [pl.BlockSpec(memory_space=pl.ANY)] * len(parcels)
        + [
            pl.BlockSpec((half_rows, width), lambda i: (i, 0)),
            pl.BlockSpec((1, 1, half_rows), lambda i: (i, 0, 0)),
        ],
        out_specs=pl.BlockSpec((half_rows, width), lambda i: (i, 0)),
        out_shape=jax.ShapeDtypeStruct((2 * half_rows, width), jnp.bfloat16),
        scratch_shapes=[
            pltpu.VMEM((keys, HD), jnp.bfloat16),
            pltpu.VMEM((keys, HD), jnp.bfloat16),
            pltpu.VMEM((2 * ctx_count, 16, HD), jnp.bfloat16),
            pltpu.SemaphoreType.DMA((6 * ctx_count,)),
        ],
        name="attend",
    )(place, *parcels, queries, seg)


def blend_kernel(owner_ref, *refs):
    weight_any, out_ref, square_ref, mixed_buf, buffer, total_ref, sems = refs[4:]
    width = mixed_buf.shape[2]

    def weight_copy(step):
        columns = pl.ds(pl.multiple_of(owner_ref[step] * width, LANES), width)
        return pltpu.make_async_copy(
            weight_any.at[:, columns], buffer.at[step], sems.at[4 + step]
        )

    for step in range(4):
        weight_copy(step).start()
    run_copies([(refs[step], mixed_buf.at[step]) for step in range(4)], sems)
    total_ref[...] = jnp.zeros_like(total_ref)

    def add(step, _):
        weight_copy(step).wait()
        term = dot_dims(mixed_buf[step], buffer[step], ((1,), (1,)))
        total_ref[...] += term.astype(jnp.bfloat16).astype(jnp.float32)
        return 0

    lax.fori_loop(0, 4, add, 0)
    branch = total_ref[...].astype(jnp.bfloat16)
    out_ref[...] = branch
    square = jnp.square(branch.astype(jnp.float32))
    square = jnp.sum(square.reshape(-1, 8, square.shape[1]), axis=0)
    part = square[:, :LANES]
    for block in range(1, square.shape[1] // LANES):
        part += square[:, block * LANES : (block + 1) * LANES]
    square_ref[...] = jnp.sum(part, axis=0, keepdims=True)


def blend(owners, mixed, weight):
    count, width = mixed[0].shape
    features = weight.shape[0]
    any_spec = pl.BlockSpec(memory_space=pl.ANY)
    vmem_spec = pl.BlockSpec(memory_space=pltpu.VMEM)
    return pl.pallas_call(
        blend_kernel,
        in_specs=[pl.BlockSpec(memory_space=pltpu.SMEM)] + [any_spec] * 5,
        out_specs=[vmem_spec, vmem_spec],
        out_shape=[
            jax.ShapeDtypeStruct((count, features), jnp.bfloat16),
            jax.ShapeDtypeStruct((1, LANES), jnp.float32),
        ],
        scratch_shapes=[
            pltpu.VMEM((4, count, width), jnp.bfloat16),
            pltpu.VMEM((4, features, width), jnp.bfloat16),
            pltpu.VMEM((count, features), jnp.float32),
            pltpu.SemaphoreType.DMA((8,)),
        ],
        name="blend",
    )(owners, *mixed, weight)


def shards(
    tokens,
    norm_gain,
    query_weight,
    key_weight,
    value_weight,
    output_weight,
    query_noise,
    key_noise,
    value_noise,
    output_noise,
    sign,
    segment_ids,
    doc_weight,
):
    factor = sign[0].astype(jnp.float32) * perturb_step
    half_rows = tokens.shape[2]
    model_width = tokens.shape[3]
    local_rows = 2 * half_rows
    ctx = lax.axis_index("ctx")
    tp = lax.axis_index("tp")
    ctx_count = lax.axis_size("ctx")
    columns = lax.axis_size("dp") // 2
    x = lax.axis_index("dp") // 2
    seq_len = local_rows * ctx_count
    heads = query_weight.shape[1] // HD
    width = heads * HD

    own_pair = perturbed(
        jnp.concatenate([key_weight, value_weight], axis=1),
        jnp.concatenate([key_noise, value_noise], axis=1),
        factor,
    )
    own_query = perturbed(query_weight, query_noise, factor)
    dp_count = lax.axis_size("dp")
    spread = jnp.broadcast_to(own_pair[None], (dp_count,) + own_pair.shape)
    spread, own_query = lax.optimization_barrier((spread, own_query))
    other = from_y(own_query)
    line = lax.all_to_all(spread, "dp", 0, 0).reshape(-1, 2 * HD)
    own_out = perturbed(after(output_weight, own_query), output_noise, factor).T
    out_weight = lax.all_gather(own_out, ("ctx", "dp"), axis=0, tiled=True)
    even = lax.axis_index("dp") % 2 == 0
    right = jnp.where(
        even,
        jnp.concatenate([own_query, other], axis=0),
        jnp.concatenate([other, own_query], axis=0),
    )

    place = jnp.stack([ctx, x]).astype(jnp.int32)
    rows_in = tokens[0].reshape(local_rows, model_width)
    normed = [norm(place, rows_in, norm_gain, ctx_count, 0, half_rows)]
    offsets = jnp.arange(half_rows, dtype=jnp.int32)
    local_pos = jnp.concatenate(
        [ctx * half_rows + offsets, seq_len - (ctx + 1) * half_rows + offsets]
    )
    cosine, sine = rope_tables(local_pos)
    seg_rows = segment_ids[0].astype(jnp.bfloat16).reshape(2, half_rows // LANES, LANES)
    seg_rows = jnp.pad(seg_rows, ((0, 0), (0, 16 - seg_rows.shape[1]), (0, 0)))

    depth = line.shape[0]
    fold = right.shape[0]
    ring = jnp.concatenate([line, right[:, : 2 * HD], right[:, 2 * HD :]], axis=0)
    up, down = [ring], [ring]
    for step in range(3):
        ends = (up[-1], down[-1])
        if step:
            ends = lax.optimization_barrier(ends + (normed[step - 1],))
            normed[step - 1] = ends[2]
        else:
            ends = lax.optimization_barrier(ends)
        up.append(from_z(ends[0], 1))
        down.append(from_z(ends[1], -1))
        if step == 0:
            normed.append(
                norm(
                    after(place, up[1]), rows_in, norm_gain, ctx_count, half_rows, half_rows
                )
            )
    span = model_width // ctx_count
    pair_partial = project_pair(
        [down[2], down[1], up[0], up[1], up[2]], normed, ((6 * span, 2 * span), (0, 3 * span))
    )
    last_up = jnp.concatenate([up[3][: depth // 2], up[3][depth : depth + fold]], axis=0)
    last_down = jnp.concatenate([down[3][depth // 2 : depth], down[3][depth + fold :]], axis=0)
    last_up, last_down, cosine, sine, seg_rows, pair_partial = lax.optimization_barrier(
        (last_up, last_down, cosine, sine, seg_rows, pair_partial)
    )
    far_up = from_z(last_up, 1)
    far_down = from_z(last_down, -1)
    column = jnp.concatenate(
        [piece[depth : depth + fold] for piece in up]
        + [far_up[depth // 2 :]]
        + [piece[depth : depth + fold] for piece in down[:0:-1]]
        + [piece[depth + fold :] for piece in up]
        + [far_down[depth // 2 :]]
        + [piece[depth + fold :] for piece in down[:0:-1]],
        axis=0,
    )
    next_x = from_x(column, 1)
    last_x = from_x(column, -1)
    parcel = project_pair(
        [up[3], far_up, far_down, down[3]],
        (after(normed[0], column), normed[1]),
        ((3 * span, 3 * span),),
        (pair_partial, cosine, sine, seg_rows),
    )

    parcel_up, parcel_down = [parcel], [parcel]
    for step in range(3):
        ends = (parcel_up[-1], parcel_down[-1])
        if step == 2:
            ends = lax.optimization_barrier(ends + (next_x, last_x))[:2]
        parcel_up.append(from_z(ends[0], 1))
        parcel_down.append(from_z(ends[1], -1))
    middle = column.shape[0] // 2
    next_half, last_half = lax.optimization_barrier(
        (next_x[:middle], last_x[middle:], parcel_up[1], parcel_down[1])
    )[:2]
    query_partial = project_queries(
        place, [column, next_x, last_x], normed, ctx_count, columns
    )
    last_up, last_down, query_partial = lax.optimization_barrier(
        (parcel_up[3][:1], parcel_down[3][1:], query_partial)
    )
    parcels = (
        parcel_up + [from_z(last_up, 1), from_z(last_down, -1)] + parcel_down[:0:-1]
    )
    queries = project_queries(
        place,
        [from_x(next_half, 1), from_x(last_half, -1)],
        normed,
        ctx_count,
        columns,
        (query_partial, cosine, sine),
    )

    own_seg = segment_ids[0].reshape(2, 1, half_rows)
    mixed = attend(place, parcels, queries, own_seg, half_rows, heads)
    near = from_tp(mixed, 1)
    far = from_tp(mixed, 2)
    owners = jnp.stack([tp, tp ^ 1, tp ^ 2, tp ^ 3]).astype(jnp.int32)
    branch, squares = blend(owners, [mixed, near, far, from_tp(far, 1)], out_weight)
    everyone = ctx_count * lax.axis_size("tp") * lax.axis_size("dp")
    shares = lax.all_to_all(
        jnp.broadcast_to(squares * doc_weight[0], (everyone, LANES)),
        mesh_axes,
        0,
        0,
        tiled=True,
    )
    loss = jnp.sum(shares) / (seq_len * model_width)
    return (branch.reshape(1, 2, half_rows, branch.shape[1]), loss.reshape(1))


def solution(mesh):
    return jax.shard_map(
        shards,
        mesh=mesh,
        in_specs=(
            P("dp", None, "ctx", None),
            P(),
            P(("ctx", "dp"), "tp"),
            P(("ctx", "dp"), "tp"),
            P(("ctx", "dp"), "tp"),
            P(None, ("tp", "ctx", "dp")),
            P(("ctx", "dp"), "tp"),
            P(("ctx", "dp"), "tp"),
            P(("ctx", "dp"), "tp"),
            P(None, ("tp", "ctx", "dp")),
            P(),
            P("dp", None, "ctx"),
            P("dp"),
        ),
        out_specs=(P("dp", None, "ctx", "tp"), P()),
        check_vma=False,
    )
```

```python
import math

import jax
import jax.numpy as jnp
from jax import lax
from jax.experimental import pallas as pl
from jax.experimental.pallas import tpu as pltpu
from jax.sharding import PartitionSpec as P

HD = 128
LANES = 128

perturb_step = 0.004
rope_base = 500000.0
norm_epsilon = 1e-05
masked_score = -1e30
mesh_axes = ("ctx", "tp", "dp")


def perturbed(weight, noise, factor):
    return (weight.astype(jnp.float32) + factor * noise.astype(jnp.float32)).astype(jnp.bfloat16)


def dot_dims(lhs, rhs, dims):
    return lax.dot_general(lhs, rhs, (dims, ((), ())), preferred_element_type=jnp.float32)


def rope_tables(positions):
    half = HD // 2
    inverse = rope_base ** (-jnp.arange(half, dtype=jnp.float32) * 2.0 / HD)
    angles = positions.astype(jnp.float32)[:, None] * inverse[None, :]
    cosine = jnp.cos(angles)
    sine = jnp.sin(angles)
    return (
        jnp.concatenate([cosine, cosine], axis=1),
        jnp.concatenate([-sine, sine], axis=1),
    )


def fetch(values, source):
    sizes = [lax.axis_size(axis) for axis in mesh_axes]
    pairs = []
    for c in range(sizes[0]):
        for t in range(sizes[1]):
            for d in range(sizes[2]):
                fc, ft, fd = source(c, t, d)
                pairs.append(((fc * sizes[1] + ft) * sizes[2] + fd, (c * sizes[1] + t) * sizes[2] + d))
    return lax.ppermute(values, mesh_axes, pairs)


def from_z(values, step):
    count = lax.axis_size("ctx")
    return fetch(values, lambda c, t, d: ((c + step) % count, t, d))


def from_x(values, step):
    count = lax.axis_size("dp") // 2
    return fetch(values, lambda c, t, d: (c, t, ((d // 2 + step) % count) * 2 + d % 2))


def from_y(values):
    return fetch(values, lambda c, t, d: (c, t, d ^ 1))


def from_tp(values, flip):
    return fetch(values, lambda c, t, d: (c, t ^ flip, d))


def after(value, *others):
    return lax.optimization_barrier((value,) + others)[0]


def norm_kernel(place_ref, tokens_ref, gain_ref, out_ref, *, groups):
    width = tokens_ref.shape[1]
    depth = width // groups
    values = tokens_ref[...].astype(jnp.float32)
    mean = jnp.sum(values * values, axis=1, keepdims=True) / width
    rate = lax.rsqrt(mean + norm_epsilon)
    for group in range(groups):
        columns = slice(group * depth, (group + 1) * depth)
        part = tokens_ref[:, columns].astype(jnp.float32) * rate * gain_ref[:, columns]
        target = lax.rem(group + groups - place_ref[0], groups)
        target = pl.multiple_of(target * depth, depth)
        out_ref[:, pl.ds(target, depth)] = part.astype(jnp.bfloat16)


def norm(place, tokens, gain, groups, start, count, rows=64):
    width = tokens.shape[1]
    return pl.pallas_call(
        lambda *refs: norm_kernel(*refs, groups=groups),
        grid_spec=pltpu.PrefetchScalarGridSpec(
            num_scalar_prefetch=1,
            grid=(count // rows,),
            in_specs=[
                pl.BlockSpec((rows, width), lambda i, _: (i + start // rows, 0)),
                pl.BlockSpec((1, width), lambda i, _: (0, 0)),
            ],
            out_specs=pl.BlockSpec((rows, width), lambda i, _: (i, 0)),
        ),
        out_shape=jax.ShapeDtypeStruct((count, width), jnp.bfloat16),
        name="norm",
    )(place, tokens, gain.reshape(1, width))


def turn(part, cosine, sine):
    return part * cosine + pltpu.roll(part, HD // 2, 1) * sine


def run_copies(pairs, sems):
    copies = [
        pltpu.make_async_copy(source, target, sems.at[at])
        for at, (source, target) in enumerate(pairs)
    ]
    for copy in copies:
        copy.start()
    for copy in copies:
        copy.wait()


def load_columns(normed_any, normed_ref, ranges):
    pairs = []
    target = 0
    for start, size in ranges:
        for half, source in enumerate(normed_any):
            rows = source.shape[0]
            pairs.append(
                (
                    source.at[:, pl.ds(start, size)],
                    normed_ref.at[pl.ds(half * rows, rows), pl.ds(target, size)],
                )
            )
        target += size
    return pairs


def pair_sums(pieces, normed_any, ranges, buffer, normed_ref, sems):
    pairs = load_columns(normed_any, normed_ref, ranges)
    start = 0
    for piece in pieces:
        size = piece.shape[0] * 2 // 3
        pairs.append((piece.at[pl.ds(0, size)], buffer.at[pl.ds(start, size)]))
        start += size
    run_copies(pairs, sems)
    return jnp.dot(normed_ref[...], buffer[...], preferred_element_type=jnp.float32)


def pair_first_kernel(*refs, count, ranges):
    out_ref, buffer, normed_ref, sems = refs[count + 2 :]
    out_ref[...] = pair_sums(
        refs[:count], refs[count : count + 2], ranges, buffer, normed_ref, sems
    )


def pair_last_kernel(*refs, count, ranges):
    sums_ref, cos_ref, sin_ref, seg_ref, parcel_ref = refs[count + 2 : count + 7]
    buffer, normed_ref, sems = refs[count + 7 :]
    sums = sums_ref[...] + pair_sums(
        refs[:count], refs[count : count + 2], ranges, buffer, normed_ref, sems
    )
    half_rows = refs[count].shape[0]
    keys = turn(sums[:, :HD], cos_ref[...], sin_ref[...]).astype(jnp.bfloat16)
    values = sums[:, HD:].astype(jnp.bfloat16)
    for half in range(2):
        rows_of = slice(half * half_rows, (half + 1) * half_rows)
        parcel_ref[half, :half_rows] = keys[rows_of]
        parcel_ref[half, half_rows : 2 * half_rows] = values[rows_of]
        parcel_ref[half, 2 * half_rows :] = seg_ref[half]


def project_pair(pieces, normed, ranges, tail=None):
    half_rows = normed[0].shape[0]
    depth = sum(size for _, size in ranges)
    count = len(pieces)
    any_spec = pl.BlockSpec(memory_space=pl.ANY)
    vmem_spec = pl.BlockSpec(memory_space=pltpu.VMEM)
    kernel = pair_first_kernel if tail is None else pair_last_kernel
    if tail is None:
        out = jax.ShapeDtypeStruct((2 * half_rows, 2 * HD), jnp.float32)
    else:
        out = jax.ShapeDtypeStruct((2, 2 * half_rows + tail[3].shape[1], HD), jnp.bfloat16)
    extra = () if tail is None else tail
    return pl.pallas_call(
        lambda *refs: kernel(*refs, count=count, ranges=ranges),
        in_specs=[any_spec] * (count + 2) + [vmem_spec] * len(extra),
        out_specs=vmem_spec,
        out_shape=out,
        scratch_shapes=[
            pltpu.VMEM((depth, 2 * HD), jnp.bfloat16),
            pltpu.VMEM((2 * half_rows, depth), jnp.bfloat16),
            pltpu.SemaphoreType.DMA((count + 2 * len(ranges),)),
        ],
        name="pair_first" if tail is None else "pair_last",
    )(*pieces, *normed, *extra)


def place_columns(source, rows, buffer, first, half, near, late):
    width = source.shape[1]
    head = 3 * LANES
    lanes = pl.ds(half * width, width)
    depth = 8 * LANES
    pairs = []
    if near:
        pairs.append(
            (source.at[pl.ds(rows, head)], buffer.at[pl.ds(first, head), lanes])
        )
        tail = 2 * LANES
        pairs.append(
            (
                source.at[pl.ds(rows + head, tail)],
                buffer.at[pl.ds(first + depth - tail, tail), lanes],
            )
        )
        rows += head + tail
    if late:
        pairs.append(
            (source.at[pl.ds(rows, head)], buffer.at[pl.ds(first + head, head), lanes])
        )
    return pairs


def query_first_kernel(place_ref, *refs, groups, columns):
    first_any, second_any, out_ref, buffer, normed_ref, sems = refs[6:]
    depth = groups * LANES
    pairs = load_columns((first_any, second_any), normed_ref, ((0, normed_ref.shape[1]),))
    for at in range(3):
        near, late = refs[2 * at : 2 * at + 2]
        for half in range(2):
            pairs += place_columns(near, half * 5 * LANES, buffer, at * depth, half, True, False)
            pairs += place_columns(late, half * 3 * LANES, buffer, at * depth, half, False, True)
    run_copies(pairs, sems)
    sums = None
    for at, step in enumerate((0, 1, columns - 1)):
        column = lax.rem(place_ref[1] + step, columns)
        parts = []
        for group in range(groups):
            start = pl.multiple_of((group * columns + column) * LANES, LANES)
            parts.append(normed_ref[:, pl.ds(start, LANES)])
        term = jnp.dot(
            jnp.concatenate(parts, axis=1),
            buffer[at * depth : (at + 1) * depth],
            preferred_element_type=jnp.float32,
        )
        sums = term if sums is None else sums + term
    out_ref[...] = sums


def query_last_kernel(place_ref, *refs, groups, columns):
    top_any, low_any, first_any, second_any = refs[:4]
    sums_ref, cos_ref, sin_ref, out_ref, buffer, normed_ref, sems = refs[4:]
    column = lax.rem(place_ref[1] + columns // 2, columns)
    ranges = [
        (pl.multiple_of((group * columns + column) * LANES, LANES), LANES)
        for group in range(groups)
    ]
    pairs = load_columns((first_any, second_any), normed_ref, ranges)
    for half, part in enumerate((top_any, low_any)):
        pairs += place_columns(part, 0, buffer, 0, half, True, True)
    run_copies(pairs, sems)
    sums = sums_ref[...] + jnp.dot(
        normed_ref[...], buffer[...], preferred_element_type=jnp.float32
    )
    for head in range(sums.shape[1] // HD):
        lanes = slice(head * HD, (head + 1) * HD)
        part = turn(sums[:, lanes], cos_ref[...], sin_ref[...])
        out_ref[:, lanes] = part.astype(jnp.bfloat16)


def project_queries(place, pieces, normed, groups, columns, tail=None):
    half_rows, model_width = normed[0].shape
    width = 2 * pieces[0].shape[1]
    depth = groups * LANES
    any_spec = pl.BlockSpec(memory_space=pl.ANY)
    vmem_spec = pl.BlockSpec(memory_space=pltpu.VMEM)
    kernel = query_first_kernel if tail is None else query_last_kernel
    extra = () if tail is None else tail
    shape = (2 * half_rows, width)
    return pl.pallas_call(
        lambda *refs: kernel(*refs, groups=groups, columns=columns),
        in_specs=[pl.BlockSpec(memory_space=pltpu.SMEM)]
        + [any_spec] * (len(pieces) + 2)
        + [vmem_spec] * len(extra),
        out_specs=vmem_spec,
        out_shape=jax.ShapeDtypeStruct(shape, jnp.float32 if tail is None else jnp.bfloat16),
        scratch_shapes=[
            pltpu.VMEM((depth * (3 if tail is None else 1), width), jnp.bfloat16),
            pltpu.VMEM((2 * half_rows, model_width if tail is None else depth), jnp.bfloat16),
            pltpu.SemaphoreType.DMA((20 if tail is None else 2 * groups + 6,)),
        ],
        name="query_first" if tail is None else "query_last",
    )(place, *pieces, *normed, *extra)


def attend_kernel(place_ref, *refs, half_rows, heads, ctx_count):
    query_ref, seg_ref, out_ref, key_buf, value_buf, seg_buf, sems = refs[ctx_count + 1 :]
    which = pl.program_id(0)
    ctx = place_ref[0]
    blocks = 2 * ctx_count
    span = 2 * half_rows
    seg_count = half_rows // LANES

    @pl.when(which == 0)
    def _():
        pairs = []
        sources = []
        for step in range(ctx_count + 1):
            parcel = refs[step]
            distance = step if step <= ctx_count // 2 else step - 1
            if parcel.shape[0] == 1:
                sources.append((parcel.at[0], distance, step - ctx_count // 2))
            else:
                sources.append((parcel.at[0], distance, 0))
                sources.append((parcel.at[1], distance, 1))
        for source, distance, half in sources:
            holder = lax.rem(ctx + distance, ctx_count)
            block = blocks - 1 - holder if half else holder
            rows = pl.ds(pl.multiple_of(block * half_rows, half_rows), half_rows)
            pairs.append((source.at[pl.ds(0, half_rows)], key_buf.at[rows]))
            pairs.append((source.at[pl.ds(half_rows, half_rows)], value_buf.at[rows]))
            pairs.append(
                (source.at[pl.ds(2 * half_rows, 16)], seg_buf.at[block])
            )
        run_copies(pairs, sems)

    all_seg = seg_buf[...].astype(jnp.float32)
    real = lax.broadcasted_iota(jnp.int32, all_seg.shape, 1) < seg_count
    own_seg = seg_ref[0]
    first = jnp.zeros(own_seg.shape, jnp.int32)
    for doc in range(1, 4):
        smaller = jnp.where(real & (all_seg < doc), 1.0, 0.0)
        before = jnp.sum(jnp.sum(smaller, axis=0), axis=(0, 1), keepdims=True)
        first = jnp.where(own_seg == doc, before.astype(jnp.int32), first)
    own = jnp.where(which == 0, ctx, blocks - 1 - ctx)
    low = jnp.min(first) // span
    last = own * half_rows // span
    inner = jnp.minimum((jnp.max(first) + span - 1) // span, last)

    queries = jnp.concatenate(
        [query_ref[:, h * HD : (h + 1) * HD] for h in range(heads)], axis=0
    )
    rows = heads * half_rows
    factor = math.log2(math.e) / HD**0.5
    first = jnp.concatenate([first] * heads, axis=1)
    query_pos = own * half_rows + lax.rem(
        lax.broadcasted_iota(jnp.int32, (1, rows), 1), half_rows
    )

    def step(block, state, masked):
        highest, totals, accum = state
        start = pl.multiple_of(block * span, span)
        scores = dot_dims(key_buf[pl.ds(start, span)], queries, ((1,), (1,)))
        if masked:
            key_pos = start + lax.broadcasted_iota(jnp.int32, (span, rows), 0)
            allowed = (key_pos <= query_pos) & (key_pos >= first)
            limited = jnp.where(allowed, scores, masked_score)
        else:
            limited = scores
        new_high = jnp.maximum(highest, jnp.max(limited, axis=0, keepdims=True))
        shrink = jnp.exp2((highest - new_high) * factor)
        weights = jnp.exp2((scores - new_high) * factor)
        if masked:
            weights = jnp.where(allowed, weights, 0.0)
        new_totals = totals * shrink + jnp.sum(weights, axis=0, keepdims=True)
        added = dot_dims(
            value_buf[pl.ds(start, span)], weights.astype(jnp.bfloat16), ((0,), (0,))
        )
        return (new_high, new_totals, accum * shrink + added)

    state = (
        jnp.full((1, rows), masked_score, jnp.float32),
        jnp.zeros((1, rows), jnp.float32),
        jnp.zeros((HD, rows), jnp.float32),
    )
    state = lax.fori_loop(inner, last, lambda b, s: step(b, s, False), state)
    edges = jnp.minimum(inner, last) - low
    state = lax.fori_loop(
        0,
        edges + 1,
        lambda b, s: step(jnp.where(b < edges, low + b, last), s, True),
        state,
    )
    _, totals, accum = state
    mixed = (accum / totals).astype(jnp.bfloat16)
    for h in range(heads):
        out_ref[:, h * HD : (h + 1) * HD] = mixed[:, h * half_rows : (h + 1) * half_rows].T


def attend(place, parcels, queries, seg, half_rows, heads):
    ctx_count = len(parcels) - 1
    width = heads * HD
    keys = 2 * ctx_count * half_rows
    return pl.pallas_call(
        lambda *refs: attend_kernel(
            *refs, half_rows=half_rows, heads=heads, ctx_count=ctx_count
        ),
        grid=(2,),
        in_specs=[pl.BlockSpec(memory_space=pltpu.SMEM)]
        + [pl.BlockSpec(memory_space=pl.ANY)] * len(parcels)
        + [
            pl.BlockSpec((half_rows, width), lambda i: (i, 0)),
            pl.BlockSpec((1, 1, half_rows), lambda i: (i, 0, 0)),
        ],
        out_specs=pl.BlockSpec((half_rows, width), lambda i: (i, 0)),
        out_shape=jax.ShapeDtypeStruct((2 * half_rows, width), jnp.bfloat16),
        scratch_shapes=[
            pltpu.VMEM((keys, HD), jnp.bfloat16),
            pltpu.VMEM((keys, HD), jnp.bfloat16),
            pltpu.VMEM((2 * ctx_count, 16, HD), jnp.bfloat16),
            pltpu.SemaphoreType.DMA((6 * ctx_count,)),
        ],
        name="attend",
    )(place, *parcels, queries, seg)


def blend_kernel(owner_ref, *refs):
    weight_any, out_ref, square_ref, mixed_buf, buffer, total_ref, sems = refs[4:]
    width = mixed_buf.shape[2]

    def weight_copy(step):
        columns = pl.ds(pl.multiple_of(owner_ref[step] * width, LANES), width)
        return pltpu.make_async_copy(
            weight_any.at[:, columns], buffer.at[step], sems.at[4 + step]
        )

    for step in range(4):
        weight_copy(step).start()
    run_copies([(refs[step], mixed_buf.at[step]) for step in range(4)], sems)
    total_ref[...] = jnp.zeros_like(total_ref)

    def add(step, _):
        weight_copy(step).wait()
        term = dot_dims(mixed_buf[step], buffer[step], ((1,), (1,)))
        total_ref[...] += term.astype(jnp.bfloat16).astype(jnp.float32)
        return 0

    lax.fori_loop(0, 4, add, 0)
    branch = total_ref[...].astype(jnp.bfloat16)
    out_ref[...] = branch
    square = jnp.square(branch.astype(jnp.float32))
    square = jnp.sum(square.reshape(-1, 8, square.shape[1]), axis=0)
    part = square[:, :LANES]
    for block in range(1, square.shape[1] // LANES):
        part += square[:, block * LANES : (block + 1) * LANES]
    square_ref[...] = jnp.sum(part, axis=0, keepdims=True)


def blend(owners, mixed, weight):
    count, width = mixed[0].shape
    features = weight.shape[0]
    any_spec = pl.BlockSpec(memory_space=pl.ANY)
    vmem_spec = pl.BlockSpec(memory_space=pltpu.VMEM)
    return pl.pallas_call(
        blend_kernel,
        in_specs=[pl.BlockSpec(memory_space=pltpu.SMEM)] + [any_spec] * 5,
        out_specs=[vmem_spec, vmem_spec],
        out_shape=[
            jax.ShapeDtypeStruct((count, features), jnp.bfloat16),
            jax.ShapeDtypeStruct((1, LANES), jnp.float32),
        ],
        scratch_shapes=[
            pltpu.VMEM((4, count, width), jnp.bfloat16),
            pltpu.VMEM((4, features, width), jnp.bfloat16),
            pltpu.VMEM((count, features), jnp.float32),
            pltpu.SemaphoreType.DMA((8,)),
        ],
        name="blend",
    )(owners, *mixed, weight)


def shards(
    tokens,
    norm_gain,
    query_weight,
    key_weight,
    value_weight,
    output_weight,
    query_noise,
    key_noise,
    value_noise,
    output_noise,
    sign,
    segment_ids,
    doc_weight,
):
    factor = sign[0].astype(jnp.float32) * perturb_step
    half_rows = tokens.shape[2]
    model_width = tokens.shape[3]
    local_rows = 2 * half_rows
    ctx = lax.axis_index("ctx")
    tp = lax.axis_index("tp")
    ctx_count = lax.axis_size("ctx")
    columns = lax.axis_size("dp") // 2
    x = lax.axis_index("dp") // 2
    seq_len = local_rows * ctx_count
    heads = query_weight.shape[1] // HD
    width = heads * HD

    own_out = perturbed(output_weight, output_noise, factor).T
    out_weight = lax.all_gather(own_out, ("ctx", "dp"), axis=0, tiled=True)
    key_weight, query_weight = lax.optimization_barrier((key_weight, query_weight, own_out))[:2]
    own_pair = perturbed(
        jnp.concatenate([key_weight, value_weight], axis=1),
        jnp.concatenate([key_noise, value_noise], axis=1),
        factor,
    )
    own_query = perturbed(query_weight, query_noise, factor)
    dp_count = lax.axis_size("dp")
    spread = jnp.broadcast_to(own_pair[None], (dp_count,) + own_pair.shape)
    spread, own_query = lax.optimization_barrier((spread, own_query))
    other = from_y(own_query)
    line = lax.all_to_all(spread, "dp", 0, 0).reshape(-1, 2 * HD)
    even = lax.axis_index("dp") % 2 == 0
    right = jnp.where(
        even,
        jnp.concatenate([own_query, other], axis=0),
        jnp.concatenate([other, own_query], axis=0),
    )

    place = jnp.stack([ctx, x]).astype(jnp.int32)
    rows_in = tokens[0].reshape(local_rows, model_width)
    normed = [norm(place, rows_in, norm_gain, ctx_count, 0, half_rows)]
    offsets = jnp.arange(half_rows, dtype=jnp.int32)
    local_pos = jnp.concatenate(
        [ctx * half_rows + offsets, seq_len - (ctx + 1) * half_rows + offsets]
    )
    cosine, sine = rope_tables(local_pos)
    seg_rows = segment_ids[0].astype(jnp.bfloat16).reshape(2, half_rows // LANES, LANES)
    seg_rows = jnp.pad(seg_rows, ((0, 0), (0, 16 - seg_rows.shape[1]), (0, 0)))

    depth = line.shape[0]
    fold = right.shape[0]
    ring = jnp.concatenate([line, right[:, : 2 * HD], right[:, 2 * HD :]], axis=0)
    up, down = [ring], [ring]
    for step in range(3):
        ends = (up[-1], down[-1])
        if step:
            ends = lax.optimization_barrier(ends + (normed[step - 1],))
            normed[step - 1] = ends[2]
        else:
            ends = lax.optimization_barrier(ends)
        up.append(from_z(ends[0], 1))
        down.append(from_z(ends[1], -1))
        if step == 0:
            normed.append(
                norm(
                    after(place, up[1]), rows_in, norm_gain, ctx_count, half_rows, half_rows
                )
            )
    span = model_width // ctx_count
    pair_partial = project_pair(
        [down[2], down[1], up[0], up[1], up[2]], normed, ((6 * span, 2 * span), (0, 3 * span))
    )
    near_pieces = [up[0], up[1], up[2], down[2], down[1]]
    near = jnp.concatenate(
        [piece[depth : depth + fold] for piece in near_pieces]
        + [piece[depth + fold :] for piece in near_pieces],
        axis=0,
    )
    last_up = jnp.concatenate([up[3][: depth // 2], up[3][depth : depth + fold]], axis=0)
    last_down = jnp.concatenate([down[3][depth // 2 : depth], down[3][depth + fold :]], axis=0)
    last_up, last_down, cosine, sine, seg_rows, pair_partial, near = lax.optimization_barrier(
        (last_up, last_down, cosine, sine, seg_rows, pair_partial, near)
    )
    near_next = from_x(near, 1)
    near_last = from_x(near, -1)
    far_up = from_z(last_up, 1)
    far_down = from_z(last_down, -1)
    late = jnp.concatenate(
        [
            up[3][depth : depth + fold],
            far_up[depth // 2 :],
            down[3][depth : depth + fold],
            up[3][depth + fold :],
            far_down[depth // 2 :],
            down[3][depth + fold :],
        ],
        axis=0,
    )
    parcel = project_pair(
        [up[3], far_up, far_down, down[3]],
        normed,
        ((3 * span, 3 * span),),
        (pair_partial, cosine, sine, seg_rows),
    )

    late, near_next, near_last, _ = lax.optimization_barrier(
        (late, near_next, near_last, parcel)
    )
    late_next = from_x(late, 1)
    late_last = from_x(late, -1)

    parcel_up = [parcel, from_z(parcel, 1)]
    parcel_down = [parcel, from_z(parcel, -1)]
    ends = lax.optimization_barrier((parcel_up[1], parcel_down[1], near_next, near_last))
    parcel_up.append(from_z(ends[0], 1))
    parcel_down.append(from_z(ends[1], -1))
    near_half = near.shape[0] // 2
    late_half = late.shape[0] // 2
    far_next = from_x(
        jnp.concatenate([near_next[:near_half], late_next[:late_half]], axis=0), 1
    )
    far_last = from_x(
        jnp.concatenate([near_last[near_half:], late_last[late_half:]], axis=0), -1
    )
    query_partial = project_queries(
        place,
        [near, late, near_next, late_next, near_last, late_last],
        normed,
        ctx_count,
        columns,
    )
    ends = lax.optimization_barrier((parcel_up[2], parcel_down[2], query_partial))
    parcel_up.append(from_z(ends[0], 1))
    parcel_down.append(from_z(ends[1], -1))
    queries = project_queries(
        place, [far_next, far_last], normed, ctx_count, columns, (ends[2], cosine, sine)
    )
    last_up, last_down, queries = lax.optimization_barrier(
        (parcel_up[3][:1], parcel_down[3][1:], queries)
    )
    parcels = (
        parcel_up + [from_z(last_up, 1), from_z(last_down, -1)] + parcel_down[:0:-1]
    )

    own_seg = segment_ids[0].reshape(2, 1, half_rows)
    mixed = attend(place, parcels, queries, own_seg, half_rows, heads)
    near = from_tp(mixed, 1)
    far = from_tp(mixed, 2)
    owners = jnp.stack([tp, tp ^ 1, tp ^ 2, tp ^ 3]).astype(jnp.int32)
    branch, squares = blend(owners, [mixed, near, far, from_tp(far, 1)], out_weight)
    everyone = ctx_count * lax.axis_size("tp") * lax.axis_size("dp")
    shares = lax.all_to_all(
        jnp.broadcast_to(squares * doc_weight[0], (everyone, LANES)),
        mesh_axes,
        0,
        0,
        tiled=True,
    )
    loss = jnp.sum(shares) / (seq_len * model_width)
    return (branch.reshape(1, 2, half_rows, branch.shape[1]), loss.reshape(1))


def solution(mesh):
    return jax.shard_map(
        shards,
        mesh=mesh,
        in_specs=(
            P("dp", None, "ctx", None),
            P(),
            P(("ctx", "dp"), "tp"),
            P(("ctx", "dp"), "tp"),
            P(("ctx", "dp"), "tp"),
            P(None, ("tp", "ctx", "dp")),
            P(("ctx", "dp"), "tp"),
            P(("ctx", "dp"), "tp"),
            P(("ctx", "dp"), "tp"),
            P(None, ("tp", "ctx", "dp")),
            P(),
            P("dp", None, "ctx"),
            P("dp"),
        ),
        out_specs=(P("dp", None, "ctx", "tp"), P()),
        check_vma=False,
    )
```

```python
import math

import jax
import jax.numpy as jnp
from jax import lax
from jax.experimental import pallas as pl
from jax.experimental.pallas import tpu as pltpu
from jax.sharding import PartitionSpec as P

HD = 128
LANES = 128

perturb_step = 0.004
rope_base = 500000.0
norm_epsilon = 1e-05
masked_score = -1e30
mesh_axes = ("ctx", "tp", "dp")


def perturbed(weight, noise, factor):
    return (weight.astype(jnp.float32) + factor * noise.astype(jnp.float32)).astype(jnp.bfloat16)


def dot_dims(lhs, rhs, dims):
    return lax.dot_general(lhs, rhs, (dims, ((), ())), preferred_element_type=jnp.float32)


def rope_tables(positions):
    half = HD // 2
    inverse = rope_base ** (-jnp.arange(half, dtype=jnp.float32) * 2.0 / HD)
    angles = positions.astype(jnp.float32)[:, None] * inverse[None, :]
    cosine = jnp.cos(angles)
    sine = jnp.sin(angles)
    return (
        jnp.concatenate([cosine, cosine], axis=1),
        jnp.concatenate([-sine, sine], axis=1),
    )


def fetch(values, source):
    sizes = [lax.axis_size(axis) for axis in mesh_axes]
    pairs = []
    for c in range(sizes[0]):
        for t in range(sizes[1]):
            for d in range(sizes[2]):
                fc, ft, fd = source(c, t, d)
                pairs.append(((fc * sizes[1] + ft) * sizes[2] + fd, (c * sizes[1] + t) * sizes[2] + d))
    return lax.ppermute(values, mesh_axes, pairs)


def from_z(values, step):
    count = lax.axis_size("ctx")
    return fetch(values, lambda c, t, d: ((c + step) % count, t, d))


def from_x(values, step):
    count = lax.axis_size("dp") // 2
    return fetch(values, lambda c, t, d: (c, t, ((d // 2 + step) % count) * 2 + d % 2))


def from_y(values):
    return fetch(values, lambda c, t, d: (c, t, d ^ 1))


def from_tp(values, flip):
    return fetch(values, lambda c, t, d: (c, t ^ flip, d))


def after(value, *others):
    return lax.optimization_barrier((value,) + others)[0]


def norm_kernel(place_ref, tokens_ref, gain_ref, out_ref, *, groups):
    width = tokens_ref.shape[1]
    depth = width // groups
    values = tokens_ref[...].astype(jnp.float32)
    mean = jnp.sum(values * values, axis=1, keepdims=True) / width
    rate = lax.rsqrt(mean + norm_epsilon)
    for group in range(groups):
        columns = slice(group * depth, (group + 1) * depth)
        part = tokens_ref[:, columns].astype(jnp.float32) * rate * gain_ref[:, columns]
        target = lax.rem(group + groups - place_ref[0], groups)
        target = pl.multiple_of(target * depth, depth)
        out_ref[:, pl.ds(target, depth)] = part.astype(jnp.bfloat16)


def norm(place, tokens, gain, groups, start, count, rows=64):
    width = tokens.shape[1]
    return pl.pallas_call(
        lambda *refs: norm_kernel(*refs, groups=groups),
        grid_spec=pltpu.PrefetchScalarGridSpec(
            num_scalar_prefetch=1,
            grid=(count // rows,),
            in_specs=[
                pl.BlockSpec((rows, width), lambda i, _: (i + start // rows, 0)),
                pl.BlockSpec((1, width), lambda i, _: (0, 0)),
            ],
            out_specs=pl.BlockSpec((rows, width), lambda i, _: (i, 0)),
        ),
        out_shape=jax.ShapeDtypeStruct((count, width), jnp.bfloat16),
        name="norm",
    )(place, tokens, gain.reshape(1, width))


def turn(part, cosine, sine):
    return part * cosine + pltpu.roll(part, HD // 2, 1) * sine


def run_copies(pairs, sems):
    copies = [
        pltpu.make_async_copy(source, target, sems.at[at])
        for at, (source, target) in enumerate(pairs)
    ]
    for copy in copies:
        copy.start()
    for copy in copies:
        copy.wait()


def load_columns(normed_any, normed_ref, ranges):
    pairs = []
    target = 0
    for start, size in ranges:
        for half, source in enumerate(normed_any):
            rows = source.shape[0]
            pairs.append(
                (
                    source.at[:, pl.ds(start, size)],
                    normed_ref.at[pl.ds(half * rows, rows), pl.ds(target, size)],
                )
            )
        target += size
    return pairs


def pair_sums(pieces, normed_any, ranges, buffer, normed_ref, sems):
    pairs = load_columns(normed_any, normed_ref, ranges)
    start = 0
    for piece in pieces:
        size = piece.shape[0] * 2 // 3
        pairs.append((piece.at[pl.ds(0, size)], buffer.at[pl.ds(start, size)]))
        start += size
    run_copies(pairs, sems)
    return jnp.dot(normed_ref[...], buffer[...], preferred_element_type=jnp.float32)


def pair_first_kernel(*refs, count, ranges):
    out_ref, buffer, normed_ref, sems = refs[count + 2 :]
    out_ref[...] = pair_sums(
        refs[:count], refs[count : count + 2], ranges, buffer, normed_ref, sems
    )


def pair_last_kernel(*refs, count, ranges):
    sums_ref, cos_ref, sin_ref, seg_ref, parcel_ref = refs[count + 2 : count + 7]
    buffer, normed_ref, sems = refs[count + 7 :]
    sums = sums_ref[...] + pair_sums(
        refs[:count], refs[count : count + 2], ranges, buffer, normed_ref, sems
    )
    half_rows = refs[count].shape[0]
    keys = turn(sums[:, :HD], cos_ref[...], sin_ref[...]).astype(jnp.bfloat16)
    values = sums[:, HD:].astype(jnp.bfloat16)
    for half in range(2):
        rows_of = slice(half * half_rows, (half + 1) * half_rows)
        parcel_ref[half, :half_rows] = keys[rows_of]
        parcel_ref[half, half_rows : 2 * half_rows] = values[rows_of]
        parcel_ref[half, 2 * half_rows :] = seg_ref[half]


def project_pair(pieces, normed, ranges, tail=None):
    half_rows = normed[0].shape[0]
    depth = sum(size for _, size in ranges)
    count = len(pieces)
    any_spec = pl.BlockSpec(memory_space=pl.ANY)
    vmem_spec = pl.BlockSpec(memory_space=pltpu.VMEM)
    kernel = pair_first_kernel if tail is None else pair_last_kernel
    if tail is None:
        out = jax.ShapeDtypeStruct((2 * half_rows, 2 * HD), jnp.float32)
    else:
        out = jax.ShapeDtypeStruct((2, 2 * half_rows + tail[3].shape[1], HD), jnp.bfloat16)
    extra = () if tail is None else tail
    return pl.pallas_call(
        lambda *refs: kernel(*refs, count=count, ranges=ranges),
        in_specs=[any_spec] * (count + 2) + [vmem_spec] * len(extra),
        out_specs=vmem_spec,
        out_shape=out,
        scratch_shapes=[
            pltpu.VMEM((depth, 2 * HD), jnp.bfloat16),
            pltpu.VMEM((2 * half_rows, depth), jnp.bfloat16),
            pltpu.SemaphoreType.DMA((count + 2 * len(ranges),)),
        ],
        name="pair_first" if tail is None else "pair_last",
    )(*pieces, *normed, *extra)


def assemble_kernel(*refs, spans):
    out_any, sems = refs[-2:]
    pairs = []
    for piece, start, target, size in spans:
        pairs.append((refs[piece].at[pl.ds(start, size)], out_any.at[pl.ds(target, size)]))
    run_copies(pairs, sems)


def assemble(pieces, spans, rows):
    any_spec = pl.BlockSpec(memory_space=pl.ANY)
    return pl.pallas_call(
        lambda *refs: assemble_kernel(*refs, spans=spans),
        in_specs=[any_spec] * len(pieces),
        out_specs=any_spec,
        out_shape=jax.ShapeDtypeStruct((rows, pieces[0].shape[1]), pieces[0].dtype),
        scratch_shapes=[pltpu.SemaphoreType.DMA((len(spans),))],
        name="assemble",
    )(*pieces)


def column_parts(source, depth):
    return (source.at[pl.ds(0, depth)], source.at[pl.ds(depth, depth)])


def query_first_kernel(place_ref, *refs, groups, columns):
    own_any, next_any, last_any, first_any, second_any, out_ref = refs[:6]
    buffer, normed_ref, sems = refs[6:]
    depth = groups * LANES
    width = own_any.shape[1]
    pairs = load_columns((first_any, second_any), normed_ref, ((0, normed_ref.shape[1]),))
    for at, source in enumerate((own_any, next_any, last_any)):
        for half, part in enumerate(column_parts(source, depth)):
            pairs.append(
                (part, buffer.at[pl.ds(at * depth, depth), pl.ds(half * width, width)])
            )
    run_copies(pairs, sems)
    sums = None
    for at, step in enumerate((0, 1, columns - 1)):
        column = lax.rem(place_ref[1] + step, columns)
        parts = []
        for group in range(groups):
            start = pl.multiple_of((group * columns + column) * LANES, LANES)
            parts.append(normed_ref[:, pl.ds(start, LANES)])
        term = jnp.dot(
            jnp.concatenate(parts, axis=1),
            buffer[at * depth : (at + 1) * depth],
            preferred_element_type=jnp.float32,
        )
        sums = term if sums is None else sums + term
    out_ref[...] = sums


def query_last_kernel(place_ref, *refs, groups, columns):
    top_any, low_any, first_any, second_any = refs[:4]
    sums_ref, cos_ref, sin_ref, out_ref, buffer, normed_ref, sems = refs[4:]
    width = top_any.shape[1]
    column = lax.rem(place_ref[1] + columns // 2, columns)
    ranges = [
        (pl.multiple_of((group * columns + column) * LANES, LANES), LANES)
        for group in range(groups)
    ]
    pairs = load_columns((first_any, second_any), normed_ref, ranges)
    for half, part in enumerate((top_any, low_any)):
        pairs.append((part, buffer.at[:, pl.ds(half * width, width)]))
    run_copies(pairs, sems)
    sums = sums_ref[...] + jnp.dot(
        normed_ref[...], buffer[...], preferred_element_type=jnp.float32
    )
    for head in range(sums.shape[1] // HD):
        lanes = slice(head * HD, (head + 1) * HD)
        part = turn(sums[:, lanes], cos_ref[...], sin_ref[...])
        out_ref[:, lanes] = part.astype(jnp.bfloat16)


def project_queries(place, pieces, normed, groups, columns, tail=None):
    half_rows, model_width = normed[0].shape
    width = 2 * pieces[0].shape[1]
    depth = groups * LANES
    any_spec = pl.BlockSpec(memory_space=pl.ANY)
    vmem_spec = pl.BlockSpec(memory_space=pltpu.VMEM)
    kernel = query_first_kernel if tail is None else query_last_kernel
    extra = () if tail is None else tail
    shape = (2 * half_rows, width)
    return pl.pallas_call(
        lambda *refs: kernel(*refs, groups=groups, columns=columns),
        in_specs=[pl.BlockSpec(memory_space=pltpu.SMEM)]
        + [any_spec] * (len(pieces) + 2)
        + [vmem_spec] * len(extra),
        out_specs=vmem_spec,
        out_shape=jax.ShapeDtypeStruct(shape, jnp.float32 if tail is None else jnp.bfloat16),
        scratch_shapes=[
            pltpu.VMEM((depth * (3 if tail is None else 1), width), jnp.bfloat16),
            pltpu.VMEM((2 * half_rows, model_width if tail is None else depth), jnp.bfloat16),
            pltpu.SemaphoreType.DMA((8 if tail is None else 2 * groups + 2,)),
        ],
        name="query_first" if tail is None else "query_last",
    )(place, *pieces, *normed, *extra)


def attend_kernel(place_ref, *refs, half_rows, heads, ctx_count):
    query_ref, seg_ref, out_ref, key_buf, value_buf, seg_buf, sems = refs[ctx_count + 1 :]
    which = pl.program_id(0)
    ctx = place_ref[0]
    blocks = 2 * ctx_count
    span = 2 * half_rows
    seg_count = half_rows // LANES

    @pl.when(which == 0)
    def _():
        pairs = []
        sources = []
        for step in range(ctx_count + 1):
            parcel = refs[step]
            distance = step if step <= ctx_count // 2 else step - 1
            if parcel.shape[0] == 1:
                sources.append((parcel.at[0], distance, step - ctx_count // 2))
            else:
                sources.append((parcel.at[0], distance, 0))
                sources.append((parcel.at[1], distance, 1))
        for source, distance, half in sources:
            holder = lax.rem(ctx + distance, ctx_count)
            block = blocks - 1 - holder if half else holder
            rows = pl.ds(pl.multiple_of(block * half_rows, half_rows), half_rows)
            pairs.append((source.at[pl.ds(0, half_rows)], key_buf.at[rows]))
            pairs.append((source.at[pl.ds(half_rows, half_rows)], value_buf.at[rows]))
            pairs.append(
                (source.at[pl.ds(2 * half_rows, 16)], seg_buf.at[block])
            )
        run_copies(pairs, sems)

    all_seg = seg_buf[...].astype(jnp.float32)
    real = lax.broadcasted_iota(jnp.int32, all_seg.shape, 1) < seg_count
    own_seg = seg_ref[0]
    first = jnp.zeros(own_seg.shape, jnp.int32)
    for doc in range(1, 4):
        smaller = jnp.where(real & (all_seg < doc), 1.0, 0.0)
        before = jnp.sum(jnp.sum(smaller, axis=0), axis=(0, 1), keepdims=True)
        first = jnp.where(own_seg == doc, before.astype(jnp.int32), first)
    own = jnp.where(which == 0, ctx, blocks - 1 - ctx)
    low = jnp.min(first) // span
    last = own * half_rows // span
    inner = jnp.minimum((jnp.max(first) + span - 1) // span, last)

    queries = jnp.concatenate(
        [query_ref[:, h * HD : (h + 1) * HD] for h in range(heads)], axis=0
    )
    rows = heads * half_rows
    factor = math.log2(math.e) / HD**0.5
    first = jnp.concatenate([first] * heads, axis=1)
    query_pos = own * half_rows + lax.rem(
        lax.broadcasted_iota(jnp.int32, (1, rows), 1), half_rows
    )

    def step(block, state, masked):
        highest, totals, accum = state
        start = pl.multiple_of(block * span, span)
        scores = dot_dims(key_buf[pl.ds(start, span)], queries, ((1,), (1,)))
        if masked:
            key_pos = start + lax.broadcasted_iota(jnp.int32, (span, rows), 0)
            allowed = (key_pos <= query_pos) & (key_pos >= first)
            limited = jnp.where(allowed, scores, masked_score)
        else:
            limited = scores
        new_high = jnp.maximum(highest, jnp.max(limited, axis=0, keepdims=True))
        shrink = jnp.exp2((highest - new_high) * factor)
        weights = jnp.exp2((scores - new_high) * factor)
        if masked:
            weights = jnp.where(allowed, weights, 0.0)
        new_totals = totals * shrink + jnp.sum(weights, axis=0, keepdims=True)
        added = dot_dims(
            value_buf[pl.ds(start, span)], weights.astype(jnp.bfloat16), ((0,), (0,))
        )
        return (new_high, new_totals, accum * shrink + added)

    state = (
        jnp.full((1, rows), masked_score, jnp.float32),
        jnp.zeros((1, rows), jnp.float32),
        jnp.zeros((HD, rows), jnp.float32),
    )
    state = lax.fori_loop(inner, last, lambda b, s: step(b, s, False), state)
    edges = jnp.minimum(inner, last) - low
    state = lax.fori_loop(
        0,
        edges + 1,
        lambda b, s: step(jnp.where(b < edges, low + b, last), s, True),
        state,
    )
    _, totals, accum = state
    mixed = (accum / totals).astype(jnp.bfloat16)
    for h in range(heads):
        out_ref[:, h * HD : (h + 1) * HD] = mixed[:, h * half_rows : (h + 1) * half_rows].T


def attend(place, parcels, queries, seg, half_rows, heads):
    ctx_count = len(parcels) - 1
    width = heads * HD
    keys = 2 * ctx_count * half_rows
    return pl.pallas_call(
        lambda *refs: attend_kernel(
            *refs, half_rows=half_rows, heads=heads, ctx_count=ctx_count
        ),
        grid=(2,),
        in_specs=[pl.BlockSpec(memory_space=pltpu.SMEM)]
        + [pl.BlockSpec(memory_space=pl.ANY)] * len(parcels)
        + [
            pl.BlockSpec((half_rows, width), lambda i: (i, 0)),
            pl.BlockSpec((1, 1, half_rows), lambda i: (i, 0, 0)),
        ],
        out_specs=pl.BlockSpec((half_rows, width), lambda i: (i, 0)),
        out_shape=jax.ShapeDtypeStruct((2 * half_rows, width), jnp.bfloat16),
        scratch_shapes=[
            pltpu.VMEM((keys, HD), jnp.bfloat16),
            pltpu.VMEM((keys, HD), jnp.bfloat16),
            pltpu.VMEM((2 * ctx_count, 16, HD), jnp.bfloat16),
            pltpu.SemaphoreType.DMA((6 * ctx_count,)),
        ],
        name="attend",
    )(place, *parcels, queries, seg)


def blend_kernel(owner_ref, *refs):
    weight_any, out_ref, square_ref, mixed_buf, buffer, total_ref, sems = refs[4:]
    width = mixed_buf.shape[2]

    def weight_copy(step):
        columns = pl.ds(pl.multiple_of(owner_ref[step] * width, LANES), width)
        return pltpu.make_async_copy(
            weight_any.at[:, columns], buffer.at[step], sems.at[4 + step]
        )

    for step in range(4):
        weight_copy(step).start()
    run_copies([(refs[step], mixed_buf.at[step]) for step in range(4)], sems)
    total_ref[...] = jnp.zeros_like(total_ref)

    def add(step, _):
        weight_copy(step).wait()
        term = dot_dims(mixed_buf[step], buffer[step], ((1,), (1,)))
        total_ref[...] += term.astype(jnp.bfloat16).astype(jnp.float32)
        return 0

    lax.fori_loop(0, 4, add, 0)
    branch = total_ref[...].astype(jnp.bfloat16)
    out_ref[...] = branch
    square = jnp.square(branch.astype(jnp.float32))
    square = jnp.sum(square.reshape(-1, 8, square.shape[1]), axis=0)
    part = square[:, :LANES]
    for block in range(1, square.shape[1] // LANES):
        part += square[:, block * LANES : (block + 1) * LANES]
    square_ref[...] = jnp.sum(part, axis=0, keepdims=True)


def blend(owners, mixed, weight):
    count, width = mixed[0].shape
    features = weight.shape[0]
    any_spec = pl.BlockSpec(memory_space=pl.ANY)
    vmem_spec = pl.BlockSpec(memory_space=pltpu.VMEM)
    return pl.pallas_call(
        blend_kernel,
        in_specs=[pl.BlockSpec(memory_space=pltpu.SMEM)] + [any_spec] * 5,
        out_specs=[vmem_spec, vmem_spec],
        out_shape=[
            jax.ShapeDtypeStruct((count, features), jnp.bfloat16),
            jax.ShapeDtypeStruct((1, LANES), jnp.float32),
        ],
        scratch_shapes=[
            pltpu.VMEM((4, count, width), jnp.bfloat16),
            pltpu.VMEM((4, features, width), jnp.bfloat16),
            pltpu.VMEM((count, features), jnp.float32),
            pltpu.SemaphoreType.DMA((8,)),
        ],
        name="blend",
    )(owners, *mixed, weight)


def shards(
    tokens,
    norm_gain,
    query_weight,
    key_weight,
    value_weight,
    output_weight,
    query_noise,
    key_noise,
    value_noise,
    output_noise,
    sign,
    segment_ids,
    doc_weight,
):
    factor = sign[0].astype(jnp.float32) * perturb_step
    half_rows = tokens.shape[2]
    model_width = tokens.shape[3]
    local_rows = 2 * half_rows
    ctx = lax.axis_index("ctx")
    tp = lax.axis_index("tp")
    ctx_count = lax.axis_size("ctx")
    columns = lax.axis_size("dp") // 2
    x = lax.axis_index("dp") // 2
    seq_len = local_rows * ctx_count
    heads = query_weight.shape[1] // HD
    width = heads * HD

    own_pair = perturbed(
        jnp.concatenate([key_weight, value_weight], axis=1),
        jnp.concatenate([key_noise, value_noise], axis=1),
        factor,
    )
    own_query = perturbed(query_weight, query_noise, factor)
    dp_count = lax.axis_size("dp")
    spread = jnp.broadcast_to(own_pair[None], (dp_count,) + own_pair.shape)
    spread, own_query = lax.optimization_barrier((spread, own_query))
    other = from_y(own_query)
    line = lax.all_to_all(spread, "dp", 0, 0).reshape(-1, 2 * HD)
    own_out = perturbed(after(output_weight, own_query), output_noise, factor).T
    out_weight = lax.all_gather(own_out, ("ctx", "dp"), axis=0, tiled=True)
    even = lax.axis_index("dp") % 2 == 0
    right = jnp.where(
        even,
        jnp.concatenate([own_query, other], axis=0),
        jnp.concatenate([other, own_query], axis=0),
    )

    place = jnp.stack([ctx, x]).astype(jnp.int32)
    rows_in = tokens[0].reshape(local_rows, model_width)
    normed = [norm(place, rows_in, norm_gain, ctx_count, 0, half_rows)]
    offsets = jnp.arange(half_rows, dtype=jnp.int32)
    local_pos = jnp.concatenate(
        [ctx * half_rows + offsets, seq_len - (ctx + 1) * half_rows + offsets]
    )
    cosine, sine = rope_tables(local_pos)
    seg_rows = segment_ids[0].astype(jnp.bfloat16).reshape(2, half_rows // LANES, LANES)
    seg_rows = jnp.pad(seg_rows, ((0, 0), (0, 16 - seg_rows.shape[1]), (0, 0)))

    depth = line.shape[0]
    fold = right.shape[0]
    ring = jnp.concatenate([line, right[:, : 2 * HD], right[:, 2 * HD :]], axis=0)
    up, down = [ring], [ring]
    for step in range(3):
        ends = (up[-1], down[-1])
        if step:
            ends = lax.optimization_barrier(ends + (normed[step - 1],))
            normed[step - 1] = ends[2]
        else:
            ends = lax.optimization_barrier(ends)
        up.append(from_z(ends[0], 1))
        down.append(from_z(ends[1], -1))
        if step == 0:
            normed.append(
                norm(
                    after(place, up[1]), rows_in, norm_gain, ctx_count, half_rows, half_rows
                )
            )
    span = model_width // ctx_count
    pair_partial = project_pair(
        [down[2], down[1], up[0], up[1], up[2]], normed, ((6 * span, 2 * span), (0, 3 * span))
    )
    last_up = jnp.concatenate([up[3][: depth // 2], up[3][depth : depth + fold]], axis=0)
    last_down = jnp.concatenate([down[3][depth // 2 : depth], down[3][depth + fold :]], axis=0)
    last_up, last_down, cosine, sine, seg_rows, pair_partial = lax.optimization_barrier(
        (last_up, last_down, cosine, sine, seg_rows, pair_partial)
    )
    far_up = from_z(last_up, 1)
    far_down = from_z(last_down, -1)
    pieces = up + [far_up, far_down] + down[:0:-1]
    spans = []
    for half in range(2):
        for entry in range(ctx_count):
            target = (half * ctx_count + entry) * fold
            if entry == ctx_count // 2:
                spans.append((entry + half, depth // 2, target, fold))
            else:
                piece = entry if entry < ctx_count // 2 else entry + 1
                spans.append((piece, depth + half * fold, target, fold))
    column = assemble(pieces, spans, 2 * ctx_count * fold)
    next_x = from_x(column, 1)
    last_x = from_x(column, -1)
    parcel = project_pair(
        [up[3], far_up, far_down, down[3]],
        (after(normed[0], column), normed[1]),
        ((3 * span, 3 * span),),
        (pair_partial, cosine, sine, seg_rows),
    )

    parcel_up, parcel_down = [parcel], [parcel]
    for step in range(3):
        ends = (parcel_up[-1], parcel_down[-1])
        if step == 2:
            ends = lax.optimization_barrier(ends + (next_x, last_x))[:2]
        parcel_up.append(from_z(ends[0], 1))
        parcel_down.append(from_z(ends[1], -1))
    middle = column.shape[0] // 2
    next_half, last_half = lax.optimization_barrier(
        (next_x[:middle], last_x[middle:], parcel_up[1], parcel_down[1])
    )[:2]
    query_partial = project_queries(
        place, [column, next_x, last_x], normed, ctx_count, columns
    )
    last_up, last_down, query_partial = lax.optimization_barrier(
        (parcel_up[3][:1], parcel_down[3][1:], query_partial)
    )
    parcels = (
        parcel_up + [from_z(last_up, 1), from_z(last_down, -1)] + parcel_down[:0:-1]
    )
    queries = project_queries(
        place,
        [from_x(next_half, 1), from_x(last_half, -1)],
        normed,
        ctx_count,
        columns,
        (query_partial, cosine, sine),
    )

    own_seg = segment_ids[0].reshape(2, 1, half_rows)
    mixed = attend(place, parcels, queries, own_seg, half_rows, heads)
    near = from_tp(mixed, 1)
    far = from_tp(mixed, 2)
    owners = jnp.stack([tp, tp ^ 1, tp ^ 2, tp ^ 3]).astype(jnp.int32)
    branch, squares = blend(owners, [mixed, near, far, from_tp(far, 1)], out_weight)
    everyone = ctx_count * lax.axis_size("tp") * lax.axis_size("dp")
    shares = lax.all_to_all(
        jnp.broadcast_to(squares * doc_weight[0], (everyone, LANES)),
        mesh_axes,
        0,
        0,
        tiled=True,
    )
    loss = jnp.sum(shares) / (seq_len * model_width)
    return (branch.reshape(1, 2, half_rows, branch.shape[1]), loss.reshape(1))


def solution(mesh):
    return jax.shard_map(
        shards,
        mesh=mesh,
        in_specs=(
            P("dp", None, "ctx", None),
            P(),
            P(("ctx", "dp"), "tp"),
            P(("ctx", "dp"), "tp"),
            P(("ctx", "dp"), "tp"),
            P(None, ("tp", "ctx", "dp")),
            P(("ctx", "dp"), "tp"),
            P(("ctx", "dp"), "tp"),
            P(("ctx", "dp"), "tp"),
            P(None, ("tp", "ctx", "dp")),
            P(),
            P("dp", None, "ctx"),
            P("dp"),
        ),
        out_specs=(P("dp", None, "ctx", "tp"), P()),
        check_vma=False,
    )
```

```python
import math

import jax
import jax.numpy as jnp
from jax import lax
from jax.experimental import pallas as pl
from jax.experimental.pallas import tpu as pltpu
from jax.sharding import PartitionSpec as P

HD = 128
LANES = 128

perturb_step = 0.004
rope_base = 500000.0
norm_epsilon = 1e-05
masked_score = -1e30
mesh_axes = ("ctx", "tp", "dp")


def perturbed(weight, noise, factor):
    return (weight.astype(jnp.float32) + factor * noise.astype(jnp.float32)).astype(jnp.bfloat16)


def dot_dims(lhs, rhs, dims):
    return lax.dot_general(lhs, rhs, (dims, ((), ())), preferred_element_type=jnp.float32)


def rope_tables(positions):
    half = HD // 2
    inverse = rope_base ** (-jnp.arange(half, dtype=jnp.float32) * 2.0 / HD)
    angles = positions.astype(jnp.float32)[:, None] * inverse[None, :]
    cosine = jnp.cos(angles)
    sine = jnp.sin(angles)
    return (
        jnp.concatenate([cosine, cosine], axis=1),
        jnp.concatenate([-sine, sine], axis=1),
    )


def fetch(values, source):
    sizes = [lax.axis_size(axis) for axis in mesh_axes]
    pairs = []
    for c in range(sizes[0]):
        for t in range(sizes[1]):
            for d in range(sizes[2]):
                fc, ft, fd = source(c, t, d)
                pairs.append(((fc * sizes[1] + ft) * sizes[2] + fd, (c * sizes[1] + t) * sizes[2] + d))
    return lax.ppermute(values, mesh_axes, pairs)


def from_z(values, step):
    count = lax.axis_size("ctx")
    return fetch(values, lambda c, t, d: ((c + step) % count, t, d))


def from_x(values, step):
    count = lax.axis_size("dp") // 2
    return fetch(values, lambda c, t, d: (c, t, ((d // 2 + step) % count) * 2 + d % 2))


def from_y(values):
    return fetch(values, lambda c, t, d: (c, t, d ^ 1))


def from_tp(values, flip):
    return fetch(values, lambda c, t, d: (c, t ^ flip, d))


def after(value, *others):
    return lax.optimization_barrier((value,) + others)[0]


def norm_kernel(place_ref, tokens_ref, gain_ref, out_ref, *, groups):
    width = tokens_ref.shape[1]
    depth = width // groups
    values = tokens_ref[...].astype(jnp.float32)
    mean = jnp.sum(values * values, axis=1, keepdims=True) / width
    rate = lax.rsqrt(mean + norm_epsilon)
    for group in range(groups):
        columns = slice(group * depth, (group + 1) * depth)
        part = tokens_ref[:, columns].astype(jnp.float32) * rate * gain_ref[:, columns]
        target = lax.rem(group + groups - place_ref[0], groups)
        target = pl.multiple_of(target * depth, depth)
        out_ref[:, pl.ds(target, depth)] = part.astype(jnp.bfloat16)


def norm(place, tokens, gain, groups, start, count, rows=64):
    width = tokens.shape[1]
    return pl.pallas_call(
        lambda *refs: norm_kernel(*refs, groups=groups),
        grid_spec=pltpu.PrefetchScalarGridSpec(
            num_scalar_prefetch=1,
            grid=(count // rows,),
            in_specs=[
                pl.BlockSpec((rows, width), lambda i, _: (i + start // rows, 0)),
                pl.BlockSpec((1, width), lambda i, _: (0, 0)),
            ],
            out_specs=pl.BlockSpec((rows, width), lambda i, _: (i, 0)),
        ),
        out_shape=jax.ShapeDtypeStruct((count, width), jnp.bfloat16),
        name="norm",
    )(place, tokens, gain.reshape(1, width))


def turn(part, cosine, sine):
    return part * cosine + pltpu.roll(part, HD // 2, 1) * sine


def run_copies(pairs, sems):
    copies = [
        pltpu.make_async_copy(source, target, sems.at[at])
        for at, (source, target) in enumerate(pairs)
    ]
    for copy in copies:
        copy.start()
    for copy in copies:
        copy.wait()


def load_columns(normed_any, normed_ref, ranges):
    pairs = []
    target = 0
    for start, size in ranges:
        for half, source in enumerate(normed_any):
            rows = source.shape[0]
            pairs.append(
                (
                    source.at[:, pl.ds(start, size)],
                    normed_ref.at[pl.ds(half * rows, rows), pl.ds(target, size)],
                )
            )
        target += size
    return pairs


def pair_sums(pieces, normed_any, ranges, buffer, normed_ref, sems):
    pairs = load_columns(normed_any, normed_ref, ranges)
    start = 0
    for piece in pieces:
        size = piece.shape[0] * 2 // 3
        pairs.append((piece.at[pl.ds(0, size)], buffer.at[pl.ds(start, size)]))
        start += size
    run_copies(pairs, sems)
    return jnp.dot(normed_ref[...], buffer[...], preferred_element_type=jnp.float32)


def pair_first_kernel(*refs, count, ranges):
    out_ref, buffer, normed_ref, sems = refs[count + 2 :]
    out_ref[...] = pair_sums(
        refs[:count], refs[count : count + 2], ranges, buffer, normed_ref, sems
    )


def pair_last_kernel(*refs, count, ranges):
    sums_ref, cos_ref, sin_ref, seg_ref, parcel_ref = refs[count + 2 : count + 7]
    buffer, normed_ref, sems = refs[count + 7 :]
    sums = sums_ref[...] + pair_sums(
        refs[:count], refs[count : count + 2], ranges, buffer, normed_ref, sems
    )
    half_rows = refs[count].shape[0]
    keys = turn(sums[:, :HD], cos_ref[...], sin_ref[...]).astype(jnp.bfloat16)
    values = sums[:, HD:].astype(jnp.bfloat16)
    for half in range(2):
        rows_of = slice(half * half_rows, (half + 1) * half_rows)
        parcel_ref[half, :half_rows] = keys[rows_of]
        parcel_ref[half, half_rows : 2 * half_rows] = values[rows_of]
        parcel_ref[half, 2 * half_rows :] = seg_ref[half]


def project_pair(pieces, normed, ranges, tail=None):
    half_rows = normed[0].shape[0]
    depth = sum(size for _, size in ranges)
    count = len(pieces)
    any_spec = pl.BlockSpec(memory_space=pl.ANY)
    vmem_spec = pl.BlockSpec(memory_space=pltpu.VMEM)
    kernel = pair_first_kernel if tail is None else pair_last_kernel
    if tail is None:
        out = jax.ShapeDtypeStruct((2 * half_rows, 2 * HD), jnp.float32)
    else:
        out = jax.ShapeDtypeStruct((2, 2 * half_rows + tail[3].shape[1], HD), jnp.bfloat16)
    extra = () if tail is None else tail
    return pl.pallas_call(
        lambda *refs: kernel(*refs, count=count, ranges=ranges),
        in_specs=[any_spec] * (count + 2) + [vmem_spec] * len(extra),
        out_specs=vmem_spec,
        out_shape=out,
        scratch_shapes=[
            pltpu.VMEM((depth, 2 * HD), jnp.bfloat16),
            pltpu.VMEM((2 * half_rows, depth), jnp.bfloat16),
            pltpu.SemaphoreType.DMA((count + 2 * len(ranges),)),
        ],
        name="pair_first" if tail is None else "pair_last",
    )(*pieces, *normed, *extra)


def assemble_kernel(*refs, spans):
    out_any, sems = refs[-2:]
    pairs = []
    for piece, start, target, size in spans:
        pairs.append((refs[piece].at[pl.ds(start, size)], out_any.at[pl.ds(target, size)]))
    run_copies(pairs, sems)


def assemble(pieces, spans, rows):
    any_spec = pl.BlockSpec(memory_space=pl.ANY)
    return pl.pallas_call(
        lambda *refs: assemble_kernel(*refs, spans=spans),
        in_specs=[any_spec] * len(pieces),
        out_specs=pl.BlockSpec(memory_space=pltpu.VMEM),
        out_shape=jax.ShapeDtypeStruct((rows, pieces[0].shape[1]), pieces[0].dtype),
        scratch_shapes=[pltpu.SemaphoreType.DMA((len(spans),))],
        name="assemble",
    )(*pieces)


def column_parts(source, depth):
    return (source.at[pl.ds(0, depth)], source.at[pl.ds(depth, depth)])


def query_first_kernel(place_ref, *refs, groups, columns):
    own_any, next_any, last_any, first_any, second_any, out_ref = refs[:6]
    buffer, normed_ref, sems = refs[6:]
    depth = groups * LANES
    width = own_any.shape[1]
    pairs = load_columns((first_any, second_any), normed_ref, ((0, normed_ref.shape[1]),))
    for at, source in enumerate((own_any, next_any, last_any)):
        for half, part in enumerate(column_parts(source, depth)):
            pairs.append(
                (part, buffer.at[pl.ds(at * depth, depth), pl.ds(half * width, width)])
            )
    run_copies(pairs, sems)
    sums = None
    for at, step in enumerate((0, 1, columns - 1)):
        column = lax.rem(place_ref[1] + step, columns)
        parts = []
        for group in range(groups):
            start = pl.multiple_of((group * columns + column) * LANES, LANES)
            parts.append(normed_ref[:, pl.ds(start, LANES)])
        term = jnp.dot(
            jnp.concatenate(parts, axis=1),
            buffer[at * depth : (at + 1) * depth],
            preferred_element_type=jnp.float32,
        )
        sums = term if sums is None else sums + term
    out_ref[...] = sums


def query_last_kernel(place_ref, *refs, groups, columns):
    top_any, low_any, first_any, second_any = refs[:4]
    sums_ref, cos_ref, sin_ref, out_ref, buffer, normed_ref, sems = refs[4:]
    width = top_any.shape[1]
    column = lax.rem(place_ref[1] + columns // 2, columns)
    ranges = [
        (pl.multiple_of((group * columns + column) * LANES, LANES), LANES)
        for group in range(groups)
    ]
    pairs = load_columns((first_any, second_any), normed_ref, ranges)
    for half, part in enumerate((top_any, low_any)):
        pairs.append((part, buffer.at[:, pl.ds(half * width, width)]))
    run_copies(pairs, sems)
    sums = sums_ref[...] + jnp.dot(
        normed_ref[...], buffer[...], preferred_element_type=jnp.float32
    )
    for head in range(sums.shape[1] // HD):
        lanes = slice(head * HD, (head + 1) * HD)
        part = turn(sums[:, lanes], cos_ref[...], sin_ref[...])
        out_ref[:, lanes] = part.astype(jnp.bfloat16)


def project_queries(place, pieces, normed, groups, columns, tail=None):
    half_rows, model_width = normed[0].shape
    width = 2 * pieces[0].shape[1]
    depth = groups * LANES
    any_spec = pl.BlockSpec(memory_space=pl.ANY)
    vmem_spec = pl.BlockSpec(memory_space=pltpu.VMEM)
    kernel = query_first_kernel if tail is None else query_last_kernel
    extra = () if tail is None else tail
    shape = (2 * half_rows, width)
    return pl.pallas_call(
        lambda *refs: kernel(*refs, groups=groups, columns=columns),
        in_specs=[pl.BlockSpec(memory_space=pltpu.SMEM)]
        + [any_spec] * (len(pieces) + 2)
        + [vmem_spec] * len(extra),
        out_specs=vmem_spec,
        out_shape=jax.ShapeDtypeStruct(shape, jnp.float32 if tail is None else jnp.bfloat16),
        scratch_shapes=[
            pltpu.VMEM((depth * (3 if tail is None else 1), width), jnp.bfloat16),
            pltpu.VMEM((2 * half_rows, model_width if tail is None else depth), jnp.bfloat16),
            pltpu.SemaphoreType.DMA((8 if tail is None else 2 * groups + 2,)),
        ],
        name="query_first" if tail is None else "query_last",
    )(place, *pieces, *normed, *extra)


def attend_kernel(place_ref, *refs, half_rows, heads, ctx_count):
    query_ref, seg_ref, out_ref, key_buf, value_buf, seg_buf, sems = refs[ctx_count + 1 :]
    which = pl.program_id(0)
    ctx = place_ref[0]
    blocks = 2 * ctx_count
    span = 2 * half_rows
    seg_count = half_rows // LANES

    @pl.when(which == 0)
    def _():
        pairs = []
        sources = []
        for step in range(ctx_count + 1):
            parcel = refs[step]
            distance = step if step <= ctx_count // 2 else step - 1
            if parcel.shape[0] == 1:
                sources.append((parcel.at[0], distance, step - ctx_count // 2))
            else:
                sources.append((parcel.at[0], distance, 0))
                sources.append((parcel.at[1], distance, 1))
        for source, distance, half in sources:
            holder = lax.rem(ctx + distance, ctx_count)
            block = blocks - 1 - holder if half else holder
            rows = pl.ds(pl.multiple_of(block * half_rows, half_rows), half_rows)
            pairs.append((source.at[pl.ds(0, half_rows)], key_buf.at[rows]))
            pairs.append((source.at[pl.ds(half_rows, half_rows)], value_buf.at[rows]))
            pairs.append(
                (source.at[pl.ds(2 * half_rows, 16)], seg_buf.at[block])
            )
        run_copies(pairs, sems)

    all_seg = seg_buf[...].astype(jnp.float32)
    real = lax.broadcasted_iota(jnp.int32, all_seg.shape, 1) < seg_count
    own_seg = seg_ref[0]
    first = jnp.zeros(own_seg.shape, jnp.int32)
    for doc in range(1, 4):
        smaller = jnp.where(real & (all_seg < doc), 1.0, 0.0)
        before = jnp.sum(jnp.sum(smaller, axis=0), axis=(0, 1), keepdims=True)
        first = jnp.where(own_seg == doc, before.astype(jnp.int32), first)
    own = jnp.where(which == 0, ctx, blocks - 1 - ctx)
    low = jnp.min(first) // span
    last = own * half_rows // span
    inner = jnp.minimum((jnp.max(first) + span - 1) // span, last)

    queries = jnp.concatenate(
        [query_ref[:, h * HD : (h + 1) * HD] for h in range(heads)], axis=0
    )
    rows = heads * half_rows
    factor = math.log2(math.e) / HD**0.5
    first = jnp.concatenate([first] * heads, axis=1)
    query_pos = own * half_rows + lax.rem(
        lax.broadcasted_iota(jnp.int32, (1, rows), 1), half_rows
    )

    def step(block, state, masked):
        highest, totals, accum = state
        start = pl.multiple_of(block * span, span)
        scores = dot_dims(key_buf[pl.ds(start, span)], queries, ((1,), (1,)))
        if masked:
            key_pos = start + lax.broadcasted_iota(jnp.int32, (span, rows), 0)
            allowed = (key_pos <= query_pos) & (key_pos >= first)
            limited = jnp.where(allowed, scores, masked_score)
        else:
            limited = scores
        new_high = jnp.maximum(highest, jnp.max(limited, axis=0, keepdims=True))
        shrink = jnp.exp2((highest - new_high) * factor)
        weights = jnp.exp2((scores - new_high) * factor)
        if masked:
            weights = jnp.where(allowed, weights, 0.0)
        new_totals = totals * shrink + jnp.sum(weights, axis=0, keepdims=True)
        added = dot_dims(
            value_buf[pl.ds(start, span)], weights.astype(jnp.bfloat16), ((0,), (0,))
        )
        return (new_high, new_totals, accum * shrink + added)

    state = (
        jnp.full((1, rows), masked_score, jnp.float32),
        jnp.zeros((1, rows), jnp.float32),
        jnp.zeros((HD, rows), jnp.float32),
    )
    state = lax.fori_loop(inner, last, lambda b, s: step(b, s, False), state)
    edges = jnp.minimum(inner, last) - low
    state = lax.fori_loop(
        0,
        edges + 1,
        lambda b, s: step(jnp.where(b < edges, low + b, last), s, True),
        state,
    )
    _, totals, accum = state
    mixed = (accum / totals).astype(jnp.bfloat16)
    for h in range(heads):
        out_ref[:, h * HD : (h + 1) * HD] = mixed[:, h * half_rows : (h + 1) * half_rows].T


def attend(place, parcels, queries, seg, half_rows, heads):
    ctx_count = len(parcels) - 1
    width = heads * HD
    keys = 2 * ctx_count * half_rows
    return pl.pallas_call(
        lambda *refs: attend_kernel(
            *refs, half_rows=half_rows, heads=heads, ctx_count=ctx_count
        ),
        grid=(2,),
        in_specs=[pl.BlockSpec(memory_space=pltpu.SMEM)]
        + [pl.BlockSpec(memory_space=pl.ANY)] * len(parcels)
        + [
            pl.BlockSpec((half_rows, width), lambda i: (i, 0)),
            pl.BlockSpec((1, 1, half_rows), lambda i: (i, 0, 0)),
        ],
        out_specs=pl.BlockSpec((half_rows, width), lambda i: (i, 0)),
        out_shape=jax.ShapeDtypeStruct((2 * half_rows, width), jnp.bfloat16),
        scratch_shapes=[
            pltpu.VMEM((keys, HD), jnp.bfloat16),
            pltpu.VMEM((keys, HD), jnp.bfloat16),
            pltpu.VMEM((2 * ctx_count, 16, HD), jnp.bfloat16),
            pltpu.SemaphoreType.DMA((6 * ctx_count,)),
        ],
        name="attend",
    )(place, *parcels, queries, seg)


def blend_kernel(owner_ref, *refs):
    weight_any, out_ref, square_ref, mixed_buf, buffer, total_ref, sems = refs[4:]
    width = mixed_buf.shape[2]

    def weight_copy(step):
        columns = pl.ds(pl.multiple_of(owner_ref[step] * width, LANES), width)
        return pltpu.make_async_copy(
            weight_any.at[:, columns], buffer.at[step], sems.at[4 + step]
        )

    for step in range(4):
        weight_copy(step).start()
    run_copies([(refs[step], mixed_buf.at[step]) for step in range(4)], sems)
    total_ref[...] = jnp.zeros_like(total_ref)

    def add(step, _):
        weight_copy(step).wait()
        term = dot_dims(mixed_buf[step], buffer[step], ((1,), (1,)))
        total_ref[...] += term.astype(jnp.bfloat16).astype(jnp.float32)
        return 0

    lax.fori_loop(0, 4, add, 0)
    branch = total_ref[...].astype(jnp.bfloat16)
    out_ref[...] = branch
    square = jnp.square(branch.astype(jnp.float32))
    square = jnp.sum(square.reshape(-1, 8, square.shape[1]), axis=0)
    part = square[:, :LANES]
    for block in range(1, square.shape[1] // LANES):
        part += square[:, block * LANES : (block + 1) * LANES]
    square_ref[...] = jnp.sum(part, axis=0, keepdims=True)


def blend(owners, mixed, weight):
    count, width = mixed[0].shape
    features = weight.shape[0]
    any_spec = pl.BlockSpec(memory_space=pl.ANY)
    vmem_spec = pl.BlockSpec(memory_space=pltpu.VMEM)
    return pl.pallas_call(
        blend_kernel,
        in_specs=[pl.BlockSpec(memory_space=pltpu.SMEM)] + [any_spec] * 5,
        out_specs=[vmem_spec, vmem_spec],
        out_shape=[
            jax.ShapeDtypeStruct((count, features), jnp.bfloat16),
            jax.ShapeDtypeStruct((1, LANES), jnp.float32),
        ],
        scratch_shapes=[
            pltpu.VMEM((4, count, width), jnp.bfloat16),
            pltpu.VMEM((4, features, width), jnp.bfloat16),
            pltpu.VMEM((count, features), jnp.float32),
            pltpu.SemaphoreType.DMA((8,)),
        ],
        name="blend",
    )(owners, *mixed, weight)


def shards(
    tokens,
    norm_gain,
    query_weight,
    key_weight,
    value_weight,
    output_weight,
    query_noise,
    key_noise,
    value_noise,
    output_noise,
    sign,
    segment_ids,
    doc_weight,
):
    factor = sign[0].astype(jnp.float32) * perturb_step
    half_rows = tokens.shape[2]
    model_width = tokens.shape[3]
    local_rows = 2 * half_rows
    ctx = lax.axis_index("ctx")
    tp = lax.axis_index("tp")
    ctx_count = lax.axis_size("ctx")
    columns = lax.axis_size("dp") // 2
    x = lax.axis_index("dp") // 2
    seq_len = local_rows * ctx_count
    heads = query_weight.shape[1] // HD
    width = heads * HD

    own_pair = perturbed(
        jnp.concatenate([key_weight, value_weight], axis=1),
        jnp.concatenate([key_noise, value_noise], axis=1),
        factor,
    )
    own_query = perturbed(query_weight, query_noise, factor)
    dp_count = lax.axis_size("dp")
    spread = jnp.broadcast_to(own_pair[None], (dp_count,) + own_pair.shape)
    spread, own_query = lax.optimization_barrier((spread, own_query))
    other = from_y(own_query)
    line = lax.all_to_all(spread, "dp", 0, 0).reshape(-1, 2 * HD)
    own_out = perturbed(after(output_weight, own_query), output_noise, factor).T
    out_weight = lax.all_gather(own_out, ("ctx", "dp"), axis=0, tiled=True)
    even = lax.axis_index("dp") % 2 == 0
    right = jnp.where(
        even,
        jnp.concatenate([own_query, other], axis=0),
        jnp.concatenate([other, own_query], axis=0),
    )

    place = jnp.stack([ctx, x]).astype(jnp.int32)
    rows_in = tokens[0].reshape(local_rows, model_width)
    normed = [norm(place, rows_in, norm_gain, ctx_count, 0, half_rows)]
    offsets = jnp.arange(half_rows, dtype=jnp.int32)
    local_pos = jnp.concatenate(
        [ctx * half_rows + offsets, seq_len - (ctx + 1) * half_rows + offsets]
    )
    cosine, sine = rope_tables(local_pos)
    seg_rows = segment_ids[0].astype(jnp.bfloat16).reshape(2, half_rows // LANES, LANES)
    seg_rows = jnp.pad(seg_rows, ((0, 0), (0, 16 - seg_rows.shape[1]), (0, 0)))

    depth = line.shape[0]
    fold = right.shape[0]
    ring = jnp.concatenate([line, right[:, : 2 * HD], right[:, 2 * HD :]], axis=0)
    up, down = [ring], [ring]
    for step in range(3):
        ends = (up[-1], down[-1])
        if step:
            ends = lax.optimization_barrier(ends + (normed[step - 1],))
            normed[step - 1] = ends[2]
        else:
            ends = lax.optimization_barrier(ends)
        up.append(from_z(ends[0], 1))
        down.append(from_z(ends[1], -1))
        if step == 0:
            normed.append(
                norm(
                    after(place, up[1]), rows_in, norm_gain, ctx_count, half_rows, half_rows
                )
            )
    span = model_width // ctx_count
    pair_partial = project_pair(
        [down[2], down[1], up[0], up[1], up[2]], normed, ((6 * span, 2 * span), (0, 3 * span))
    )
    last_up = jnp.concatenate([up[3][: depth // 2], up[3][depth : depth + fold]], axis=0)
    last_down = jnp.concatenate([down[3][depth // 2 : depth], down[3][depth + fold :]], axis=0)
    last_up, last_down, cosine, sine, seg_rows, pair_partial = lax.optimization_barrier(
        (last_up, last_down, cosine, sine, seg_rows, pair_partial)
    )
    far_up = from_z(last_up, 1)
    far_down = from_z(last_down, -1)
    pieces = up + [far_up, far_down] + down[:0:-1]
    spans = []
    for half in range(2):
        for entry in range(ctx_count):
            target = (half * ctx_count + entry) * fold
            if entry == ctx_count // 2:
                spans.append((entry + half, depth // 2, target, fold))
            else:
                piece = entry if entry < ctx_count // 2 else entry + 1
                spans.append((piece, depth + half * fold, target, fold))
    column = assemble(pieces, spans, 2 * ctx_count * fold)
    next_x = from_x(column, 1)
    last_x = from_x(column, -1)
    parcel = project_pair(
        [up[3], far_up, far_down, down[3]],
        (after(normed[0], column), normed[1]),
        ((3 * span, 3 * span),),
        (pair_partial, cosine, sine, seg_rows),
    )

    parcel_up, parcel_down = [parcel], [parcel]
    for step in range(3):
        ends = (parcel_up[-1], parcel_down[-1])
        if step == 2:
            ends = lax.optimization_barrier(ends + (next_x, last_x))[:2]
        parcel_up.append(from_z(ends[0], 1))
        parcel_down.append(from_z(ends[1], -1))
    middle = column.shape[0] // 2
    next_half, last_half = lax.optimization_barrier(
        (next_x[:middle], last_x[middle:], parcel_up[1], parcel_down[1])
    )[:2]
    query_partial = project_queries(
        place, [column, next_x, last_x], normed, ctx_count, columns
    )
    last_up, last_down, query_partial = lax.optimization_barrier(
        (parcel_up[3][:1], parcel_down[3][1:], query_partial)
    )
    parcels = (
        parcel_up + [from_z(last_up, 1), from_z(last_down, -1)] + parcel_down[:0:-1]
    )
    queries = project_queries(
        place,
        [from_x(next_half, 1), from_x(last_half, -1)],
        normed,
        ctx_count,
        columns,
        (query_partial, cosine, sine),
    )

    own_seg = segment_ids[0].reshape(2, 1, half_rows)
    mixed = attend(place, parcels, queries, own_seg, half_rows, heads)
    near = from_tp(mixed, 1)
    far = from_tp(mixed, 2)
    owners = jnp.stack([tp, tp ^ 1, tp ^ 2, tp ^ 3]).astype(jnp.int32)
    branch, squares = blend(owners, [mixed, near, far, from_tp(far, 1)], out_weight)
    everyone = ctx_count * lax.axis_size("tp") * lax.axis_size("dp")
    shares = lax.all_to_all(
        jnp.broadcast_to(squares * doc_weight[0], (everyone, LANES)),
        mesh_axes,
        0,
        0,
        tiled=True,
    )
    loss = jnp.sum(shares) / (seq_len * model_width)
    return (branch.reshape(1, 2, half_rows, branch.shape[1]), loss.reshape(1))


def solution(mesh):
    return jax.shard_map(
        shards,
        mesh=mesh,
        in_specs=(
            P("dp", None, "ctx", None),
            P(),
            P(("ctx", "dp"), "tp"),
            P(("ctx", "dp"), "tp"),
            P(("ctx", "dp"), "tp"),
            P(None, ("tp", "ctx", "dp")),
            P(("ctx", "dp"), "tp"),
            P(("ctx", "dp"), "tp"),
            P(("ctx", "dp"), "tp"),
            P(None, ("tp", "ctx", "dp")),
            P(),
            P("dp", None, "ctx"),
            P("dp"),
        ),
        out_specs=(P("dp", None, "ctx", "tp"), P()),
        check_vma=False,
    )
```
